32 devices in a mesh: slab: 8 (over z, y), patch: 4 (over x, core).
Axes of the slice: x: 2, y: 2, z: 4, core: 2. Of those that a mesh axis runs over, the one named last changes fastest.
Arguments:
- fluid_state: float32 [16, 256, 256], P('slab', 'patch'), may hold values from -6 to 6
- fluid_rhs: float32 [16, 256, 256], P('slab', 'patch'), may hold values from -24 to 24
- element_scale: float32 [16, 256], P('slab', 'patch'), may hold values from 1 to 4
- element_matrix: bfloat16 [256, 256], replicated
- couple_x: bfloat16 [256, 256], replicated, may hold values from -0.09375 to 0.09375
- couple_y: bfloat16 [256, 256], replicated, may hold values from -0.09375 to 0.09375
- block_inverse: bfloat16 [256, 256], replicated
- traction_map: bfloat16 [3, 256], replicated, may hold values from -0.375 to 0.375
- slot_elem: int32 [8, 4, 1024], P('slab', 'patch'), may hold values from 0 to 127
- slot_point: int32 [8, 4, 1024], P('slab', 'patch'), may hold values from 0 to 8191
- slot_count: int32 [8, 4, 4], P('slab', 'patch'), may hold values from 0 to 256, as said below
- displacement: float32 [3, 256, 128], P(None, 'patch'), may hold values from -6 to 6
- stiffness: float32 [256, 128], P('patch'), may hold values from 0.03 to 0.3
Outputs:
- fluid_out: float32 [16, 256, 256], P('slab', 'patch')
- displacement_new: float32 [3, 256, 128], P(None, 'patch')
- wall_motion: float32 [3, 8, 4, 1024], P(None, 'slab', 'patch')
The draws below stay inside these ranges and needn't reach their ends.
Inputs may be any that keep to these rules, and one draw needn't show every extreme that they name: For every block and owner only the first slot_count slots of that owner's 256 slots are live; the count 256 is reached for some block and owner in every draw.
All inputs are finite; a program needn't handle non-finite values.
Results may differ from the reference program's by a relative error of at most 0.0049.
Values may be sent and summed in bfloat16 or wider, within the bound.
A program may use at most 128 MiB of HBM per device.

```python
import math
import jax
import jax.numpy as jnp

DOF = 256
EX_DEV = 2
EY_DEV = 64
SWEEPS = 3
NU = 64
NV = 128
CAP = 256
QDEV = 1024
NX = 16
NY = 256
NU_ALL = 256
N_SLAB = 8
N_PATCH = 4


def draw_element_matrix(key, part):
    noise = jax.random.normal(jax.random.fold_in(key, 3), (DOF, DOF), jnp.float32)
    return (4.0 * jnp.eye(DOF, dtype=jnp.float32) + noise / jnp.sqrt(DOF * 1.0)).astype(jnp.bfloat16)


def draw_block_inverse(key, part):
    noise = jax.random.normal(jax.random.fold_in(key, 5), (DOF, DOF), jnp.float32)
    return (0.25 * jnp.eye(DOF, dtype=jnp.float32) + 0.1 * noise / jnp.sqrt(DOF * 1.0)).astype(jnp.bfloat16)


def draw_slot_count(key, part):
    first, second = jax.random.split(jax.random.fold_in(key, 11), 2)
    base = jax.random.randint(first, (N_SLAB, N_PATCH, N_PATCH), CAP // 2, CAP + 1)
    slab_rank = jnp.arange(N_SLAB, dtype=jnp.int32)[:, None, None]
    counts = (base * (slab_rank + 1) // N_SLAB).reshape(-1)
    chosen = jax.random.randint(second, (), 0, N_SLAB * N_PATCH * N_PATCH)
    counts = counts.at[chosen].set(CAP)
    return counts.reshape(N_SLAB, N_PATCH, N_PATCH).astype(jnp.int32)


def plant(values, stream_key, least, largest):
    extent = values.shape
    place = [jax.random.randint(jax.random.fold_in(stream_key, axis), (), 0, extent[axis]) for axis in range(len(extent))]
    values = values.at[tuple(place)].set(least)
    longest = extent.index(max(extent))
    place[longest] = (place[longest] + 1) % extent[longest]
    return values.at[tuple(place)].set(largest)


def steps_of(key, extent, pieces, low, largest):
    loudness = 1.0
    for position, shards_of in pieces:
        steps = jax.random.uniform(jax.random.fold_in(jax.random.fold_in(key, 6), position), (shards_of,), jnp.float32, low / len(pieces), largest / len(pieces))
        loudness = loudness * jnp.repeat(jnp.exp(steps), extent[position] // shards_of).reshape((-1,) + (1,) * (len(extent) - 1 - position))
    return loudness


def centred(rng, dims, scale, reach, cuts=(), kind=jnp.bfloat16):
    array = jax.random.normal(rng, dims, jnp.float32) * scale
    if len(cuts) > 0:
        array = steps_of(rng, dims, cuts, -0.22, 0.18) * array
    return jnp.clip(array, min=-reach, max=reach).astype(kind)


def setup_inputs(seed: int = 0) -> dict:
    streams_of = jax.random.split(jax.random.key(seed), 14)
    fluid_state = centred(streams_of[0], (NX, NY, DOF), 1.0, 6.0, ((0, 8), (1, 4)), jnp.float32)
    fluid_rhs = centred(streams_of[1], (NX, NY, DOF), 4.0, 24.0, ((0, 8), (1, 4)), jnp.float32)
    element_scale = jnp.clip(jnp.exp(math.log(4.0) - 1.3862944 * jax.random.uniform(streams_of[2], (NX, NY), jnp.float32) ** steps_of(streams_of[2], (NX, NY), ((0, 8), (1, 4)), -0.2, 0.2)), 1.0, 4.0)
    element_matrix = draw_element_matrix(jax.random.fold_in(streams_of[13], 71), 0)
    couple_x = centred(streams_of[4], (DOF, DOF), (16 * DOF) ** -0.5, 0.09375)
    couple_y = centred(streams_of[5], (DOF, DOF), (16 * DOF) ** -0.5, 0.09375)
    block_inverse = draw_block_inverse(jax.random.fold_in(streams_of[13], 71), 0)
    traction_map = centred(streams_of[7], (3, DOF), DOF ** -0.5, 0.375)
    slot_elem = plant(jax.random.randint(streams_of[8], (N_SLAB, N_PATCH, QDEV), 0, EX_DEV * EY_DEV), jax.random.fold_in(streams_of[8], 1), 0, (EX_DEV * EY_DEV) - 1).astype(jnp.int32)
    slot_point = plant(jax.random.randint(streams_of[9], (N_SLAB, N_PATCH, QDEV), 0, NU * NV), jax.random.fold_in(streams_of[9], 1), 0, (NU * NV) - 1).astype(jnp.int32)
    slot_count = draw_slot_count(jax.random.fold_in(streams_of[13], 71), 0)
    displacement = centred(streams_of[11], (3, NU_ALL, NV), 1.0, 6.0, ((1, 4),), jnp.float32)
    stiffness = jnp.clip(jnp.exp(math.log(0.3) - 2.3025852 * jax.random.uniform(streams_of[12], (NU_ALL, NV), jnp.float32) ** steps_of(streams_of[12], (NU_ALL, NV), ((0, 4),), -0.2, 0.2)), 0.03, 0.3)
    return {"fluid_state": fluid_state, "fluid_rhs": fluid_rhs, "element_scale": element_scale, "element_matrix": element_matrix, "couple_x": couple_x, "couple_y": couple_y, "block_inverse": block_inverse, "traction_map": traction_map, "slot_elem": slot_elem, "slot_point": slot_point, "slot_count": slot_count, "displacement": displacement, "stiffness": stiffness}


def element_apply(rounded, scale, element_matrix, couple_x, couple_y):
    padded = jnp.pad(rounded, ((1, 1), (1, 1), (0, 0)))
    along_x = (padded[:-2, 1:-1].astype(jnp.float32) + padded[2:, 1:-1].astype(jnp.float32)).astype(jnp.bfloat16)
    along_y = (padded[1:-1, :-2].astype(jnp.float32) + padded[1:-1, 2:].astype(jnp.float32)).astype(jnp.bfloat16)
    width = rounded.shape[2]
    own = jnp.dot(rounded.reshape(-1, width), element_matrix, preferred_element_type=jnp.float32)
    side_x = jnp.dot(along_x.reshape(-1, width), couple_x, preferred_element_type=jnp.float32)
    side_y = jnp.dot(along_y.reshape(-1, width), couple_y, preferred_element_type=jnp.float32)
    return scale[:, :, None] * own.reshape(rounded.shape) - side_x.reshape(rounded.shape) - side_y.reshape(rounded.shape)


def laplace_net(field):
    edged = jnp.pad(field, ((0, 0), (1, 1), (1, 1)))
    return 4.0 * field - (edged[:, 2:, 1:-1] + edged[:, :-2, 1:-1] + edged[:, 1:-1, 2:] + edged[:, 1:-1, :-2])


def pick_rows(block, picks):
    return block[picks]


def reference(fluid_state, fluid_rhs, element_scale, element_matrix, couple_x, couple_y, block_inverse, traction_map, slot_elem, slot_point, slot_count, displacement, stiffness):
    state = fluid_state
    for sweep in range(SWEEPS):
        rounded = state.astype(jnp.bfloat16)
        applied = element_apply(rounded, element_scale, element_matrix, couple_x, couple_y)
        residue = (fluid_rhs - applied).astype(jnp.bfloat16)
        update = jnp.dot(residue.reshape(-1, DOF), block_inverse, preferred_element_type=jnp.float32).reshape(state.shape)
        state = state + update / element_scale[:, :, None]
    fluid_out = state
    final = fluid_out.astype(jnp.bfloat16)
    blocks = final.reshape(N_SLAB, EX_DEV, N_PATCH, EY_DEV, DOF).transpose(0, 2, 1, 3, 4).reshape(N_SLAB, N_PATCH, EX_DEV * EY_DEV, DOF)
    rows = jax.vmap(jax.vmap(pick_rows))(blocks, slot_elem)
    pull = jnp.einsum("cd,snqd->csnq", traction_map.astype(jnp.float32), rows.astype(jnp.float32))
    slot_ids = jnp.arange(QDEV, dtype=jnp.int32)
    owner = slot_ids // CAP
    limit = jnp.take(slot_count, owner, axis=2)
    live = ((slot_ids % CAP)[None, None, :] < limit).astype(jnp.float32)
    target = owner[None, None, :] * (NU * NV) + slot_point
    loads = jnp.zeros((3, N_PATCH * NU * NV), jnp.float32).at[:, target.reshape(-1)].add((pull * live[None]).reshape(3, -1))
    loads = loads.reshape(3, NU_ALL, NV)
    bend = laplace_net(displacement)
    stiff_term = stiffness[None] * (laplace_net(bend) + 4.0 * bend)
    displacement_new = displacement + (loads - stiff_term) / (36.0 * stiffness[None])
    wall_motion = displacement_new.reshape(3, -1)[:, target.reshape(-1)].reshape(3, N_SLAB, N_PATCH, QDEV) * live[None]
    return fluid_out, displacement_new, wall_motion
```

```python
import functools

import jax
import jax.numpy as jnp
from jax import lax
from jax.experimental import pallas as pl
from jax.experimental.pallas import tpu as pltpu
from jax.sharding import PartitionSpec as P

SWEEPS = 3
PACK = 16
EDGE = 8
SPARE = 8 * 2**20
DEEP = 16
LOAD_ORDER = (7, 6, 3, 4, 5, 2, 0, 1, 9, 8, 10, 11, 12)
MESH = pl.DeviceIdType.MESH
F32 = jnp.float32
BF16 = jnp.bfloat16


def dot(a, b):
    return jnp.dot(a, b, preferred_element_type=F32)


def dot_nt(a, b):
    return lax.dot_general(a, b, (((1,), (1,)), ((), ())), preferred_element_type=F32)


def split_point(point, cols):
    if cols & (cols - 1) == 0:
        return lax.shift_right_logical(point, cols.bit_length() - 1), point & (cols - 1)
    row = lax.div(point, cols)
    return row, point - row * cols


def column(row_vector):
    n = row_vector.shape[1]
    shape = (n, n)
    eye = lax.broadcasted_iota(jnp.int32, shape, 0) == lax.broadcasted_iota(jnp.int32, shape, 1)
    return jnp.sum(jnp.where(eye, jnp.broadcast_to(row_vector, shape), 0.0), axis=1, keepdims=True)


def laplace(x):
    rows, cols = x.shape
    lane = lax.broadcasted_iota(jnp.int32, x.shape, 1)
    left = jnp.where(lane == 0, 0.0, pltpu.roll(x, 1, 1))
    right = jnp.where(lane == cols - 1, 0.0, pltpu.roll(x, cols - 1, 1))
    return 4.0 * x - (pltpu.roll(x, 1, 0) + pltpu.roll(x, rows - 1, 0) + left + right)


def join(*parts):
    return jnp.concatenate(parts, axis=0)


def blank(rows, cols):
    return jnp.zeros((rows, cols), F32)


def make_words(traction, inverse, matrix, couple_x, couple_y):
    comps, dof = traction.shape
    base0 = dot_nt(traction, inverse)
    low = base0.astype(BF16)
    one = join(dot_nt(low, couple_x), traction.astype(F32) - dot_nt(low, matrix), dot_nt(low, couple_y))
    base1 = dot_nt(one.astype(BF16), inverse)
    low = base1.astype(BF16)
    by_x, by_y = dot_nt(low, couple_x), dot_nt(low, couple_y)
    by_d = one - dot_nt(low, matrix)
    two = join(
        by_d[:comps], by_x, by_y[:comps], blank(DEEP - 5 * comps, dof),
        by_d[comps:], by_y[comps:], blank(DEEP - 4 * comps, dof),
    )
    base2 = dot_nt(two.astype(BF16), inverse)
    low = base2.astype(BF16)
    three = join(two - dot_nt(low, matrix), dot_nt(low, couple_x), dot_nt(low, couple_y))
    rest = join(base2, base1, blank(DEEP - 3 * comps, dof), base0, blank(DEEP - comps, dof))
    return three.astype(BF16), rest.astype(BF16)


def kernel(slabs, patches, args, *refs):
    hbm, refs = refs[:args], refs[args:]
    (fluid_ref, net_ref, wall_ref), refs = refs[:3], refs[3:]
    staged, refs = refs[:args], refs[args:]
    (state_ref, rhs_ref, scale_ref, matrix_ref, cx_ref, cy_ref, inverse_ref, traction_ref) = staged[:8]
    (elem_ref, point_ref, count_ref, disp_ref, stiff_ref) = staged[8:]
    (vb, halo_x, halo_y, halo_d, points, pulls, pull_out, picks_out, picks_in) = refs[:9]
    (onehot_elem, onehot_row, onehot_col, rest_buf, gain_buf) = refs[9:14]
    (near_out, near_in, far_out, far_in, side_out, side_in, tip_out, tip_in, w_out, w_in) = refs[14:24]
    (load_sem, sx, rx, sy, ry, sd, rd, sp1, rp1, sp2, rp2, sq, rq, sw, rw) = refs[24:39]
    (s_near, r_near, s_far, r_far, s_side, r_side, s_tip, r_tip, s_w, r_w, near_sem) = refs[39:]

    loads_in = [pltpu.make_async_copy(hbm[n], staged[n], load_sem.at[n]) for n in range(args)]
    for n in LOAD_ORDER:
        loads_in[n].start()

    def ready(*names):
        for n in names:
            loads_in[n].wait()

    s = lax.axis_index("slab")
    p = lax.axis_index("patch")
    ex, ey, dof = state_ref.shape
    comps, rows, cols = disp_ref.shape
    cap = elem_ref.shape[2] // patches
    wide_lanes = ex * ey

    def slab_peer(j):
        return lax.rem(s + j, slabs)

    def patch_peer(j):
        return lax.rem(p + j, patches)

    def slab_sides(reach, semaphore):
        @pl.when(s >= reach)
        def _():
            pl.semaphore_signal(semaphore, inc=1, device_id=(s - reach, p), device_id_type=MESH)

        @pl.when(s + reach < slabs)
        def _():
            pl.semaphore_signal(semaphore, inc=1, device_id=(s + reach, p), device_id_type=MESH)

    def slab_count(reach):
        return jnp.where(s >= reach, 1, 0) + jnp.where(s + reach < slabs, 1, 0)

    reaches = []
    while 2 ** (len(reaches) + 1) < slabs - 1:
        reaches.append(2 ** (len(reaches) + 1))

    def near_signal(n):
        slab_sides(reaches[n], near_sem.at[n])

    def near_wait(n):
        pl.semaphore_wait(near_sem.at[n], slab_count(reaches[n]))

    has_prev_s, has_next_s = s > 0, s < slabs - 1
    has_prev_p, has_next_p = p > 0, p < patches - 1
    has_far_prev, has_far_next = s > 1, s < slabs - 2

    barrier = pltpu.get_barrier_semaphore()
    for j in range(1, patches):
        pl.semaphore_signal(barrier, inc=1, device_id=(s, patch_peer(j)), device_id_type=MESH)
    for reach in (1, 2):

        @pl.when(s >= reach)
        def _():
            for j in range(patches):
                pl.semaphore_signal(barrier, inc=1, device_id=(s - reach, patch_peer(j)), device_id_type=MESH)

        @pl.when(s + reach < slabs)
        def _():
            for j in range(patches):
                pl.semaphore_signal(barrier, inc=1, device_id=(s + reach, patch_peer(j)), device_id_type=MESH)

    awaited = patches - 1 + patches * (slab_count(1) + slab_count(2))

    def remote(src, dst, send, recv, target):
        return pltpu.make_async_remote_copy(
            src_ref=src, dst_ref=dst, send_sem=send, recv_sem=recv, device_id=target, device_id_type=MESH
        )

    def slab_at(step):
        return jnp.clip(s + step, 0, slabs - 1)

    def patch_at(step):
        return jnp.clip(p + step, 0, patches - 1)

    def x_up(k):
        return remote(vb.at[k, ex - 1], halo_x.at[k, 0], sx.at[k, 0], rx.at[k, 0], (slab_at(1), p))

    def x_down(k):
        return remote(vb.at[k, 0], halo_x.at[k, 1], sx.at[k, 1], rx.at[k, 1], (slab_at(-1), p))

    def y_up(k):
        return remote(
            vb.at[k, :, pl.ds(ey - PACK, PACK)], halo_y.at[k, 0], sy.at[k, 0], ry.at[k, 0], (s, patch_at(1))
        )

    def y_down(k):
        return remote(vb.at[k, :, pl.ds(0, PACK)], halo_y.at[k, 1], sy.at[k, 1], ry.at[k, 1], (s, patch_at(-1)))

    def d_up():
        return remote(disp_ref.at[:, pl.ds(rows - EDGE, EDGE)], halo_d.at[0], sd.at[0], rd.at[0], (s, patch_at(1)))

    def d_down():
        return remote(disp_ref.at[:, pl.ds(0, EDGE)], halo_d.at[1], sd.at[1], rd.at[1], (s, patch_at(-1)))

    def near_copy(n):
        return remote(near_out, near_in.at[n], s_near.at[n], r_near.at[n], (slab_at(1 - 2 * n), p))

    def far_copy(n):
        return remote(far_out, far_in.at[n], s_far.at[n], r_far.at[n], (slab_at(2 - 4 * n), p))

    def side_copy(n):
        return remote(side_out.at[n], side_in.at[n], s_side.at[n], r_side.at[n], (s, patch_at(1 - 2 * n)))

    def tip_copy(n, m):
        q = 2 * n + m
        return remote(tip_out.at[q], tip_in.at[q], s_tip.at[q], r_tip.at[q], (slab_at(1 - 2 * n), patch_at(1 - 2 * m)))

    def w_copy(a, b):
        q = 3 * (1 - a) + 1 - b
        return remote(w_out, w_in.at[q], s_w.at[q], r_w.at[q], (slab_at(a), patch_at(b)))

    to_s, from_s = (has_next_s, has_prev_s), (has_prev_s, has_next_s)
    to_p, from_p = (has_next_p, has_prev_p), (has_prev_p, has_next_p)
    to_far, from_far = (has_far_next, has_far_prev), (has_far_prev, has_far_next)
    corners = [(n, m) for n in range(2) for m in range(2)]
    around = [(a, b) for a in (-1, 0, 1) for b in (-1, 0, 1) if (a, b) != (0, 0)]

    def exists(a, b):
        ok_s = {-1: has_prev_s, 0: None, 1: has_next_s}[a]
        ok_p = {-1: has_prev_p, 0: None, 1: has_next_p}[b]
        if ok_s is None:
            return ok_p
        return ok_s if ok_p is None else jnp.logical_and(ok_s, ok_p)

    def point_first(j, mine):
        peer = patch_peer(j)
        src = point_ref.at[0, :, pl.ds(pl.multiple_of(peer * cap, cap), cap)]
        slot = p if mine else peer
        return remote(src, points.at[s, slot], sp1.at[j], rp1.at[slot], (s, peer))

    def point_second(j, mine):
        peer = slab_peer(j)
        slot = s if mine else peer
        return remote(points.at[s], points.at[slot], sp2.at[j], rp2.at[slot], (peer, p))

    def pull_copy(j, i):
        to = (slab_peer(j), patch_peer(i))
        return remote(pull_out.at[to[1]], pulls.at[s, p], sq.at[j, i], rq.at[s, p], to)

    def pull_arrival(slab, patch):
        return remote(pull_out.at[p], pulls.at[slab, patch], sq.at[0, 0], rq.at[slab, patch], (slab, patch))

    def pick_copy(j, mine):
        peer = patch_peer(j)
        slot = p if mine else peer
        return remote(picks_out.at[peer], picks_in.at[slot], sw.at[j], rw.at[slot], (s, peer))

    def send_halos(k):
        pl.when(has_next_s)(lambda: x_up(k).start())
        pl.when(has_prev_s)(lambda: x_down(k).start())
        pl.when(has_next_p)(lambda: y_up(k).start())
        pl.when(has_prev_p)(lambda: y_down(k).start())

    def build_points(slab):
        for k in range(patches):
            row, col = split_point(points[slab, k], cols)
            span = pl.ds(k * cap, cap)
            onehot_row[slab, :, span] = jnp.where(
                lax.broadcasted_iota(jnp.int32, (rows, cap), 0) == row, 1.0, 0.0
            ).astype(BF16)
            onehot_col[slab, :, span] = jnp.where(
                lax.broadcasted_iota(jnp.int32, (cols, cap), 0) == col, 1.0, 0.0
            ).astype(BF16)

    def lives(k):
        lane = lax.broadcasted_iota(jnp.int32, (1, cap), 1)
        return lane < count_ref[0, :, k : k + 1]

    def shell():
        pl.when(has_prev_p)(lambda: d_up().wait_recv())
        pl.when(has_next_p)(lambda: d_down().wait_recv())
        total = rows + 2 * EDGE
        line = lax.broadcasted_iota(jnp.int32, (total, cols), 0)
        first = jnp.where(has_prev_p, 0, EDGE)
        last = jnp.where(has_next_p, total, EDGE + rows)
        valid = (line >= first) & (line < last)
        gain = 1.0 / (36.0 * stiff_ref[...])
        gain_buf[...] = gain
        for c in range(comps):
            field = jnp.concatenate([halo_d[0, c], disp_ref[c], halo_d[1, c]], axis=0)
            field = jnp.where(valid, field, 0.0)
            bend = jnp.where(valid, laplace(field), 0.0)
            full = (laplace(bend) + 4.0 * bend)[EDGE : EDGE + rows]
            rest_buf[c] = disp_ref[c] - stiff_ref[...] * full * gain

    with jax.named_scope("words"):
        ready(7, 6, 4, 3, 5)
        words, rest = make_words(
            traction_ref[...], inverse_ref[...], matrix_ref[...], cx_ref[...], cy_ref[...]
        )
    ready(2)
    w_out[...] = blank(*w_out.shape)
    w_out[:, 0:ey] = 1.0 / scale_ref[...]
    ready(0)
    rounded0 = state_ref[...].astype(BF16)
    vb[0] = rounded0
    ready(1)
    wet = rhs_ref[...].astype(BF16)
    with jax.named_scope("project"):
        own_v = dot_nt(words, rounded0.reshape(wide_lanes, dof))
        own_r = dot_nt(rest, wet.reshape(wide_lanes, dof))
        spare = join(blank(2 * DEEP - comps - 1, wide_lanes), own_r[2 * DEEP : 2 * DEEP + comps], blank(1, wide_lanes))
        near_out[...] = join(
            own_v[0:DEEP], own_v[2 * DEEP : 4 * DEEP] + spare, own_v[4 * DEEP : 5 * DEEP], own_r[0:DEEP]
        ).astype(BF16)
        far_out[...] = own_v[2 * DEEP : 2 * DEEP + 8].astype(BF16)

        def state_at(i, c):
            return state_ref[i, c : c + 1]

        def rhs_at(i, c):
            return rhs_ref[i, c : c + 1]

        for m in range(2):
            edge = [ey - 1 - j if m == 0 else j for j in range(SWEEPS)]
            lines = [state_at(i, c) for i in range(ex) for c in edge]
            lines += [rhs_at(i, c) for i in range(ex) for c in edge[: SWEEPS - 1]]
            side_out[m] = join(*lines, blank(DEEP - len(lines), dof)).astype(BF16)
            for n in range(2):
                order = [ex - 1, ex - 2] if n == 0 else [0, 1]
                tip_out[2 * n + m] = join(
                    state_at(order[0], edge[0]),
                    state_at(order[0], edge[1]),
                    state_at(order[1], edge[0]),
                    rhs_at(order[0], edge[0]),
                ).astype(BF16)

    with jax.named_scope("w_barrier"):
        pl.semaphore_wait(barrier, awaited)
    for n in range(2):
        pl.when(to_s[n])(lambda: near_copy(n).start())
    for n, m in corners:
        pl.when(jnp.logical_and(to_s[n], to_p[m]))(lambda: tip_copy(n, m).start())
    for n in range(2):
        pl.when(to_far[n])(lambda: far_copy(n).start())
    for m in range(2):
        pl.when(to_p[m])(lambda: side_copy(m).start())
    for a, b in around:
        pl.when(exists(a, b))(lambda: w_copy(a, b).start())
    if reaches:
        near_signal(0)
    ready(9)
    for j in range(1, patches):
        point_first(j, True).start()
    ready(11)
    pl.when(has_next_p)(lambda: d_up().start())
    pl.when(has_prev_p)(lambda: d_down().start())
    ready(8, 10, 12)
    for owner in range(patches):

        @pl.when(p == owner)
        def _():
            points[s, owner] = point_ref[0, :, owner * cap : (owner + 1) * cap]

    for owner in range(patches):
        elem = elem_ref[0, :, owner * cap : (owner + 1) * cap]
        hit = (lax.broadcasted_iota(jnp.int32, (wide_lanes, cap), 0) == elem) & lives(owner)
        onehot_elem[owner] = jnp.where(hit, 1.0, 0.0).astype(BF16)
    for n in range(len(reaches)):
        with jax.named_scope("w_reach"):
            near_wait(n)
        if n + 1 < len(reaches):
            near_signal(n + 1)
        if n == 0:
            send_halos(0)
            with jax.named_scope("w_pt1"):
                for j in range(1, patches):
                    point_first(j, False).wait_recv()
            build_points(s)
    if not reaches:
        send_halos(0)
        for j in range(1, patches):
            point_first(j, False).wait_recv()
        build_points(s)
    for j in range(1, slabs):
        point_second(j, True).start()
    with jax.named_scope("shell"):
        shell()
    scales = [column(scale_ref[i : i + 1, :]) for i in range(ex)]
    inverses = [1.0 / x for x in scales]

    lane = lax.broadcasted_iota(jnp.int32, (1, wide_lanes), 1)
    low_half = lane < ey
    tail_half = lane < ey + ey // 2

    def halves(x):
        return jnp.where(low_half, x, 0.0), jnp.where(low_half, pltpu.roll(x, ey, 1), 0.0)

    span_rows = list(range(-ex, 2 * ex))
    spots_v, spots_r = [], []
    for m in range(2):
        def spot(r, j):
            return (r + ex) * wide_lanes + (wide_lanes - j if m == 0 else ey + j - 1)

        for i in range(ex):
            spots_v += [(m * DEEP + i * SWEEPS + j - 1, spot(i, j)) for j in range(1, SWEEPS + 1)]
            first = m * DEEP + ex * SWEEPS + i * (SWEEPS - 1) - 1
            spots_r += [(first + j, spot(i, j)) for j in range(1, SWEEPS)]
        for n in range(2):
            r1, r2 = (-1, -2) if n == 0 else (ex, ex + 1)
            first = 2 * DEEP + 4 * (2 * n + m)
            spots_v += [(first, spot(r1, 1)), (first + 1, spot(r1, 2)), (first + 2, spot(r2, 1))]
            spots_r += [(first + 3, spot(r1, 1))]

    def placing(spots):
        line = lax.broadcasted_iota(jnp.int32, (3 * DEEP, 1), 0)
        target = jnp.full((3 * DEEP, 1), -1, jnp.int32)
        for n, at in spots:
            target = jnp.where(line == n, at, target)
        lanes = lax.broadcasted_iota(jnp.int32, (3 * DEEP, len(span_rows) * wide_lanes), 1)
        return jnp.where(lanes == target, 1.0, 0.0).astype(BF16)

    with jax.named_scope("w_side"):
        for m in range(2):
            pl.when(from_p[m])(lambda: side_copy(m).wait_recv())
        for a, b in around:
            pl.when(exists(-a, -b))(lambda: w_copy(a, b).wait_recv())
        for n, m in corners:
            pl.when(jnp.logical_and(from_s[n], from_p[m]))(lambda: tip_copy(n, m).wait_recv())
    with jax.named_scope("place"):
        stack = join(
            *[jnp.where(from_p[m], side_in[m].astype(F32), 0.0) for m in range(2)],
            *[
                jnp.where(jnp.logical_and(from_s[n], from_p[m]), tip_in[2 * n + m].astype(F32), 0.0)
                for n, m in corners
            ],
        ).astype(BF16)
        placed_v = dot(dot_nt(words, stack).astype(BF16), placing(spots_v))
        placed_r = dot(dot_nt(rest, stack).astype(BF16), placing(spots_r))

        def piece(x, r):
            return x[:, (r + ex) * wide_lanes : (r + ex + 1) * wide_lanes]

        def weight(a, b):
            if (a, b) == (0, 0):
                return w_out[...]
            return jnp.where(exists(a, b), w_in[3 * (a + 1) + b + 1], 0.0)

        w_rows = {}
        for a in (-1, 0, 1):
            middle = weight(a, 0)
            before, after = pltpu.roll(weight(a, -1), ey, 1), pltpu.roll(weight(a, 1), ey, 1)
            both = jnp.where(low_half, middle, jnp.where(tail_half, after, before))
            for i in range(ex):
                w_rows[a * ex + i] = both[i : i + 1]

    with jax.named_scope("w_near"):
        for n in range(2):
            pl.when(from_far[n])(lambda: far_copy(n).wait_recv())
            pl.when(from_s[n])(lambda: near_copy(n).wait_recv())

    with jax.named_scope("stencil"):
        by_d, by_x, by_y, by_r2, by_r1, by_r0 = {}, {}, {}, {}, {}, {}
        for i, (v_half, r_half) in enumerate(zip(halves(own_v), halves(own_r))):
            full, side = v_half + piece(placed_v, i), r_half + piece(placed_r, i)
            by_d[i], by_x[i], by_y[i] = (full[k * 2 * DEEP : (k + 1) * 2 * DEEP] for k in range(3))
            by_r2[i], by_r1[i], by_r0[i] = (
                side[: 2 * DEEP], side[2 * DEEP : 2 * DEEP + 3 * comps], side[3 * DEEP : 3 * DEEP + comps]
            )
        for n in range(2):
            got = jnp.where(from_s[n], near_in[n].astype(F32), 0.0)
            for i, half in enumerate(halves(got)):
                r = i - ex if n == 0 else i + ex
                edge_v, edge_r = piece(placed_v, r), piece(placed_r, r)
                by_d[r] = half[0:DEEP] + edge_v[0:DEEP]
                by_x[r] = half[DEEP : 3 * DEEP] + edge_v[2 * DEEP : 4 * DEEP]
                by_y[r] = half[3 * DEEP : 4 * DEEP] + edge_v[4 * DEEP : 5 * DEEP]
                by_r2[r] = half[4 * DEEP : 5 * DEEP] + edge_r[0:DEEP]
                by_r1[r] = half[3 * DEEP - comps - 1 : 3 * DEEP - 1]
            beyond = halves(jnp.where(from_far[n], far_in[n].astype(F32), 0.0))[1 - n]
            by_x[-ex - 1 if n == 0 else 2 * ex] = join(beyond, blank(DEEP - 8, wide_lanes))

        def turn(x):
            return pltpu.roll(x, 1, 1) + pltpu.roll(x, wide_lanes - 1, 1)

        one = {}
        for r in span_rows:
            n = 2 * DEEP if 0 <= r < ex else DEEP
            one[r] = by_d[r] + w_rows[r] * (by_x[r - 1][:n] + by_x[r + 1][:n] + turn(by_y[r]) + by_r2[r])
        two = {}
        for r in range(-1, ex + 1):
            if 0 <= r < ex:
                d_part = join(one[r][:comps], one[r][DEEP : DEEP + 2 * comps])
                y_part = join(one[r][4 * comps : 5 * comps], one[r][DEEP + 2 * comps : DEEP + 4 * comps])
                n = 3 * comps
            else:
                d_part, y_part = one[r][:comps], one[r][4 * comps : 5 * comps]
                n = comps
            x_part = one[r - 1][comps : comps + n] + one[r + 1][comps : comps + n]
            two[r] = d_part + w_rows[r] * (x_part + turn(y_part) + by_r1[r])
        drawn = []
        for r in range(ex):
            x_part = two[r - 1][:comps] + two[r + 1][:comps]
            drawn.append(
                two[r][comps : 2 * comps]
                + w_rows[r] * (x_part + turn(two[r][2 * comps : 3 * comps]) + by_r0[r])
            )
        traction = jnp.where(low_half, drawn[0], pltpu.roll(drawn[1], ey, 1)).astype(BF16)
        for owner in range(patches):
            pull_out[owner] = dot(traction, onehot_elem[owner]).astype(BF16)
    with jax.named_scope("s_pull"):
        for j in sorted(range(slabs), key=lambda j: -min(j, slabs - j)):
            for i in range(patches):
                if (j, i) != (0, 0):
                    pull_copy(j, i).start()
    pulls[s, p] = pull_out[p]

    def sweep(k, v):
        rounded = rounded0 if k == 0 else vb[k]
        own = dot(rounded.reshape(ex * ey, dof), matrix_ref[...]).reshape(ex, ey, dof)
        base = [rhs_ref[i] - scales[i] * own[i] for i in range(ex)]
        wide = rounded.astype(F32)
        with jax.named_scope("w_halo"):
            pl.when(has_prev_p)(lambda: y_up(k).wait_recv())
            pl.when(has_next_p)(lambda: y_down(k).wait_recv())
            pl.when(has_prev_s)(lambda: x_up(k).wait_recv())
            pl.when(has_next_s)(lambda: x_down(k).wait_recv())
        line = lax.broadcasted_iota(jnp.int32, (ey, dof), 0)
        along_y = []
        for i in range(ex):
            before = halo_y[k, 0, i].astype(F32)[PACK - 1 : PACK]
            after = halo_y[k, 1, i].astype(F32)[0:1]
            before = jnp.where(has_prev_p, before, 0.0)
            after = jnp.where(has_next_p, after, 0.0)
            prev = jnp.where(line == 0, jnp.broadcast_to(before, (ey, dof)), pltpu.roll(wide[i], 1, 0))
            following = jnp.where(line == ey - 1, jnp.broadcast_to(after, (ey, dof)), pltpu.roll(wide[i], ey - 1, 0))
            along_y.append((prev + following).astype(BF16))
        side_y = dot(jnp.concatenate(along_y, axis=0), cy_ref[...])
        low = jnp.where(has_prev_s, halo_x[k, 0].astype(F32), 0.0)
        high = jnp.where(has_next_s, halo_x[k, 1].astype(F32), 0.0)
        along_x = []
        for i in range(ex):
            below = low if i == 0 else wide[i - 1]
            above = high if i == ex - 1 else wide[i + 1]
            along_x.append((below + above).astype(BF16))
        side_x = dot(jnp.concatenate(along_x, axis=0), cx_ref[...])
        side = (side_x + side_y).reshape(ex, ey, dof)
        residue = jnp.concatenate([(base[i] + side[i]).astype(BF16) for i in range(ex)], axis=0)
        update = dot(residue, inverse_ref[...]).reshape(ex, ey, dof)
        return [v[i] + update[i] * inverses[i] for i in range(ex)]

    def keep(v, k):
        for i in range(ex):
            fluid_ref[i] = v[i]
            if k < SWEEPS:
                vb[k, i] = v[i].astype(BF16)

    with jax.named_scope("sweep0"):
        keep(sweep(0, state_ref), 1)
        send_halos(1)

    def scatter(slab, acc):
        for k in range(patches):
            span = pl.ds(k * cap, cap)
            hot = onehot_row[slab, :, span]
            value = pulls[slab, k]
            scaled = jnp.concatenate([hot * value[c : c + 1] for c in range(comps)], axis=0)
            acc = acc + dot_nt(scaled, onehot_col[slab, :, span])
        return acc

    for i in range(1, patches):
        pull_arrival(s, patch_peer(i)).wait_recv()
    acc = scatter(s, jnp.zeros((comps * rows, cols), F32))
    inner = jnp.minimum(s, slabs - 1 - s)

    def nearest(t):
        step = lax.div(t + 1, 2)
        alternate = jnp.where(lax.rem(t, 2) == 1, s + step, s - step)
        return jnp.where(t <= 2 * inner, alternate, jnp.where(s < slabs - 1 - s, t, slabs - 1 - t))

    def gathered(t, acc):
        slab = nearest(t)
        with jax.named_scope("w_point"):
            remote(points.at[s], points.at[slab], sp2.at[0], rp2.at[slab], (slab, p)).wait_recv()
        build_points(slab)
        with jax.named_scope("w_pull"):
            for i in range(patches):
                pull_arrival(slab, i).wait_recv()
        return scatter(slab, acc)

    half = (slabs + 1) // 2
    with jax.named_scope("gather1"):
        acc = lax.fori_loop(1, half, gathered, acc)
    with jax.named_scope("sweep1"):
        keep(sweep(1, fluid_ref), 2)
        send_halos(2)
    with jax.named_scope("gather2"):
        acc = lax.fori_loop(half, slabs, gathered, acc)
    loads = acc.reshape(comps, rows, cols)
    fresh = [rest_buf[c] + loads[c] * gain_buf[...] for c in range(comps)]
    narrow = jnp.concatenate([x.astype(BF16) for x in fresh], axis=0)
    for k in range(patches):
        span = pl.ds(k * cap, cap)
        spread = dot(narrow, onehot_col[s, :, span]).reshape(comps, rows, cap)
        hot = onehot_row[s, :, span].astype(F32)
        for c in range(comps):
            picks_out[k, c : c + 1] = jnp.sum(spread[c] * hot, axis=0, keepdims=True)
    with jax.named_scope("s_pick"):
        for j in range(1, patches):
            pick_copy(j, True).start()
    picks_in[p] = picks_out[p]
    for c in range(comps):
        net_ref[c] = fresh[c]
    with jax.named_scope("sweep2"):
        keep(sweep(2, fluid_ref), SWEEPS)
    with jax.named_scope("w_pick"):
        for j in range(1, patches):
            pick_copy(j, False).wait_recv()
    for k in range(patches):
        live = lives(k)
        for c in range(comps):
            wall_ref[c, 0, :, k * cap : (k + 1) * cap] = jnp.where(live, picks_in[k, c : c + 1], 0.0)

    with jax.named_scope("drain"):
        for k in range(SWEEPS):
            pl.when(has_next_s)(lambda: x_up(k).wait_send())
            pl.when(has_prev_s)(lambda: x_down(k).wait_send())
            pl.when(has_next_p)(lambda: y_up(k).wait_send())
            pl.when(has_prev_p)(lambda: y_down(k).wait_send())
        pl.when(has_next_p)(lambda: d_up().wait_send())
        pl.when(has_prev_p)(lambda: d_down().wait_send())
        for n in range(2):
            pl.when(to_s[n])(lambda: near_copy(n).wait_send())
            pl.when(to_far[n])(lambda: far_copy(n).wait_send())
            pl.when(to_p[n])(lambda: side_copy(n).wait_send())
        for n, m in corners:
            pl.when(jnp.logical_and(to_s[n], to_p[m]))(lambda: tip_copy(n, m).wait_send())
        for a, b in around:
            pl.when(exists(a, b))(lambda: w_copy(a, b).wait_send())
        for j in range(1, patches):
            point_first(j, True).wait_send()
            pick_copy(j, True).wait_send()
        for j in range(1, slabs):
            point_second(j, True).wait_send()
        for j in range(slabs):
            for i in range(patches):
                if (j, i) != (0, 0):
                    pull_copy(j, i).wait_send()


def deliver(*refs):
    copies = [pltpu.make_async_copy(refs[n], refs[n + 3], refs[6].at[n]) for n in range(3)]
    for copy in copies:
        copy.start()
    for copy in copies:
        copy.wait()


def shards(slabs, patches, *args):
    state, disp, elem = args[0], args[11], args[8]
    ex, ey, dof = state.shape
    comps, rows, cols = disp.shape
    cap = elem.shape[2] // patches
    sem = pltpu.SemaphoreType.DMA
    vmem = pl.BlockSpec(memory_space=pltpu.VMEM)
    hot_bytes = slabs * patches * cap * (rows + cols) * 2
    outs = pl.pallas_call(
        functools.partial(kernel, slabs, patches, len(args)),
        out_shape=(
            jax.ShapeDtypeStruct(state.shape, F32),
            jax.ShapeDtypeStruct(disp.shape, F32),
            jax.ShapeDtypeStruct((comps, 1, 1, elem.shape[2]), F32),
        ),
        in_specs=[pl.BlockSpec(memory_space=pltpu.HBM)] * len(args),
        out_specs=(vmem, vmem, vmem),
        scratch_shapes=[pltpu.VMEM(x.shape, x.dtype) for x in args]
        + [
            pltpu.VMEM((SWEEPS, ex, ey, dof), BF16),
            pltpu.VMEM((SWEEPS, 2, ey, dof), BF16),
            pltpu.VMEM((SWEEPS, 2, ex, PACK, dof), BF16),
            pltpu.VMEM((2, comps, EDGE, cols), F32),
            pltpu.VMEM((slabs, patches, 1, cap), jnp.int32),
            pltpu.VMEM((slabs, patches, comps, cap), BF16),
            pltpu.VMEM((patches, comps, cap), BF16),
            pltpu.VMEM((patches, comps, cap), F32),
            pltpu.VMEM((patches, comps, cap), F32),
            pltpu.VMEM((patches, ex * ey, cap), BF16),
            pltpu.VMEM((slabs, rows, patches * cap), BF16),
            pltpu.VMEM((slabs, cols, patches * cap), BF16),
            pltpu.VMEM((comps, rows, cols), F32),
            pltpu.VMEM((rows, cols), F32),
            pltpu.VMEM((5 * DEEP, ex * ey), BF16),
            pltpu.VMEM((2, 5 * DEEP, ex * ey), BF16),
            pltpu.VMEM((8, ex * ey), BF16),
            pltpu.VMEM((2, 8, ex * ey), BF16),
            pltpu.VMEM((2, DEEP, dof), BF16),
            pltpu.VMEM((2, DEEP, dof), BF16),
            pltpu.VMEM((4, 4, dof), BF16),
            pltpu.VMEM((4, 4, dof), BF16),
            pltpu.VMEM((ex, 2 * ey), F32),
            pltpu.VMEM((9, ex, 2 * ey), F32),
            sem((len(args),)),
            sem((SWEEPS, 2)),
            sem((SWEEPS, 2)),
            sem((SWEEPS, 2)),
            sem((SWEEPS, 2)),
            sem((2,)),
            sem((2,)),
            sem((patches,)),
            sem((patches,)),
            sem((slabs,)),
            sem((slabs,)),
            sem((slabs, patches)),
            sem((slabs, patches)),
            sem((patches,)),
            sem((patches,)),
            sem((2,)),
            sem((2,)),
            sem((2,)),
            sem((2,)),
            sem((2,)),
            sem((2,)),
            sem((4,)),
            sem((4,)),
            sem((9,)),
            sem((9,)),
            pltpu.SemaphoreType.REGULAR((max(slabs.bit_length(), 1),)),
        ],
        compiler_params=pltpu.CompilerParams(collective_id=0, has_side_effects=True),
    )(*args)
    return pl.pallas_call(
        deliver,
        out_shape=tuple(jax.ShapeDtypeStruct(x.shape, x.dtype) for x in outs),
        in_specs=[vmem] * 3,
        out_specs=(pl.BlockSpec(memory_space=pltpu.HBM),) * 3,
        scratch_shapes=[sem((3,))],
    )(*outs)


def solution(mesh):
    return jax.shard_map(
        functools.partial(shards, mesh.shape["slab"], mesh.shape["patch"]),
        mesh=mesh,
        in_specs=(
            P("slab", "patch", None),
            P("slab", "patch", None),
            P("slab", "patch"),
            P(),
            P(),
            P(),
            P(),
            P(),
            P("slab", "patch", None),
            P("slab", "patch", None),
            P("slab", "patch", None),
            P(None, "patch", None),
            P("patch", None),
        ),
        out_specs=(
            P("slab", "patch", None),
            P(None, "patch", None),
            P(None, "slab", "patch", None),
        ),
        check_vma=False,
    )
```

```python
import functools

import jax
import jax.numpy as jnp
from jax import lax
from jax.experimental import pallas as pl
from jax.experimental.pallas import tpu as pltpu
from jax.sharding import PartitionSpec as P

SWEEPS = 3
PACK = 16
EDGE = 8
SPARE = 8 * 2**20
DEEP = 16
LOAD_ORDER = (7, 6, 3, 4, 5, 2, 0, 1, 9, 8, 10, 11, 12)
MESH = pl.DeviceIdType.MESH
F32 = jnp.float32
BF16 = jnp.bfloat16


def dot(a, b):
    return jnp.dot(a, b, preferred_element_type=F32)


def dot_nt(a, b):
    return lax.dot_general(a, b, (((1,), (1,)), ((), ())), preferred_element_type=F32)


def split_point(point, cols):
    if cols & (cols - 1) == 0:
        return lax.shift_right_logical(point, cols.bit_length() - 1), point & (cols - 1)
    row = lax.div(point, cols)
    return row, point - row * cols


def column(row_vector):
    n = row_vector.shape[1]
    shape = (n, n)
    eye = lax.broadcasted_iota(jnp.int32, shape, 0) == lax.broadcasted_iota(jnp.int32, shape, 1)
    return jnp.sum(jnp.where(eye, jnp.broadcast_to(row_vector, shape), 0.0), axis=1, keepdims=True)


def laplace(x):
    rows, cols = x.shape
    lane = lax.broadcasted_iota(jnp.int32, x.shape, 1)
    left = jnp.where(lane == 0, 0.0, pltpu.roll(x, 1, 1))
    right = jnp.where(lane == cols - 1, 0.0, pltpu.roll(x, cols - 1, 1))
    return 4.0 * x - (pltpu.roll(x, 1, 0) + pltpu.roll(x, rows - 1, 0) + left + right)


def join(*parts):
    return jnp.concatenate(parts, axis=0)


def blank(rows, cols):
    return jnp.zeros((rows, cols), F32)


def make_words(traction, inverse, matrix, couple_x, couple_y):
    comps, dof = traction.shape
    base0 = dot_nt(traction, inverse)
    low = base0.astype(BF16)
    one = join(dot_nt(low, couple_x), traction.astype(F32) - dot_nt(low, matrix), dot_nt(low, couple_y))
    base1 = dot_nt(one.astype(BF16), inverse)
    low = base1.astype(BF16)
    by_x, by_y = dot_nt(low, couple_x), dot_nt(low, couple_y)
    by_d = one - dot_nt(low, matrix)
    two = join(
        by_d[:comps], by_x, by_y[:comps], blank(DEEP - 5 * comps, dof),
        by_d[comps:], by_y[comps:], blank(DEEP - 4 * comps, dof),
    )
    base2 = dot_nt(two.astype(BF16), inverse)
    low = base2.astype(BF16)
    three = join(two - dot_nt(low, matrix), dot_nt(low, couple_x), dot_nt(low, couple_y))
    rest = join(base2, base1, blank(DEEP - 3 * comps, dof), base0, blank(DEEP - comps, dof))
    return three.astype(BF16), rest.astype(BF16)


def kernel(slabs, patches, args, *refs):
    hbm, refs = refs[:args], refs[args:]
    (fluid_ref, net_ref, wall_ref), refs = refs[:3], refs[3:]
    staged, refs = refs[:args], refs[args:]
    (state_ref, rhs_ref, scale_ref, matrix_ref, cx_ref, cy_ref, inverse_ref, traction_ref) = staged[:8]
    (elem_ref, point_ref, count_ref, disp_ref, stiff_ref) = staged[8:]
    (vb, halo_x, halo_y, halo_d, points, pulls, pull_out, picks_out, picks_in) = refs[:9]
    (onehot_elem, onehot_row, onehot_col, rest_buf, gain_buf) = refs[9:14]
    (near_out, near_in, far_out, far_in, side_out, side_in, tip_out, tip_in, w_out, w_in) = refs[14:24]
    (load_sem, sx, rx, sy, ry, sd, rd, sp1, rp1, sp2, rp2, sq, rq, sw, rw) = refs[24:39]
    (s_near, r_near, s_far, r_far, s_side, r_side, s_tip, r_tip, s_w, r_w, near_sem) = refs[39:]

    loads_in = [pltpu.make_async_copy(hbm[n], staged[n], load_sem.at[n]) for n in range(args)]
    for n in LOAD_ORDER:
        loads_in[n].start()

    def ready(*names):
        for n in names:
            loads_in[n].wait()

    s = lax.axis_index("slab")
    p = lax.axis_index("patch")
    ex, ey, dof = state_ref.shape
    comps, rows, cols = disp_ref.shape
    cap = elem_ref.shape[2] // patches
    wide_lanes = ex * ey

    def slab_peer(j):
        return lax.rem(s + j, slabs)

    def patch_peer(j):
        return lax.rem(p + j, patches)

    def slab_sides(reach, semaphore):
        @pl.when(s >= reach)
        def _():
            pl.semaphore_signal(semaphore, inc=1, device_id=(s - reach, p), device_id_type=MESH)

        @pl.when(s + reach < slabs)
        def _():
            pl.semaphore_signal(semaphore, inc=1, device_id=(s + reach, p), device_id_type=MESH)

    def slab_count(reach):
        return jnp.where(s >= reach, 1, 0) + jnp.where(s + reach < slabs, 1, 0)

    reaches = []
    while 2 ** (len(reaches) + 1) < slabs - 1:
        reaches.append(2 ** (len(reaches) + 1))

    def near_signal(n):
        slab_sides(reaches[n], near_sem.at[n])

    def near_wait(n):
        pl.semaphore_wait(near_sem.at[n], slab_count(reaches[n]))

    has_prev_s, has_next_s = s > 0, s < slabs - 1
    has_prev_p, has_next_p = p > 0, p < patches - 1
    has_far_prev, has_far_next = s > 1, s < slabs - 2

    barrier = pltpu.get_barrier_semaphore()
    for j in range(1, patches):
        pl.semaphore_signal(barrier, inc=1, device_id=(s, patch_peer(j)), device_id_type=MESH)
    for reach in (1, 2):

        @pl.when(s >= reach)
        def _():
            for j in range(patches):
                pl.semaphore_signal(barrier, inc=1, device_id=(s - reach, patch_peer(j)), device_id_type=MESH)

        @pl.when(s + reach < slabs)
        def _():
            for j in range(patches):
                pl.semaphore_signal(barrier, inc=1, device_id=(s + reach, patch_peer(j)), device_id_type=MESH)

    awaited = patches - 1 + patches * (slab_count(1) + slab_count(2))

    def remote(src, dst, send, recv, target):
        return pltpu.make_async_remote_copy(
            src_ref=src, dst_ref=dst, send_sem=send, recv_sem=recv, device_id=target, device_id_type=MESH
        )

    def slab_at(step):
        return jnp.clip(s + step, 0, slabs - 1)

    def patch_at(step):
        return jnp.clip(p + step, 0, patches - 1)

    def x_up(k):
        return remote(vb.at[k, ex - 1], halo_x.at[k, 0], sx.at[k, 0], rx.at[k, 0], (slab_at(1), p))

    def x_down(k):
        return remote(vb.at[k, 0], halo_x.at[k, 1], sx.at[k, 1], rx.at[k, 1], (slab_at(-1), p))

    def y_up(k):
        return remote(
            vb.at[k, :, pl.ds(ey - PACK, PACK)], halo_y.at[k, 0], sy.at[k, 0], ry.at[k, 0], (s, patch_at(1))
        )

    def y_down(k):
        return remote(vb.at[k, :, pl.ds(0, PACK)], halo_y.at[k, 1], sy.at[k, 1], ry.at[k, 1], (s, patch_at(-1)))

    def d_up():
        return remote(disp_ref.at[:, pl.ds(rows - EDGE, EDGE)], halo_d.at[0], sd.at[0], rd.at[0], (s, patch_at(1)))

    def d_down():
        return remote(disp_ref.at[:, pl.ds(0, EDGE)], halo_d.at[1], sd.at[1], rd.at[1], (s, patch_at(-1)))

    def near_copy(n):
        return remote(near_out, near_in.at[n], s_near.at[n], r_near.at[n], (slab_at(1 - 2 * n), p))

    def far_copy(n):
        return remote(far_out, far_in.at[n], s_far.at[n], r_far.at[n], (slab_at(2 - 4 * n), p))

    def side_copy(n):
        return remote(side_out.at[n], side_in.at[n], s_side.at[n], r_side.at[n], (s, patch_at(1 - 2 * n)))

    def tip_copy(n, m):
        q = 2 * n + m
        return remote(tip_out.at[q], tip_in.at[q], s_tip.at[q], r_tip.at[q], (slab_at(1 - 2 * n), patch_at(1 - 2 * m)))

    def w_copy(a, b):
        q = 3 * (1 - a) + 1 - b
        return remote(w_out, w_in.at[q], s_w.at[q], r_w.at[q], (slab_at(a), patch_at(b)))

    to_s, from_s = (has_next_s, has_prev_s), (has_prev_s, has_next_s)
    to_p, from_p = (has_next_p, has_prev_p), (has_prev_p, has_next_p)
    to_far, from_far = (has_far_next, has_far_prev), (has_far_prev, has_far_next)
    corners = [(n, m) for n in range(2) for m in range(2)]
    around = [(a, b) for a in (-1, 0, 1) for b in (-1, 0, 1) if (a, b) != (0, 0)]

    def exists(a, b):
        ok_s = {-1: has_prev_s, 0: None, 1: has_next_s}[a]
        ok_p = {-1: has_prev_p, 0: None, 1: has_next_p}[b]
        if ok_s is None:
            return ok_p
        return ok_s if ok_p is None else jnp.logical_and(ok_s, ok_p)

    def point_first(j, mine):
        peer = patch_peer(j)
        src = point_ref.at[0, :, pl.ds(pl.multiple_of(peer * cap, cap), cap)]
        slot = p if mine else peer
        return remote(src, points.at[s, slot], sp1.at[j], rp1.at[slot], (s, peer))

    def point_second(j, mine):
        peer = slab_peer(j)
        slot = s if mine else peer
        return remote(points.at[s], points.at[slot], sp2.at[j], rp2.at[slot], (peer, p))

    def pull_copy(j, i):
        to = (slab_peer(j), patch_peer(i))
        return remote(pull_out.at[to[1]], pulls.at[s, p], sq.at[j, i], rq.at[s, p], to)

    def pull_arrival(slab, patch):
        return remote(pull_out.at[p], pulls.at[slab, patch], sq.at[0, 0], rq.at[slab, patch], (slab, patch))

    def pick_copy(j, mine):
        peer = patch_peer(j)
        slot = p if mine else peer
        return remote(picks_out.at[peer], picks_in.at[slot], sw.at[j], rw.at[slot], (s, peer))

    def send_halos(k):
        pl.when(has_next_s)(lambda: x_up(k).start())
        pl.when(has_prev_s)(lambda: x_down(k).start())
        pl.when(has_next_p)(lambda: y_up(k).start())
        pl.when(has_prev_p)(lambda: y_down(k).start())

    def build_points(slab):
        for k in range(patches):
            row, col = split_point(points[slab, k], cols)
            span = pl.ds(k * cap, cap)
            onehot_row[slab, :, span] = jnp.where(
                lax.broadcasted_iota(jnp.int32, (rows, cap), 0) == row, 1.0, 0.0
            ).astype(BF16)
            onehot_col[slab, :, span] = jnp.where(
                lax.broadcasted_iota(jnp.int32, (cols, cap), 0) == col, 1.0, 0.0
            ).astype(BF16)

    def lives(k):
        lane = lax.broadcasted_iota(jnp.int32, (1, cap), 1)
        return lane < count_ref[0, :, k : k + 1]

    def shell():
        pl.when(has_prev_p)(lambda: d_up().wait_recv())
        pl.when(has_next_p)(lambda: d_down().wait_recv())
        total = rows + 2 * EDGE
        line = lax.broadcasted_iota(jnp.int32, (total, cols), 0)
        first = jnp.where(has_prev_p, 0, EDGE)
        last = jnp.where(has_next_p, total, EDGE + rows)
        valid = (line >= first) & (line < last)
        gain = 1.0 / (36.0 * stiff_ref[...])
        gain_buf[...] = gain
        for c in range(comps):
            field = jnp.concatenate([halo_d[0, c], disp_ref[c], halo_d[1, c]], axis=0)
            field = jnp.where(valid, field, 0.0)
            bend = jnp.where(valid, laplace(field), 0.0)
            full = (laplace(bend) + 4.0 * bend)[EDGE : EDGE + rows]
            rest_buf[c] = disp_ref[c] - stiff_ref[...] * full * gain

    with jax.named_scope("words"):
        ready(7, 6, 4, 3, 5)
        words, rest = make_words(
            traction_ref[...], inverse_ref[...], matrix_ref[...], cx_ref[...], cy_ref[...]
        )
    ready(2)
    w_out[...] = blank(*w_out.shape)
    w_out[:, 0:ey] = 1.0 / scale_ref[...]
    ready(0)
    rounded0 = state_ref[...].astype(BF16)
    vb[0] = rounded0
    ready(1)
    wet = rhs_ref[...].astype(BF16)
    with jax.named_scope("project"):
        own_v = dot_nt(words, rounded0.reshape(wide_lanes, dof))
        own_r = dot_nt(rest, wet.reshape(wide_lanes, dof))
        spare = join(blank(2 * DEEP - comps - 1, wide_lanes), own_r[2 * DEEP : 2 * DEEP + comps], blank(1, wide_lanes))
        near_out[...] = join(
            own_v[0:DEEP], own_v[2 * DEEP : 4 * DEEP] + spare, own_v[4 * DEEP : 5 * DEEP], own_r[0:DEEP]
        ).astype(BF16)
        far_out[...] = own_v[2 * DEEP : 2 * DEEP + 8].astype(BF16)

        def state_at(i, c):
            return state_ref[i, c : c + 1]

        def rhs_at(i, c):
            return rhs_ref[i, c : c + 1]

        for m in range(2):
            edge = [ey - 1 - j if m == 0 else j for j in range(SWEEPS)]
            lines = [state_at(i, c) for i in range(ex) for c in edge]
            lines += [rhs_at(i, c) for i in range(ex) for c in edge[: SWEEPS - 1]]
            side_out[m] = join(*lines, blank(DEEP - len(lines), dof)).astype(BF16)
            for n in range(2):
                order = [ex - 1, ex - 2] if n == 0 else [0, 1]
                tip_out[2 * n + m] = join(
                    state_at(order[0], edge[0]),
                    state_at(order[0], edge[1]),
                    state_at(order[1], edge[0]),
                    rhs_at(order[0], edge[0]),
                ).astype(BF16)

    with jax.named_scope("w_barrier"):
        pl.semaphore_wait(barrier, awaited)
    for n in range(2):
        pl.when(to_s[n])(lambda: near_copy(n).start())
    for n, m in corners:
        pl.when(jnp.logical_and(to_s[n], to_p[m]))(lambda: tip_copy(n, m).start())
    for n in range(2):
        pl.when(to_far[n])(lambda: far_copy(n).start())
    for m in range(2):
        pl.when(to_p[m])(lambda: side_copy(m).start())
    for a, b in around:
        pl.when(exists(a, b))(lambda: w_copy(a, b).start())
    if reaches:
        near_signal(0)
    ready(9)
    for j in range(1, patches):
        point_first(j, True).start()
    ready(11)
    pl.when(has_next_p)(lambda: d_up().start())
    pl.when(has_prev_p)(lambda: d_down().start())
    ready(8, 10, 12)
    for owner in range(patches):

        @pl.when(p == owner)
        def _():
            points[s, owner] = point_ref[0, :, owner * cap : (owner + 1) * cap]

    for owner in range(patches):
        elem = elem_ref[0, :, owner * cap : (owner + 1) * cap]
        hit = (lax.broadcasted_iota(jnp.int32, (wide_lanes, cap), 0) == elem) & lives(owner)
        onehot_elem[owner] = jnp.where(hit, 1.0, 0.0).astype(BF16)
    if reaches:
        with jax.named_scope("w_reach"):
            near_wait(0)
        if len(reaches) > 1:
            near_signal(1)
    send_halos(0)
    scales = [column(scale_ref[i : i + 1, :]) for i in range(ex)]
    inverses = [1.0 / x for x in scales]

    lane = lax.broadcasted_iota(jnp.int32, (1, wide_lanes), 1)
    low_half = lane < ey
    tail_half = lane < ey + ey // 2

    def halves(x):
        return jnp.where(low_half, x, 0.0), jnp.where(low_half, pltpu.roll(x, ey, 1), 0.0)

    span_rows = list(range(-ex, 2 * ex))
    spots_v, spots_r = [], []
    for m in range(2):
        def spot(r, j):
            return (r + ex) * wide_lanes + (wide_lanes - j if m == 0 else ey + j - 1)

        for i in range(ex):
            spots_v += [(m * DEEP + i * SWEEPS + j - 1, spot(i, j)) for j in range(1, SWEEPS + 1)]
            first = m * DEEP + ex * SWEEPS + i * (SWEEPS - 1) - 1
            spots_r += [(first + j, spot(i, j)) for j in range(1, SWEEPS)]
        for n in range(2):
            r1, r2 = (-1, -2) if n == 0 else (ex, ex + 1)
            first = 2 * DEEP + 4 * (2 * n + m)
            spots_v += [(first, spot(r1, 1)), (first + 1, spot(r1, 2)), (first + 2, spot(r2, 1))]
            spots_r += [(first + 3, spot(r1, 1))]

    def placing(spots):
        line = lax.broadcasted_iota(jnp.int32, (3 * DEEP, 1), 0)
        target = jnp.full((3 * DEEP, 1), -1, jnp.int32)
        for n, at in spots:
            target = jnp.where(line == n, at, target)
        lanes = lax.broadcasted_iota(jnp.int32, (3 * DEEP, len(span_rows) * wide_lanes), 1)
        return jnp.where(lanes == target, 1.0, 0.0).astype(BF16)

    place_v, place_r = placing(spots_v), placing(spots_r)
    for n in range(1, len(reaches)):
        with jax.named_scope("w_reach"):
            near_wait(n)
        if n + 1 < len(reaches):
            near_signal(n + 1)
    with jax.named_scope("w_pt1"):
        for j in range(1, patches):
            point_first(j, False).wait_recv()
    for j in range(1, slabs):
        point_second(j, True).start()

    with jax.named_scope("w_side"):
        for m in range(2):
            pl.when(from_p[m])(lambda: side_copy(m).wait_recv())
        for a, b in around:
            pl.when(exists(-a, -b))(lambda: w_copy(a, b).wait_recv())
        for n, m in corners:
            pl.when(jnp.logical_and(from_s[n], from_p[m]))(lambda: tip_copy(n, m).wait_recv())
    with jax.named_scope("place"):
        stack = join(
            *[jnp.where(from_p[m], side_in[m].astype(F32), 0.0) for m in range(2)],
            *[
                jnp.where(jnp.logical_and(from_s[n], from_p[m]), tip_in[2 * n + m].astype(F32), 0.0)
                for n, m in corners
            ],
        ).astype(BF16)
        placed_v = dot(dot_nt(words, stack).astype(BF16), place_v)
        placed_r = dot(dot_nt(rest, stack).astype(BF16), place_r)

        def piece(x, r):
            return x[:, (r + ex) * wide_lanes : (r + ex + 1) * wide_lanes]

        def weight(a, b):
            if (a, b) == (0, 0):
                return w_out[...]
            return jnp.where(exists(a, b), w_in[3 * (a + 1) + b + 1], 0.0)

        w_rows = {}
        for a in (-1, 0, 1):
            middle = weight(a, 0)
            before, after = pltpu.roll(weight(a, -1), ey, 1), pltpu.roll(weight(a, 1), ey, 1)
            both = jnp.where(low_half, middle, jnp.where(tail_half, after, before))
            for i in range(ex):
                w_rows[a * ex + i] = both[i : i + 1]

    with jax.named_scope("w_near"):
        for n in range(2):
            pl.when(from_far[n])(lambda: far_copy(n).wait_recv())
            pl.when(from_s[n])(lambda: near_copy(n).wait_recv())

    with jax.named_scope("stencil"):
        by_d, by_x, by_y, by_r2, by_r1, by_r0 = {}, {}, {}, {}, {}, {}
        for i, (v_half, r_half) in enumerate(zip(halves(own_v), halves(own_r))):
            full, side = v_half + piece(placed_v, i), r_half + piece(placed_r, i)
            by_d[i], by_x[i], by_y[i] = (full[k * 2 * DEEP : (k + 1) * 2 * DEEP] for k in range(3))
            by_r2[i], by_r1[i], by_r0[i] = (
                side[: 2 * DEEP], side[2 * DEEP : 2 * DEEP + 3 * comps], side[3 * DEEP : 3 * DEEP + comps]
            )
        for n in range(2):
            got = jnp.where(from_s[n], near_in[n].astype(F32), 0.0)
            for i, half in enumerate(halves(got)):
                r = i - ex if n == 0 else i + ex
                edge_v, edge_r = piece(placed_v, r), piece(placed_r, r)
                by_d[r] = half[0:DEEP] + edge_v[0:DEEP]
                by_x[r] = half[DEEP : 3 * DEEP] + edge_v[2 * DEEP : 4 * DEEP]
                by_y[r] = half[3 * DEEP : 4 * DEEP] + edge_v[4 * DEEP : 5 * DEEP]
                by_r2[r] = half[4 * DEEP : 5 * DEEP] + edge_r[0:DEEP]
                by_r1[r] = half[3 * DEEP - comps - 1 : 3 * DEEP - 1]
            beyond = halves(jnp.where(from_far[n], far_in[n].astype(F32), 0.0))[1 - n]
            by_x[-ex - 1 if n == 0 else 2 * ex] = join(beyond, blank(DEEP - 8, wide_lanes))

        def turn(x):
            return pltpu.roll(x, 1, 1) + pltpu.roll(x, wide_lanes - 1, 1)

        one = {}
        for r in span_rows:
            n = 2 * DEEP if 0 <= r < ex else DEEP
            one[r] = by_d[r] + w_rows[r] * (by_x[r - 1][:n] + by_x[r + 1][:n] + turn(by_y[r]) + by_r2[r])
        two = {}
        for r in range(-1, ex + 1):
            if 0 <= r < ex:
                d_part = join(one[r][:comps], one[r][DEEP : DEEP + 2 * comps])
                y_part = join(one[r][4 * comps : 5 * comps], one[r][DEEP + 2 * comps : DEEP + 4 * comps])
                n = 3 * comps
            else:
                d_part, y_part = one[r][:comps], one[r][4 * comps : 5 * comps]
                n = comps
            x_part = one[r - 1][comps : comps + n] + one[r + 1][comps : comps + n]
            two[r] = d_part + w_rows[r] * (x_part + turn(y_part) + by_r1[r])
        drawn = []
        for r in range(ex):
            x_part = two[r - 1][:comps] + two[r + 1][:comps]
            drawn.append(
                two[r][comps : 2 * comps]
                + w_rows[r] * (x_part + turn(two[r][2 * comps : 3 * comps]) + by_r0[r])
            )
        traction = jnp.where(low_half, drawn[0], pltpu.roll(drawn[1], ey, 1)).astype(BF16)
        for owner in range(patches):
            pull_out[owner] = dot(traction, onehot_elem[owner]).astype(BF16)
    with jax.named_scope("s_pull"):
        for j in sorted(range(slabs), key=lambda j: -min(j, slabs - j)):
            for i in range(patches):
                if (j, i) != (0, 0):
                    pull_copy(j, i).start()
    pulls[s, p] = pull_out[p]

    def sweep(k, v):
        rounded = rounded0 if k == 0 else vb[k]
        own = dot(rounded.reshape(ex * ey, dof), matrix_ref[...]).reshape(ex, ey, dof)
        base = [rhs_ref[i] - scales[i] * own[i] for i in range(ex)]
        wide = rounded.astype(F32)
        with jax.named_scope("w_halo"):
            pl.when(has_prev_p)(lambda: y_up(k).wait_recv())
            pl.when(has_next_p)(lambda: y_down(k).wait_recv())
            pl.when(has_prev_s)(lambda: x_up(k).wait_recv())
            pl.when(has_next_s)(lambda: x_down(k).wait_recv())
        line = lax.broadcasted_iota(jnp.int32, (ey, dof), 0)
        along_y = []
        for i in range(ex):
            before = halo_y[k, 0, i].astype(F32)[PACK - 1 : PACK]
            after = halo_y[k, 1, i].astype(F32)[0:1]
            before = jnp.where(has_prev_p, before, 0.0)
            after = jnp.where(has_next_p, after, 0.0)
            prev = jnp.where(line == 0, jnp.broadcast_to(before, (ey, dof)), pltpu.roll(wide[i], 1, 0))
            following = jnp.where(line == ey - 1, jnp.broadcast_to(after, (ey, dof)), pltpu.roll(wide[i], ey - 1, 0))
            along_y.append((prev + following).astype(BF16))
        side_y = dot(jnp.concatenate(along_y, axis=0), cy_ref[...])
        low = jnp.where(has_prev_s, halo_x[k, 0].astype(F32), 0.0)
        high = jnp.where(has_next_s, halo_x[k, 1].astype(F32), 0.0)
        along_x = []
        for i in range(ex):
            below = low if i == 0 else wide[i - 1]
            above = high if i == ex - 1 else wide[i + 1]
            along_x.append((below + above).astype(BF16))
        side_x = dot(jnp.concatenate(along_x, axis=0), cx_ref[...])
        side = (side_x + side_y).reshape(ex, ey, dof)
        residue = jnp.concatenate([(base[i] + side[i]).astype(BF16) for i in range(ex)], axis=0)
        update = dot(residue, inverse_ref[...]).reshape(ex, ey, dof)
        return [v[i] + update[i] * inverses[i] for i in range(ex)]

    def keep(v, k):
        for i in range(ex):
            fluid_ref[i] = v[i]
            if k < SWEEPS:
                vb[k, i] = v[i].astype(BF16)

    with jax.named_scope("sweep0"):
        keep(sweep(0, state_ref), 1)
        send_halos(1)

    def scatter(slab, acc):
        for k in range(patches):
            span = pl.ds(k * cap, cap)
            hot = onehot_row[slab, :, span]
            value = pulls[slab, k]
            scaled = jnp.concatenate([hot * value[c : c + 1] for c in range(comps)], axis=0)
            acc = acc + dot_nt(scaled, onehot_col[slab, :, span])
        return acc

    inner = jnp.minimum(s, slabs - 1 - s)

    def nearest(t):
        step = lax.div(t + 1, 2)
        alternate = jnp.where(lax.rem(t, 2) == 1, s + step, s - step)
        return jnp.where(t <= 2 * inner, alternate, jnp.where(s < slabs - 1 - s, t, slabs - 1 - t))

    def prepared(t, carry):
        slab = nearest(t)
        with jax.named_scope("w_point"):
            remote(points.at[s], points.at[slab], sp2.at[0], rp2.at[slab], (slab, p)).wait_recv()
        build_points(slab)
        return carry

    def gathered(t, acc):
        slab = nearest(t)
        with jax.named_scope("w_pull"):
            for i in range(patches):
                pull_arrival(slab, i).wait_recv()
        return scatter(slab, acc)

    half = (slabs + 1) // 2
    build_points(s)
    with jax.named_scope("shell"):
        shell()
    with jax.named_scope("build1"):
        lax.fori_loop(1, half, prepared, 0)
    with jax.named_scope("w_own"):
        for i in range(1, patches):
            pull_arrival(s, patch_peer(i)).wait_recv()
    acc = scatter(s, jnp.zeros((comps * rows, cols), F32))
    with jax.named_scope("gather1"):
        acc = lax.fori_loop(1, half, gathered, acc)
    with jax.named_scope("build2"):
        lax.fori_loop(half, slabs, prepared, 0)
    with jax.named_scope("sweep1"):
        keep(sweep(1, fluid_ref), 2)
        send_halos(2)
    with jax.named_scope("gather2"):
        acc = lax.fori_loop(half, slabs, gathered, acc)
    loads = acc.reshape(comps, rows, cols)
    fresh = [rest_buf[c] + loads[c] * gain_buf[...] for c in range(comps)]
    narrow = jnp.concatenate([x.astype(BF16) for x in fresh], axis=0)
    for k in range(patches):
        span = pl.ds(k * cap, cap)
        spread = dot(narrow, onehot_col[s, :, span]).reshape(comps, rows, cap)
        hot = onehot_row[s, :, span].astype(F32)
        for c in range(comps):
            picks_out[k, c : c + 1] = jnp.sum(spread[c] * hot, axis=0, keepdims=True)
    with jax.named_scope("s_pick"):
        for j in range(1, patches):
            pick_copy(j, True).start()
    picks_in[p] = picks_out[p]
    for c in range(comps):
        net_ref[c] = fresh[c]
    with jax.named_scope("sweep2"):
        keep(sweep(2, fluid_ref), SWEEPS)
    with jax.named_scope("w_pick"):
        for j in range(1, patches):
            pick_copy(j, False).wait_recv()
    for k in range(patches):
        live = lives(k)
        for c in range(comps):
            wall_ref[c, 0, :, k * cap : (k + 1) * cap] = jnp.where(live, picks_in[k, c : c + 1], 0.0)

    with jax.named_scope("drain"):
        for k in range(SWEEPS):
            pl.when(has_next_s)(lambda: x_up(k).wait_send())
            pl.when(has_prev_s)(lambda: x_down(k).wait_send())
            pl.when(has_next_p)(lambda: y_up(k).wait_send())
            pl.when(has_prev_p)(lambda: y_down(k).wait_send())
        pl.when(has_next_p)(lambda: d_up().wait_send())
        pl.when(has_prev_p)(lambda: d_down().wait_send())
        for n in range(2):
            pl.when(to_s[n])(lambda: near_copy(n).wait_send())
            pl.when(to_far[n])(lambda: far_copy(n).wait_send())
            pl.when(to_p[n])(lambda: side_copy(n).wait_send())
        for n, m in corners:
            pl.when(jnp.logical_and(to_s[n], to_p[m]))(lambda: tip_copy(n, m).wait_send())
        for a, b in around:
            pl.when(exists(a, b))(lambda: w_copy(a, b).wait_send())
        for j in range(1, patches):
            point_first(j, True).wait_send()
            pick_copy(j, True).wait_send()
        for j in range(1, slabs):
            point_second(j, True).wait_send()
        for j in range(slabs):
            for i in range(patches):
                if (j, i) != (0, 0):
                    pull_copy(j, i).wait_send()


def deliver(*refs):
    copies = [pltpu.make_async_copy(refs[n], refs[n + 3], refs[6].at[n]) for n in range(3)]
    for copy in copies:
        copy.start()
    for copy in copies:
        copy.wait()


def shards(slabs, patches, *args):
    state, disp, elem = args[0], args[11], args[8]
    ex, ey, dof = state.shape
    comps, rows, cols = disp.shape
    cap = elem.shape[2] // patches
    sem = pltpu.SemaphoreType.DMA
    vmem = pl.BlockSpec(memory_space=pltpu.VMEM)
    hot_bytes = slabs * patches * cap * (rows + cols) * 2
    outs = pl.pallas_call(
        functools.partial(kernel, slabs, patches, len(args)),
        out_shape=(
            pltpu.VMEM(state.shape, F32),
            pltpu.VMEM(disp.shape, F32),
            pltpu.VMEM((comps, 1, 1, elem.shape[2]), F32),
        ),
        in_specs=[pl.BlockSpec(memory_space=pltpu.HBM)] * len(args),
        out_specs=(vmem, vmem, vmem),
        scratch_shapes=[pltpu.VMEM(x.shape, x.dtype) for x in args]
        + [
            pltpu.VMEM((SWEEPS, ex, ey, dof), BF16),
            pltpu.VMEM((SWEEPS, 2, ey, dof), BF16),
            pltpu.VMEM((SWEEPS, 2, ex, PACK, dof), BF16),
            pltpu.VMEM((2, comps, EDGE, cols), F32),
            pltpu.VMEM((slabs, patches, 1, cap), jnp.int32),
            pltpu.VMEM((slabs, patches, comps, cap), BF16),
            pltpu.VMEM((patches, comps, cap), BF16),
            pltpu.VMEM((patches, comps, cap), F32),
            pltpu.VMEM((patches, comps, cap), F32),
            pltpu.VMEM((patches, ex * ey, cap), BF16),
            pltpu.VMEM((slabs, rows, patches * cap), BF16),
            pltpu.VMEM((slabs, cols, patches * cap), BF16),
            pltpu.VMEM((comps, rows, cols), F32),
            pltpu.VMEM((rows, cols), F32),
            pltpu.VMEM((5 * DEEP, ex * ey), BF16),
            pltpu.VMEM((2, 5 * DEEP, ex * ey), BF16),
            pltpu.VMEM((8, ex * ey), BF16),
            pltpu.VMEM((2, 8, ex * ey), BF16),
            pltpu.VMEM((2, DEEP, dof), BF16),
            pltpu.VMEM((2, DEEP, dof), BF16),
            pltpu.VMEM((4, 4, dof), BF16),
            pltpu.VMEM((4, 4, dof), BF16),
            pltpu.VMEM((ex, 2 * ey), F32),
            pltpu.VMEM((9, ex, 2 * ey), F32),
            sem((len(args),)),
            sem((SWEEPS, 2)),
            sem((SWEEPS, 2)),
            sem((SWEEPS, 2)),
            sem((SWEEPS, 2)),
            sem((2,)),
            sem((2,)),
            sem((patches,)),
            sem((patches,)),
            sem((slabs,)),
            sem((slabs,)),
            sem((slabs, patches)),
            sem((slabs, patches)),
            sem((patches,)),
            sem((patches,)),
            sem((2,)),
            sem((2,)),
            sem((2,)),
            sem((2,)),
            sem((2,)),
            sem((2,)),
            sem((4,)),
            sem((4,)),
            sem((9,)),
            sem((9,)),
            pltpu.SemaphoreType.REGULAR((max(slabs.bit_length(), 1),)),
        ],
        compiler_params=pltpu.CompilerParams(collective_id=0, has_side_effects=True),
    )(*args)
    return pl.pallas_call(
        deliver,
        out_shape=tuple(jax.ShapeDtypeStruct(x.shape, x.dtype) for x in outs),
        in_specs=[vmem] * 3,
        out_specs=(pl.BlockSpec(memory_space=pltpu.HBM),) * 3,
        scratch_shapes=[sem((3,))],
    )(*[pltpu.with_memory_space_constraint(x, pltpu.VMEM) for x in outs])


def solution(mesh):
    return jax.shard_map(
        functools.partial(shards, mesh.shape["slab"], mesh.shape["patch"]),
        mesh=mesh,
        in_specs=(
            P("slab", "patch", None),
            P("slab", "patch", None),
            P("slab", "patch"),
            P(),
            P(),
            P(),
            P(),
            P(),
            P("slab", "patch", None),
            P("slab", "patch", None),
            P("slab", "patch", None),
            P(None, "patch", None),
            P("patch", None),
        ),
        out_specs=(
            P("slab", "patch", None),
            P(None, "patch", None),
            P(None, "slab", "patch", None),
        ),
        check_vma=False,
    )
```

```python
import functools

import jax
import jax.numpy as jnp
from jax import lax
from jax.experimental import pallas as pl
from jax.experimental.pallas import tpu as pltpu
from jax.sharding import PartitionSpec as P

SWEEPS = 3
PACK = 16
EDGE = 8
SPARE = 8 * 2**20
DEEP = 16
TIP = 8
LOAD_ORDER = (7, 6, 3, 4, 5, 2, 0, 1, 9, 8, 10, 11, 12)
MESH = pl.DeviceIdType.MESH
F32 = jnp.float32
BF16 = jnp.bfloat16


def dot(a, b):
    return jnp.dot(a, b, preferred_element_type=F32)


def dot_nt(a, b):
    return lax.dot_general(a, b, (((1,), (1,)), ((), ())), preferred_element_type=F32)


def split_point(point, cols):
    if cols & (cols - 1) == 0:
        return lax.shift_right_logical(point, cols.bit_length() - 1), point & (cols - 1)
    row = lax.div(point, cols)
    return row, point - row * cols


def column(row_vector):
    n = row_vector.shape[1]
    shape = (n, n)
    eye = lax.broadcasted_iota(jnp.int32, shape, 0) == lax.broadcasted_iota(jnp.int32, shape, 1)
    return jnp.sum(jnp.where(eye, jnp.broadcast_to(row_vector, shape), 0.0), axis=1, keepdims=True)


def laplace(x):
    rows, cols = x.shape
    lane = lax.broadcasted_iota(jnp.int32, x.shape, 1)
    left = jnp.where(lane == 0, 0.0, pltpu.roll(x, 1, 1))
    right = jnp.where(lane == cols - 1, 0.0, pltpu.roll(x, cols - 1, 1))
    return 4.0 * x - (pltpu.roll(x, 1, 0) + pltpu.roll(x, rows - 1, 0) + left + right)


def join(*parts):
    return jnp.concatenate(parts, axis=0)


def blank(rows, cols):
    return jnp.zeros((rows, cols), F32)


def make_words(traction, inverse, matrix, couple_x, couple_y):
    comps, dof = traction.shape
    base0 = dot_nt(traction, inverse)
    low = base0.astype(BF16)
    one = join(dot_nt(low, couple_x), traction.astype(F32) - dot_nt(low, matrix), dot_nt(low, couple_y))
    base1 = dot_nt(one.astype(BF16), inverse)
    low = base1.astype(BF16)
    by_x, by_y = dot_nt(low, couple_x), dot_nt(low, couple_y)
    by_d = one - dot_nt(low, matrix)
    two = join(
        by_d[:comps], by_x, by_y[:comps], blank(DEEP - 5 * comps, dof),
        by_d[comps:], by_y[comps:], blank(DEEP - 4 * comps, dof),
    )
    base2 = dot_nt(two.astype(BF16), inverse)
    low = base2.astype(BF16)
    three = join(two - dot_nt(low, matrix), dot_nt(low, couple_x), dot_nt(low, couple_y))
    rest = join(base2, base1, blank(DEEP - 3 * comps, dof), base0, blank(DEEP - comps, dof))
    return three.astype(BF16), rest.astype(BF16)


def kernel(slabs, patches, args, *refs):
    hbm, refs = refs[:args], refs[args:]
    (fluid_ref, net_ref, wall_ref), refs = refs[:3], refs[3:]
    (state_ref, rhs_ref, scale_ref, matrices, traction_ref, slots, count_ref, nets) = refs[:8]
    refs = refs[8:]
    cx_ref, cy_ref, inverse_ref, matrix_ref = (matrices.at[n] for n in range(4))
    elem_ref, point_ref = slots.at[0], slots.at[1]
    (vb, halo_x, halo_y, halo_d, points, pulls, pull_out, picks_out, picks_in) = refs[:9]
    (onehot_elem, onehot_row, onehot_col, rest_buf, gain_buf, base_buf) = refs[9:15]
    (near_out, near_in, far_out, far_in, side_out, side_in, tip_out, tip_in) = refs[15:23]
    (load_sem, sx, rx, sy, ry, sd, rd, point_sem, rp2, pull_sem, rq, pick_sem) = refs[23:35]
    (s_near, r_near, s_far, r_far, s_side, r_side, s_tip, r_tip, near_sem) = refs[35:]
    comps = nets.shape[0] - 1
    disp_ref, stiff_ref = nets.at[pl.ds(0, comps)], nets.at[comps]
    homes = (
        (state_ref, 0), (rhs_ref, 1), (scale_ref, 2), (matrix_ref, 3), (cx_ref, 3), (cy_ref, 3), (inverse_ref, 3),
        (traction_ref, 4), (elem_ref, 5), (point_ref, 5), (count_ref, 6), (disp_ref, 7), (stiff_ref, 7),
    )

    loads_in = [pltpu.make_async_copy(hbm[n], homes[n][0], load_sem.at[homes[n][1]]) for n in range(args)]
    for n in LOAD_ORDER:
        loads_in[n].start()
    groups = (state_ref, rhs_ref, scale_ref, matrices, traction_ref, slots, count_ref, nets)

    def ready(*names):
        for n in names:
            pltpu.make_async_copy(groups[n], groups[n], load_sem.at[n]).wait()

    s = lax.axis_index("slab")
    p = lax.axis_index("patch")
    ex, ey, dof = state_ref.shape
    rows, cols = stiff_ref.shape
    cap = elem_ref.shape[2] // patches
    wide_lanes = ex * ey

    def slab_peer(j):
        return lax.rem(s + j, slabs)

    def patch_peer(j):
        return lax.rem(p + j, patches)

    def slab_sides(reach, semaphore):
        @pl.when(s >= reach)
        def _():
            pl.semaphore_signal(semaphore, inc=1, device_id=(s - reach, p), device_id_type=MESH)

        @pl.when(s + reach < slabs)
        def _():
            pl.semaphore_signal(semaphore, inc=1, device_id=(s + reach, p), device_id_type=MESH)

    def slab_count(reach):
        return jnp.where(s >= reach, 1, 0) + jnp.where(s + reach < slabs, 1, 0)

    reaches = []
    while 2 ** (len(reaches) + 1) < slabs - 1:
        reaches.append(2 ** (len(reaches) + 1))

    def near_signal(n):
        slab_sides(reaches[n], near_sem.at[n])

    def near_wait(n):
        pl.semaphore_wait(near_sem.at[n], slab_count(reaches[n]))

    has_prev_s, has_next_s = s > 0, s < slabs - 1
    has_prev_p, has_next_p = p > 0, p < patches - 1
    has_far_prev, has_far_next = s > 1, s < slabs - 2

    barrier = pltpu.get_barrier_semaphore()
    for j in range(1, patches):
        pl.semaphore_signal(barrier, inc=1, device_id=(s, patch_peer(j)), device_id_type=MESH)
    for reach in (1, 2):

        @pl.when(s >= reach)
        def _():
            for j in range(patches):
                pl.semaphore_signal(barrier, inc=1, device_id=(s - reach, patch_peer(j)), device_id_type=MESH)

        @pl.when(s + reach < slabs)
        def _():
            for j in range(patches):
                pl.semaphore_signal(barrier, inc=1, device_id=(s + reach, patch_peer(j)), device_id_type=MESH)

    awaited = patches - 1 + patches * (slab_count(1) + slab_count(2))

    def remote(src, dst, send, recv, target):
        return pltpu.make_async_remote_copy(
            src_ref=src, dst_ref=dst, send_sem=send, recv_sem=recv, device_id=target, device_id_type=MESH
        )

    def slab_at(step):
        return jnp.clip(s + step, 0, slabs - 1)

    def patch_at(step):
        return jnp.clip(p + step, 0, patches - 1)

    def x_up(k):
        return remote(vb.at[k, ex - 1], halo_x.at[k, 0], sx.at[0], rx.at[k % 2, 0], (slab_at(1), p))

    def x_down(k):
        return remote(vb.at[k, 0], halo_x.at[k, 1], sx.at[1], rx.at[k % 2, 1], (slab_at(-1), p))

    def y_up(k):
        return remote(
            vb.at[k, :, pl.ds(ey - PACK, PACK)], halo_y.at[k, 0], sy.at[0], ry.at[k % 2, 0], (s, patch_at(1))
        )

    def y_down(k):
        return remote(vb.at[k, :, pl.ds(0, PACK)], halo_y.at[k, 1], sy.at[1], ry.at[k % 2, 1], (s, patch_at(-1)))

    def d_up():
        return remote(disp_ref.at[:, pl.ds(rows - EDGE, EDGE)], halo_d.at[0], sd.at[0], rd.at[0], (s, patch_at(1)))

    def d_down():
        return remote(disp_ref.at[:, pl.ds(0, EDGE)], halo_d.at[1], sd.at[1], rd.at[1], (s, patch_at(-1)))

    def near_copy(n):
        return remote(near_out, near_in.at[n], s_near.at[n], r_near.at[n], (slab_at(1 - 2 * n), p))

    def far_copy(n):
        return remote(far_out, far_in.at[n], s_far.at[n], r_far.at[n], (slab_at(2 - 4 * n), p))

    def side_copy(n):
        return remote(side_out.at[n], side_in.at[n], s_side.at[n], r_side.at[n], (s, patch_at(1 - 2 * n)))

    def tip_copy(n, m):
        q = 2 * n + m
        return remote(tip_out.at[q], tip_in.at[q], s_tip.at[q], r_tip.at[q], (slab_at(1 - 2 * n), patch_at(1 - 2 * m)))

    to_s, from_s = (has_next_s, has_prev_s), (has_prev_s, has_next_s)
    to_p, from_p = (has_next_p, has_prev_p), (has_prev_p, has_next_p)
    to_far, from_far = (has_far_next, has_far_prev), (has_far_prev, has_far_next)
    corners = [(n, m) for n in range(2) for m in range(2)]
    def point_first(j):
        peer = patch_peer(j)
        src = point_ref.at[0, :, pl.ds(pl.multiple_of(peer * cap, cap), cap)]
        return remote(src, points.at[s, p], point_sem.at[0], point_sem.at[1], (s, peer))

    def point_second(j):
        return remote(points.at[s], points.at[s], point_sem.at[2], rp2.at[s], (slab_peer(j), p))

    def pull_copy(j, i):
        to = (slab_peer(j), patch_peer(i))
        here = pl.ds(pl.multiple_of(p * cap, cap), cap)
        return remote(pull_out.at[to[1]], pulls.at[s, :, here], pull_sem.at[0 if j else 1], rq.at[s], to)

    def pick_copy(j):
        peer = patch_peer(j)
        return remote(picks_out.at[peer], picks_in.at[p], pick_sem.at[0], pick_sem.at[1], (s, peer))

    def settle(ref, semaphore):
        pltpu.make_async_copy(ref, ref, semaphore).wait()

    def halo_sends(k, act):
        pl.when(has_next_s)(lambda: act(x_up(k)))
        pl.when(has_prev_s)(lambda: act(x_down(k)))
        pl.when(has_next_p)(lambda: act(y_up(k)))
        pl.when(has_prev_p)(lambda: act(y_down(k)))

    def send_halos(k):
        if k > 0:
            halo_sends(k - 1, lambda copy: copy.wait_send())
        halo_sends(k, lambda copy: copy.start())

    def build_points(slab):
        for k in range(patches):
            row, col = split_point(points[slab, k], cols)
            span = pl.ds(k * cap, cap)
            onehot_row[slab, :, span] = jnp.where(
                lax.broadcasted_iota(jnp.int32, (rows, cap), 0) == row, 1.0, 0.0
            ).astype(BF16)
            onehot_col[slab, :, span] = jnp.where(
                lax.broadcasted_iota(jnp.int32, (cols, cap), 0) == col, 1.0, 0.0
            ).astype(BF16)

    def lives(k):
        lane = lax.broadcasted_iota(jnp.int32, (1, cap), 1)
        return lane < count_ref[0, :, k : k + 1]

    def shell():
        pl.when(has_prev_p)(lambda: d_up().wait_recv())
        pl.when(has_next_p)(lambda: d_down().wait_recv())
        total = rows + 2 * EDGE
        line = lax.broadcasted_iota(jnp.int32, (total, cols), 0)
        first = jnp.where(has_prev_p, 0, EDGE)
        last = jnp.where(has_next_p, total, EDGE + rows)
        valid = (line >= first) & (line < last)
        gain = 1.0 / (36.0 * stiff_ref[...])
        gain_buf[...] = gain
        for c in range(comps):
            field = jnp.concatenate([halo_d[0, c], disp_ref[c], halo_d[1, c]], axis=0)
            field = jnp.where(valid, field, 0.0)
            bend = jnp.where(valid, laplace(field), 0.0)
            full = (laplace(bend) + 4.0 * bend)[EDGE : EDGE + rows]
            rest_buf[c] = disp_ref[c] - stiff_ref[...] * full * gain

    with jax.named_scope("words"):
        ready(4, 3)
        words, rest = make_words(
            traction_ref[...], inverse_ref[...], matrix_ref[...], cx_ref[...], cy_ref[...]
        )
    ready(2)
    flat = 1.0 / scale_ref[...]
    w_own = jnp.concatenate([flat, blank(ex, wide_lanes - ey)], axis=1)
    ready(0)
    rounded0 = state_ref[...].astype(BF16)
    vb[0] = rounded0
    ready(1)
    wet = rhs_ref[...].astype(BF16)
    lane = lax.broadcasted_iota(jnp.int32, (1, wide_lanes), 1)
    low_half = lane < ey
    tail_half = lane < ey + ey // 2
    w_lines = jnp.concatenate([w_own] + [blank(ex, wide_lanes)] * (dof // wide_lanes - 1), axis=1)
    with jax.named_scope("project"):
        own_v = dot_nt(words, rounded0.reshape(wide_lanes, dof))
        own_r = dot_nt(rest, wet.reshape(wide_lanes, dof))
        packed = jnp.where(low_half, w_own[0:1], pltpu.roll(w_own[1:2], ey, 1))
        spare = join(
            blank(2 * DEEP - comps - 1, wide_lanes), own_r[2 * DEEP : 2 * DEEP + comps], packed
        )
        near_out[...] = join(
            own_v[0:DEEP], own_v[2 * DEEP : 4 * DEEP] + spare, own_v[4 * DEEP : 5 * DEEP], own_r[0:DEEP]
        ).astype(BF16)
        far_out[...] = own_v[2 * DEEP : 2 * DEEP + 8].astype(BF16)

        def state_at(i, c):
            return state_ref[i, c : c + 1]

        def rhs_at(i, c):
            return rhs_ref[i, c : c + 1]

        for m in range(2):
            edge = [ey - 1 - j if m == 0 else j for j in range(SWEEPS)]
            lines = [state_at(i, c) for i in range(ex) for c in edge]
            lines += [rhs_at(i, c) for i in range(ex) for c in edge[: SWEEPS - 1]]
            side_out[m] = join(*lines, w_lines, blank(DEEP - ex - len(lines), dof)).astype(BF16)
            for n in range(2):
                order = [ex - 1, ex - 2] if n == 0 else [0, 1]
                tip_out[2 * n + m] = join(
                    state_at(order[0], edge[0]),
                    state_at(order[0], edge[1]),
                    state_at(order[1], edge[0]),
                    rhs_at(order[0], edge[0]),
                    w_lines[order[0] : order[0] + 1],
                    blank(TIP - 5, dof),
                ).astype(BF16)

    with jax.named_scope("w_barrier"):
        pl.semaphore_wait(barrier, awaited)
    for n, m in corners:
        pl.when(jnp.logical_and(to_s[n], to_p[m]))(lambda: tip_copy(n, m).start())
    for n in range(2):
        pl.when(to_s[n])(lambda: near_copy(n).start())
    for m in range(2):
        pl.when(to_p[m])(lambda: side_copy(m).start())
    for n in range(2):
        pl.when(to_far[n])(lambda: far_copy(n).start())
    if reaches:
        near_signal(0)
    ready(5)
    for j in range(1, patches):
        point_first(j).start()
    ready(7)
    pl.when(has_next_p)(lambda: d_up().start())
    pl.when(has_prev_p)(lambda: d_down().start())
    ready(6)
    for owner in range(patches):

        @pl.when(p == owner)
        def _():
            points[s, owner] = point_ref[0, :, owner * cap : (owner + 1) * cap]

    for owner in range(patches):
        elem = elem_ref[0, :, owner * cap : (owner + 1) * cap]
        hit = (lax.broadcasted_iota(jnp.int32, (wide_lanes, cap), 0) == elem) & lives(owner)
        onehot_elem[owner] = jnp.where(hit, 1.0, 0.0).astype(BF16)
    if reaches:
        with jax.named_scope("w_reach"):
            near_wait(0)
        if len(reaches) > 1:
            near_signal(1)
    send_halos(0)
    scales = [column(scale_ref[i : i + 1, :]) for i in range(ex)]
    inverses = [1.0 / x for x in scales]

    def prelude(k):
        own = dot(vb[k].reshape(ex * ey, dof), matrix_ref[...]).reshape(ex, ey, dof)
        for i in range(ex):
            base_buf[i] = rhs_ref[i] - scales[i] * own[i]

    with jax.named_scope("shell"):
        shell()
    with jax.named_scope("prelude"):
        prelude(0)

    def halves(x):
        return jnp.where(low_half, x, 0.0), jnp.where(low_half, pltpu.roll(x, ey, 1), 0.0)

    span_rows = list(range(-ex, 2 * ex))
    stack_rows = 2 * DEEP + 4 * TIP
    spots_v, spots_r = [], []
    for m in range(2):
        def spot(r, j):
            return (r + ex) * wide_lanes + (wide_lanes - j if m == 0 else ey + j - 1)

        for i in range(ex):
            spots_v += [(m * DEEP + i * SWEEPS + j - 1, spot(i, j)) for j in range(1, SWEEPS + 1)]
            first = m * DEEP + ex * SWEEPS + i * (SWEEPS - 1) - 1
            spots_r += [(first + j, spot(i, j)) for j in range(1, SWEEPS)]
        for n in range(2):
            r1, r2 = (-1, -2) if n == 0 else (ex, ex + 1)
            first = 2 * DEEP + TIP * (2 * n + m)
            spots_v += [(first, spot(r1, 1)), (first + 1, spot(r1, 2)), (first + 2, spot(r2, 1))]
            spots_r += [(first + 3, spot(r1, 1))]

    def placing(spots):
        line = lax.broadcasted_iota(jnp.int32, (stack_rows, 1), 0)
        target = jnp.full((stack_rows, 1), -1, jnp.int32)
        for n, at in spots:
            target = jnp.where(line == n, at, target)
        lanes = lax.broadcasted_iota(jnp.int32, (stack_rows, len(span_rows) * wide_lanes), 1)
        return jnp.where(lanes == target, 1.0, 0.0).astype(BF16)

    place_v, place_r = placing(spots_v), placing(spots_r)
    with jax.named_scope("w_side"):
        for m in range(2):
            pl.when(from_p[m])(lambda: side_copy(m).wait_recv())
        for n, m in corners:
            pl.when(jnp.logical_and(from_s[n], from_p[m]))(lambda: tip_copy(n, m).wait_recv())
    with jax.named_scope("place"):
        sides = [jnp.where(from_p[m], side_in[m].astype(F32), 0.0) for m in range(2)]
        tips = [
            jnp.where(jnp.logical_and(from_s[n], from_p[m]), tip_in[2 * n + m].astype(F32), 0.0) for n, m in corners
        ]
        stack = join(*sides, *tips).astype(BF16)
        placed_v = dot(dot_nt(words, stack).astype(BF16), place_v)
        placed_r = dot(dot_nt(rest, stack).astype(BF16), place_r)

        def piece(x, r):
            return x[:, (r + ex) * wide_lanes : (r + ex + 1) * wide_lanes]

        def framed(middle, before, after):
            before, after = pltpu.roll(before, ey, 1), pltpu.roll(after, ey, 1)
            return jnp.where(low_half, middle, jnp.where(tail_half, after, before))

        w_at = ex * (2 * SWEEPS - 1)
        w_rows = {}
        for i in range(ex):
            ends = [sides[m][w_at + i : w_at + i + 1, :wide_lanes] for m in range(2)]
            w_rows[i] = framed(w_own[i : i + 1], *ends)
        w_tips = [[tips[2 * n + m][4:5, :wide_lanes] for m in range(2)] for n in range(2)]

    with jax.named_scope("w_near"):
        for n in range(2):
            pl.when(from_far[n])(lambda: far_copy(n).wait_recv())
            pl.when(from_s[n])(lambda: near_copy(n).wait_recv())

    with jax.named_scope("stencil"):
        by_d, by_x, by_y, by_r2, by_r1, by_r0 = {}, {}, {}, {}, {}, {}
        for i, (v_half, r_half) in enumerate(zip(halves(own_v), halves(own_r))):
            full, side = v_half + piece(placed_v, i), r_half + piece(placed_r, i)
            by_d[i], by_x[i], by_y[i] = (full[k * 2 * DEEP : (k + 1) * 2 * DEEP] for k in range(3))
            by_r2[i], by_r1[i], by_r0[i] = (
                side[: 2 * DEEP], side[2 * DEEP : 2 * DEEP + 3 * comps], side[3 * DEEP : 3 * DEEP + comps]
            )
        for n in range(2):
            got = jnp.where(from_s[n], near_in[n].astype(F32), 0.0)
            for i, half in enumerate(halves(got)):
                r = i - ex if n == 0 else i + ex
                edge_v, edge_r = piece(placed_v, r), piece(placed_r, r)
                by_d[r] = half[0:DEEP] + edge_v[0:DEEP]
                by_x[r] = half[DEEP : 3 * DEEP] + edge_v[2 * DEEP : 4 * DEEP]
                by_y[r] = half[3 * DEEP : 4 * DEEP] + edge_v[4 * DEEP : 5 * DEEP]
                by_r2[r] = half[4 * DEEP : 5 * DEEP] + edge_r[0:DEEP]
                by_r1[r] = half[3 * DEEP - comps - 1 : 3 * DEEP - 1]
                w_rows[r] = half[3 * DEEP - 1 : 3 * DEEP]
                if r in (-1, ex):
                    w_rows[r] = framed(w_rows[r], *w_tips[n])
            beyond = halves(jnp.where(from_far[n], far_in[n].astype(F32), 0.0))[1 - n]
            by_x[-ex - 1 if n == 0 else 2 * ex] = join(beyond, blank(DEEP - 8, wide_lanes))

        def turn(x):
            return pltpu.roll(x, 1, 1) + pltpu.roll(x, wide_lanes - 1, 1)

        one = {}
        for r in span_rows:
            n = 2 * DEEP if 0 <= r < ex else DEEP
            one[r] = by_d[r] + w_rows[r] * (by_x[r - 1][:n] + by_x[r + 1][:n] + turn(by_y[r]) + by_r2[r])
        two = {}
        for r in range(-1, ex + 1):
            if 0 <= r < ex:
                d_part = join(one[r][:comps], one[r][DEEP : DEEP + 2 * comps])
                y_part = join(one[r][4 * comps : 5 * comps], one[r][DEEP + 2 * comps : DEEP + 4 * comps])
                n = 3 * comps
            else:
                d_part, y_part = one[r][:comps], one[r][4 * comps : 5 * comps]
                n = comps
            x_part = one[r - 1][comps : comps + n] + one[r + 1][comps : comps + n]
            two[r] = d_part + w_rows[r] * (x_part + turn(y_part) + by_r1[r])
        drawn = []
        for r in range(ex):
            x_part = two[r - 1][:comps] + two[r + 1][:comps]
            drawn.append(
                two[r][comps : 2 * comps]
                + w_rows[r] * (x_part + turn(two[r][2 * comps : 3 * comps]) + by_r0[r])
            )
        traction = jnp.where(low_half, drawn[0], pltpu.roll(drawn[1], ey, 1)).astype(BF16)
        for owner in range(patches):
            pull_out[owner] = dot(traction, onehot_elem[owner]).astype(BF16)
    for n in range(1, len(reaches)):
        with jax.named_scope("w_reach"):
            near_wait(n)
        if n + 1 < len(reaches):
            near_signal(n + 1)
    with jax.named_scope("w_pt1"):
        settle(points.at[s, pl.ds(0, patches - 1)], point_sem.at[1])
    for j in range(1, slabs):
        point_second(j).start()
    with jax.named_scope("s_pull"):
        for j in sorted(range(slabs), key=lambda j: -min(j, slabs - j)):
            for i in range(patches):
                if (j, i) != (0, 0):
                    pull_copy(j, i).start()
    for owner in range(patches):

        @pl.when(p == owner)
        def _():
            pulls[s, :, owner * cap : (owner + 1) * cap] = pull_out[owner]


    def sweep(k, v):
        rounded = vb[k]
        wide = rounded.astype(F32)
        with jax.named_scope("w_halo"):
            pl.when(has_prev_p)(lambda: y_up(k).wait_recv())
            pl.when(has_next_p)(lambda: y_down(k).wait_recv())
            pl.when(has_prev_s)(lambda: x_up(k).wait_recv())
            pl.when(has_next_s)(lambda: x_down(k).wait_recv())
        line = lax.broadcasted_iota(jnp.int32, (ey, dof), 0)
        along_y = []
        for i in range(ex):
            before = halo_y[k, 0, i].astype(F32)[PACK - 1 : PACK]
            after = halo_y[k, 1, i].astype(F32)[0:1]
            before = jnp.where(has_prev_p, before, 0.0)
            after = jnp.where(has_next_p, after, 0.0)
            prev = jnp.where(line == 0, jnp.broadcast_to(before, (ey, dof)), pltpu.roll(wide[i], 1, 0))
            following = jnp.where(line == ey - 1, jnp.broadcast_to(after, (ey, dof)), pltpu.roll(wide[i], ey - 1, 0))
            along_y.append((prev + following).astype(BF16))
        side_y = dot(jnp.concatenate(along_y, axis=0), cy_ref[...])
        low = jnp.where(has_prev_s, halo_x[k, 0].astype(F32), 0.0)
        high = jnp.where(has_next_s, halo_x[k, 1].astype(F32), 0.0)
        along_x = []
        for i in range(ex):
            below = low if i == 0 else wide[i - 1]
            above = high if i == ex - 1 else wide[i + 1]
            along_x.append((below + above).astype(BF16))
        side_x = dot(jnp.concatenate(along_x, axis=0), cx_ref[...])
        side = (side_x + side_y).reshape(ex, ey, dof)
        residue = jnp.concatenate([(base_buf[i] + side[i]).astype(BF16) for i in range(ex)], axis=0)
        update = dot(residue, inverse_ref[...]).reshape(ex, ey, dof)
        return [v[i] + update[i] * inverses[i] for i in range(ex)]

    def keep(v, k):
        for i in range(ex):
            fluid_ref[i] = v[i]
            if k < SWEEPS:
                vb[k, i] = v[i].astype(BF16)

    with jax.named_scope("sweep0"):
        keep(sweep(0, state_ref), 1)
        send_halos(1)
        prelude(1)

    def scatter(slab, acc):
        hot = onehot_row[slab]
        value = pulls[slab]
        scaled = jnp.concatenate([hot * value[c : c + 1] for c in range(comps)], axis=0)
        return acc + dot_nt(scaled, onehot_col[slab])

    inner = jnp.minimum(s, slabs - 1 - s)

    def nearest(t):
        step = lax.div(t + 1, 2)
        alternate = jnp.where(lax.rem(t, 2) == 1, s + step, s - step)
        return jnp.where(t <= 2 * inner, alternate, jnp.where(s < slabs - 1 - s, t, slabs - 1 - t))

    def prepared(t, carry):
        slab = nearest(t)
        with jax.named_scope("w_point"):
            settle(points.at[slab], rp2.at[slab])
        build_points(slab)
        return carry

    def gathered(t, acc):
        slab = nearest(t)
        with jax.named_scope("w_pull"):
            settle(pulls.at[slab], rq.at[slab])
        return scatter(slab, acc)

    half = (slabs + 1) // 2
    build_points(s)
    with jax.named_scope("build1"):
        lax.fori_loop(1, half, prepared, 0)
    with jax.named_scope("w_own"):
        settle(pulls.at[s, :, pl.ds(0, (patches - 1) * cap)], rq.at[s])
    acc = scatter(s, jnp.zeros((comps * rows, cols), F32))
    with jax.named_scope("gather1"):
        acc = lax.fori_loop(1, half, gathered, acc)
    with jax.named_scope("build2"):
        lax.fori_loop(half, slabs, prepared, 0)
    with jax.named_scope("sweep1"):
        keep(sweep(1, fluid_ref), 2)
        send_halos(2)
    with jax.named_scope("gather2"):
        acc = lax.fori_loop(half, slabs, gathered, acc)
    loads = acc.reshape(comps, rows, cols)
    fresh = [rest_buf[c] + loads[c] * gain_buf[...] for c in range(comps)]
    narrow = jnp.concatenate([x.astype(BF16) for x in fresh], axis=0)
    for k in range(patches):
        span = pl.ds(k * cap, cap)
        spread = dot(narrow, onehot_col[s, :, span]).reshape(comps, rows, cap)
        hot = onehot_row[s, :, span].astype(F32)
        for c in range(comps):
            picks_out[k, c : c + 1] = jnp.sum(spread[c] * hot, axis=0, keepdims=True)
    with jax.named_scope("s_pick"):
        for j in range(1, patches):
            pick_copy(j).start()
    picks_in[p] = picks_out[p]
    for c in range(comps):
        net_ref[c] = fresh[c]
    with jax.named_scope("sweep2"):
        prelude(2)
        keep(sweep(2, fluid_ref), SWEEPS)
    with jax.named_scope("w_pick"):
        settle(picks_in.at[pl.ds(0, patches - 1)], pick_sem.at[1])
    for k in range(patches):
        live = lives(k)
        for c in range(comps):
            wall_ref[c, 0, :, k * cap : (k + 1) * cap] = jnp.where(live, picks_in[k, c : c + 1], 0.0)

    with jax.named_scope("drain"):
        halo_sends(SWEEPS - 1, lambda copy: copy.wait_send())
        pl.when(has_next_p)(lambda: d_up().wait_send())
        pl.when(has_prev_p)(lambda: d_down().wait_send())
        for n in range(2):
            pl.when(to_s[n])(lambda: near_copy(n).wait_send())
            pl.when(to_far[n])(lambda: far_copy(n).wait_send())
            pl.when(to_p[n])(lambda: side_copy(n).wait_send())
        for n, m in corners:
            pl.when(jnp.logical_and(to_s[n], to_p[m]))(lambda: tip_copy(n, m).wait_send())
        settle(points.at[s, pl.ds(0, patches - 1)], point_sem.at[0])
        settle(points.at[pl.ds(0, slabs - 1)], point_sem.at[2])
        settle(pulls.at[pl.ds(0, slabs - 1)], pull_sem.at[0])
        settle(pulls.at[s, :, pl.ds(0, (patches - 1) * cap)], pull_sem.at[1])
        settle(picks_in.at[pl.ds(0, patches - 1)], pick_sem.at[0])


def deliver(*refs):
    copies = [pltpu.make_async_copy(refs[n], refs[n + 3], refs[6].at[n]) for n in range(3)]
    for copy in copies:
        copy.start()
    for copy in copies:
        copy.wait()


def shards(slabs, patches, *args):
    state, disp, elem = args[0], args[11], args[8]
    ex, ey, dof = state.shape
    comps, rows, cols = disp.shape
    cap = elem.shape[2] // patches
    sem = pltpu.SemaphoreType.DMA
    vmem = pl.BlockSpec(memory_space=pltpu.VMEM)
    hot_bytes = slabs * patches * cap * (rows + cols) * 2
    outs = pl.pallas_call(
        functools.partial(kernel, slabs, patches, len(args)),
        out_shape=(
            pltpu.VMEM(state.shape, F32),
            pltpu.VMEM(disp.shape, F32),
            pltpu.VMEM((comps, 1, 1, elem.shape[2]), F32),
        ),
        in_specs=[pl.BlockSpec(memory_space=pltpu.HBM)] * len(args),
        out_specs=(vmem, vmem, vmem),
        scratch_shapes=[pltpu.VMEM(x.shape, x.dtype) for x in args[:3]]
        + [
            pltpu.VMEM((4,) + args[3].shape, BF16),
            pltpu.VMEM(args[7].shape, BF16),
            pltpu.VMEM((2,) + elem.shape, jnp.int32),
            pltpu.VMEM(args[10].shape, jnp.int32),
            pltpu.VMEM((comps + 1, rows, cols), F32),
            pltpu.VMEM((SWEEPS, ex, ey, dof), BF16),
            pltpu.VMEM((SWEEPS, 2, ey, dof), BF16),
            pltpu.VMEM((SWEEPS, 2, ex, PACK, dof), BF16),
            pltpu.VMEM((2, comps, EDGE, cols), F32),
            pltpu.VMEM((slabs, patches, 1, cap), jnp.int32),
            pltpu.VMEM((slabs, comps, patches * cap), BF16),
            pltpu.VMEM((patches, comps, cap), BF16),
            pltpu.VMEM((patches, comps, cap), F32),
            pltpu.VMEM((patches, comps, cap), F32),
            pltpu.VMEM((patches, ex * ey, cap), BF16),
            pltpu.VMEM((slabs, rows, patches * cap), BF16),
            pltpu.VMEM((slabs, cols, patches * cap), BF16),
            pltpu.VMEM((comps, rows, cols), F32),
            pltpu.VMEM((rows, cols), F32),
            pltpu.VMEM(state.shape, F32),
            pltpu.VMEM((5 * DEEP, ex * ey), BF16),
            pltpu.VMEM((2, 5 * DEEP, ex * ey), BF16),
            pltpu.VMEM((8, ex * ey), BF16),
            pltpu.VMEM((2, 8, ex * ey), BF16),
            pltpu.VMEM((2, DEEP, dof), BF16),
            pltpu.VMEM((2, DEEP, dof), BF16),
            pltpu.VMEM((4, TIP, dof), BF16),
            pltpu.VMEM((4, TIP, dof), BF16),
            sem((8,)),
            sem((2,)),
            sem((2, 2)),
            sem((2,)),
            sem((2, 2)),
            sem((2,)),
            sem((2,)),
            sem((3,)),
            sem((slabs,)),
            sem((2,)),
            sem((slabs,)),
            sem((2,)),
            sem((2,)),
            sem((2,)),
            sem((2,)),
            sem((2,)),
            sem((2,)),
            sem((2,)),
            sem((4,)),
            sem((4,)),
            pltpu.SemaphoreType.REGULAR((max(slabs.bit_length() - 2, 1),)),
        ],
        compiler_params=pltpu.CompilerParams(collective_id=0, has_side_effects=True),
    )(*args)
    return pl.pallas_call(
        deliver,
        out_shape=tuple(jax.ShapeDtypeStruct(x.shape, x.dtype) for x in outs),
        in_specs=[vmem] * 3,
        out_specs=(pl.BlockSpec(memory_space=pltpu.HBM),) * 3,
        scratch_shapes=[sem((3,))],
    )(*[pltpu.with_memory_space_constraint(x, pltpu.VMEM) for x in outs])


def solution(mesh):
    return jax.shard_map(
        functools.partial(shards, mesh.shape["slab"], mesh.shape["patch"]),
        mesh=mesh,
        in_specs=(
            P("slab", "patch", None),
            P("slab", "patch", None),
            P("slab", "patch"),
            P(),
            P(),
            P(),
            P(),
            P(),
            P("slab", "patch", None),
            P("slab", "patch", None),
            P("slab", "patch", None),
            P(None, "patch", None),
            P("patch", None),
        ),
        out_specs=(
            P("slab", "patch", None),
            P(None, "patch", None),
            P(None, "slab", "patch", None),
        ),
        check_vma=False,
    )
```

```python
import functools

import jax
import jax.numpy as jnp
from jax import lax
from jax.experimental import pallas as pl
from jax.experimental.pallas import tpu as pltpu
from jax.sharding import PartitionSpec as P

SWEEPS = 3
PACK = 16
EDGE = 8
SPARE = 8 * 2**20
DEEP = 16
TIP = 8
LOAD_ORDER = (7, 6, 3, 4, 5, 2, 0, 1, 9, 8, 10, 11, 12)
MESH = pl.DeviceIdType.MESH
F32 = jnp.float32
BF16 = jnp.bfloat16


def dot(a, b):
    return jnp.dot(a, b, preferred_element_type=F32)


def dot_nt(a, b):
    return lax.dot_general(a, b, (((1,), (1,)), ((), ())), preferred_element_type=F32)


def split_point(point, cols):
    if cols & (cols - 1) == 0:
        return lax.shift_right_logical(point, cols.bit_length() - 1), point & (cols - 1)
    row = lax.div(point, cols)
    return row, point - row * cols


def column(row_vector):
    n = row_vector.shape[1]
    shape = (n, n)
    eye = lax.broadcasted_iota(jnp.int32, shape, 0) == lax.broadcasted_iota(jnp.int32, shape, 1)
    return jnp.sum(jnp.where(eye, jnp.broadcast_to(row_vector, shape), 0.0), axis=1, keepdims=True)


def laplace(x):
    rows, cols = x.shape
    lane = lax.broadcasted_iota(jnp.int32, x.shape, 1)
    left = jnp.where(lane == 0, 0.0, pltpu.roll(x, 1, 1))
    right = jnp.where(lane == cols - 1, 0.0, pltpu.roll(x, cols - 1, 1))
    return 4.0 * x - (pltpu.roll(x, 1, 0) + pltpu.roll(x, rows - 1, 0) + left + right)


def join(*parts):
    return jnp.concatenate(parts, axis=0)


def blank(rows, cols):
    return jnp.zeros((rows, cols), F32)


def make_words(traction, inverse, matrix, couple_x, couple_y):
    comps, dof = traction.shape
    base0 = dot_nt(traction, inverse)
    low = base0.astype(BF16)
    one = join(dot_nt(low, couple_x), traction.astype(F32) - dot_nt(low, matrix), dot_nt(low, couple_y))
    base1 = dot_nt(one.astype(BF16), inverse)
    low = base1.astype(BF16)
    by_x, by_y = dot_nt(low, couple_x), dot_nt(low, couple_y)
    by_d = one - dot_nt(low, matrix)
    two = join(
        by_d[:comps], by_x, by_y[:comps], blank(DEEP - 5 * comps, dof),
        by_d[comps:], by_y[comps:], blank(DEEP - 4 * comps, dof),
    )
    base2 = dot_nt(two.astype(BF16), inverse)
    low = base2.astype(BF16)
    three = join(two - dot_nt(low, matrix), dot_nt(low, couple_x), dot_nt(low, couple_y))
    rest = join(base2, base1, blank(DEEP - 3 * comps, dof), base0, blank(DEEP - comps, dof))
    return three.astype(BF16), rest.astype(BF16)


def kernel(slabs, patches, args, *refs):
    hbm, refs = refs[:args], refs[args:]
    (fluid_ref, net_ref, wall_ref), refs = refs[:3], refs[3:]
    (state_ref, rhs_ref, scale_ref, matrices, traction_ref, slots, count_ref, nets) = refs[:8]
    refs = refs[8:]
    cx_ref, cy_ref, inverse_ref, matrix_ref = (matrices.at[n] for n in range(4))
    elem_ref, point_ref = slots.at[0], slots.at[1]
    (vb, halo_x, halo_y, halo_d, points, pulls, pull_out, picks_out, picks_in) = refs[:9]
    (onehot_elem, onehot_row, onehot_col, rest_buf, gain_buf, base_buf) = refs[9:15]
    (near_out, near_in, far_out, far_in, side_out, tip_out, rim) = refs[15:22]
    (load_sem, rx, ry, sd, rd, point_sem, rp2, pull_sem, rq, pick_sem) = refs[22:32]
    (s_near, r_near, s_far, r_far, s_side, r_side, s_tip, r_tip, near_sem) = refs[32:]
    sx, sy = s_near, s_side
    comps = nets.shape[0] - 1
    disp_ref, stiff_ref = nets.at[pl.ds(0, comps)], nets.at[comps]
    homes = (
        (state_ref, 0), (rhs_ref, 1), (scale_ref, 2), (matrix_ref, 3), (cx_ref, 3), (cy_ref, 3), (inverse_ref, 3),
        (traction_ref, 4), (elem_ref, 5), (point_ref, 5), (count_ref, 6), (disp_ref, 7), (stiff_ref, 7),
    )

    loads_in = [pltpu.make_async_copy(hbm[n], homes[n][0], load_sem.at[homes[n][1]]) for n in range(args)]
    for n in LOAD_ORDER:
        loads_in[n].start()
    groups = (state_ref, rhs_ref, scale_ref, matrices, traction_ref, slots, count_ref, nets)

    def ready(*names):
        for n in names:
            pltpu.make_async_copy(groups[n], groups[n], load_sem.at[n]).wait()

    s = lax.axis_index("slab")
    p = lax.axis_index("patch")
    ex, ey, dof = state_ref.shape
    rows, cols = stiff_ref.shape
    cap = elem_ref.shape[2] // patches
    wide_lanes = ex * ey

    def slab_peer(j):
        return lax.rem(s + j, slabs)

    def patch_peer(j):
        return lax.rem(p + j, patches)

    def slab_sides(reach, semaphore):
        @pl.when(s >= reach)
        def _():
            pl.semaphore_signal(semaphore, inc=1, device_id=(s - reach, p), device_id_type=MESH)

        @pl.when(s + reach < slabs)
        def _():
            pl.semaphore_signal(semaphore, inc=1, device_id=(s + reach, p), device_id_type=MESH)

    def slab_count(reach):
        return jnp.where(s >= reach, 1, 0) + jnp.where(s + reach < slabs, 1, 0)

    reaches = []
    while 2 ** (len(reaches) + 1) < slabs - 1:
        reaches.append(2 ** (len(reaches) + 1))

    def near_signal(n):
        slab_sides(reaches[n], near_sem.at[n])

    def near_wait(n):
        pl.semaphore_wait(near_sem.at[n], slab_count(reaches[n]))

    has_prev_s, has_next_s = s > 0, s < slabs - 1
    has_prev_p, has_next_p = p > 0, p < patches - 1
    has_far_prev, has_far_next = s > 1, s < slabs - 2

    barrier = pltpu.get_barrier_semaphore()
    for j in range(1, patches):
        pl.semaphore_signal(barrier, inc=1, device_id=(s, patch_peer(j)), device_id_type=MESH)
    for reach in (1, 2):

        @pl.when(s >= reach)
        def _():
            for j in range(patches):
                pl.semaphore_signal(barrier, inc=1, device_id=(s - reach, patch_peer(j)), device_id_type=MESH)

        @pl.when(s + reach < slabs)
        def _():
            for j in range(patches):
                pl.semaphore_signal(barrier, inc=1, device_id=(s + reach, patch_peer(j)), device_id_type=MESH)

    awaited = patches - 1 + patches * (slab_count(1) + slab_count(2))

    def remote(src, dst, send, recv, target):
        return pltpu.make_async_remote_copy(
            src_ref=src, dst_ref=dst, send_sem=send, recv_sem=recv, device_id=target, device_id_type=MESH
        )

    def slab_at(step):
        return jnp.clip(s + step, 0, slabs - 1)

    def patch_at(step):
        return jnp.clip(p + step, 0, patches - 1)

    def x_up(k):
        return remote(vb.at[k, ex - 1], halo_x.at[k, 0], sx.at[0], rx.at[k % 2, 0], (slab_at(1), p))

    def x_down(k):
        return remote(vb.at[k, 0], halo_x.at[k, 1], sx.at[1], rx.at[k % 2, 1], (slab_at(-1), p))

    def y_up(k):
        return remote(
            vb.at[k, :, pl.ds(ey - PACK, PACK)], halo_y.at[k, 0], sy.at[0], ry.at[k % 2, 0], (s, patch_at(1))
        )

    def y_down(k):
        return remote(vb.at[k, :, pl.ds(0, PACK)], halo_y.at[k, 1], sy.at[1], ry.at[k % 2, 1], (s, patch_at(-1)))

    def d_up():
        return remote(disp_ref.at[:, pl.ds(rows - EDGE, EDGE)], halo_d.at[0], sd.at[0], rd.at[0], (s, patch_at(1)))

    def d_down():
        return remote(disp_ref.at[:, pl.ds(0, EDGE)], halo_d.at[1], sd.at[1], rd.at[1], (s, patch_at(-1)))

    shift = ey - TIP
    side_base = (shift, 0)
    tip_base = [(DEEP + TIP * n + ey, DEEP + TIP * n) for n in range(2)]

    side_w = ex * (2 * SWEEPS - 1)
    side_v = SWEEPS + 2

    def near_copy(n):
        return remote(near_out, near_in.at[n], s_near.at[n], r_near.at[n], (slab_at(1 - 2 * n), p))

    def far_copy(n):
        return remote(far_out, far_in.at[n], s_far.at[n], r_far.at[n], (slab_at(2 - 4 * n), p))

    def side_copy(n):
        return remote(side_out.at[n], rim.at[pl.ds(side_base[n], DEEP)], s_side.at[n], r_side.at[n], (s, patch_at(1 - 2 * n)))

    def tip_copy(n, m):
        q = 2 * n + m
        return remote(tip_out.at[q], rim.at[pl.ds(tip_base[n][m], TIP)], s_tip.at[q], r_tip.at[q], (slab_at(1 - 2 * n), patch_at(1 - 2 * m)))

    to_s, from_s = (has_next_s, has_prev_s), (has_prev_s, has_next_s)
    to_p, from_p = (has_next_p, has_prev_p), (has_prev_p, has_next_p)
    to_far, from_far = (has_far_next, has_far_prev), (has_far_prev, has_far_next)
    corners = [(n, m) for n in range(2) for m in range(2)]
    def point_first(j):
        peer = patch_peer(j)
        src = point_ref.at[0, :, pl.ds(pl.multiple_of(peer * cap, cap), cap)]
        return remote(src, points.at[s, p], point_sem.at[0], point_sem.at[1], (s, peer))

    def point_second(j):
        return remote(points.at[s], points.at[s], point_sem.at[2], rp2.at[s], (slab_peer(j), p))

    def pull_copy(j, i):
        to = (slab_peer(j), patch_peer(i))
        here = pl.ds(pl.multiple_of(p * cap, cap), cap)
        return remote(pull_out.at[to[1]], pulls.at[s, :, here], pull_sem.at[0 if j else 1], rq.at[s], to)

    def pick_copy(j):
        peer = patch_peer(j)
        return remote(picks_out.at[peer], picks_in.at[p], pick_sem.at[0], pick_sem.at[1], (s, peer))

    def settle(ref, semaphore):
        pltpu.make_async_copy(ref, ref, semaphore).wait()

    def halo_sends(k, act):
        pl.when(has_next_s)(lambda: act(x_up(k)))
        pl.when(has_prev_s)(lambda: act(x_down(k)))
        if k > 0:
            pl.when(has_next_p)(lambda: act(y_up(k)))
            pl.when(has_prev_p)(lambda: act(y_down(k)))

    def send_halos(k):
        if k == 0:
            for n in range(2):
                pl.when(to_s[n])(lambda: near_copy(n).wait_send())
        else:
            halo_sends(k - 1, lambda copy: copy.wait_send())
        if k == 1:
            for n in range(2):
                pl.when(to_p[n])(lambda: side_copy(n).wait_send())
        halo_sends(k, lambda copy: copy.start())

    def build_points(slab):
        for k in range(patches):
            row, col = split_point(points[slab, k], cols)
            span = pl.ds(k * cap, cap)
            onehot_row[slab, :, span] = jnp.where(
                lax.broadcasted_iota(jnp.int32, (rows, cap), 0) == row, 1.0, 0.0
            ).astype(BF16)
            onehot_col[slab, :, span] = jnp.where(
                lax.broadcasted_iota(jnp.int32, (cols, cap), 0) == col, 1.0, 0.0
            ).astype(BF16)

    def lives(k):
        lane = lax.broadcasted_iota(jnp.int32, (1, cap), 1)
        return lane < count_ref[0, :, k : k + 1]

    def shell():
        pl.when(has_prev_p)(lambda: d_up().wait_recv())
        pl.when(has_next_p)(lambda: d_down().wait_recv())
        total = rows + 2 * EDGE
        line = lax.broadcasted_iota(jnp.int32, (total, cols), 0)
        first = jnp.where(has_prev_p, 0, EDGE)
        last = jnp.where(has_next_p, total, EDGE + rows)
        valid = (line >= first) & (line < last)
        gain = 1.0 / (36.0 * stiff_ref[...])
        gain_buf[...] = gain
        for c in range(comps):
            field = jnp.concatenate([halo_d[0, c], disp_ref[c], halo_d[1, c]], axis=0)
            field = jnp.where(valid, field, 0.0)
            bend = jnp.where(valid, laplace(field), 0.0)
            full = (laplace(bend) + 4.0 * bend)[EDGE : EDGE + rows]
            rest_buf[c] = disp_ref[c] - stiff_ref[...] * full * gain

    with jax.named_scope("w_mat"):
        ready(4, 3)
    with jax.named_scope("words"):
        words, rest = make_words(
            traction_ref[...], inverse_ref[...], matrix_ref[...], cx_ref[...], cy_ref[...]
        )
    ready(2)
    flat = 1.0 / scale_ref[...]
    w_own = jnp.concatenate([flat, blank(ex, wide_lanes - ey)], axis=1)
    ready(0)
    rounded0 = state_ref[...].astype(BF16)
    vb[0] = rounded0
    ready(1)
    wet = rhs_ref[...].astype(BF16)
    lane = lax.broadcasted_iota(jnp.int32, (1, wide_lanes), 1)
    low_half = lane < ey
    tail_half = lane < ey + ey // 2
    w_lines = jnp.concatenate([w_own] + [blank(ex, wide_lanes)] * (dof // wide_lanes - 1), axis=1)
    with jax.named_scope("project"):
        own_v = dot_nt(words, rounded0.reshape(wide_lanes, dof))
        own_r = dot_nt(rest, wet.reshape(wide_lanes, dof))
        packed = jnp.where(low_half, w_own[0:1], pltpu.roll(w_own[1:2], ey, 1))
        spare = join(
            blank(2 * DEEP - comps - 1, wide_lanes), own_r[2 * DEEP : 2 * DEEP + comps], packed
        )
        near_out[...] = join(
            own_v[0:DEEP], own_v[2 * DEEP : 4 * DEEP] + spare, own_v[4 * DEEP : 5 * DEEP], own_r[0:DEEP]
        ).astype(BF16)
        far_out[...] = own_v[2 * DEEP : 2 * DEEP + 8].astype(BF16)

        def state_at(i, c):
            return state_ref[i, c : c + 1]

        def rhs_at(i, c):
            return rhs_ref[i, c : c + 1]

        for m in range(2):
            close = [ey - 1 - j if m == 0 else j for j in range(SWEEPS)]
            if m == 1:
                side = [state_at(i, c) for i in range(ex) for c in close]
                side += [rhs_at(i, c) for i in range(ex) for c in close[: SWEEPS - 1]]
                side += [w_lines, blank(DEEP - side_w - ex, dof)]
            else:
                side = [w_lines, blank(side_v - ex, dof)]
                side += [state_at(i, c) for i in range(ex) for c in close[::-1]]
                side += [blank(1, dof)]
                side += [rhs_at(i, c) for i in range(ex) for c in close[: SWEEPS - 1][::-1]]
            side_out[m] = join(*side).astype(BF16)
            for n in range(2):
                r1, r2 = (ex - 1, ex - 2) if n == 0 else (0, 1)
                near2 = [state_at(r1, close[0]), state_at(r1, close[1])]
                last = [state_at(r2, close[0]), rhs_at(r1, close[0])]
                weigh = w_lines[r1 : r1 + 1]
                if m == 1:
                    tip = [weigh, blank(1, dof), *near2, *last, blank(TIP - 6, dof)]
                else:
                    tip = [*near2[::-1], blank(1, dof), *last, weigh, blank(TIP - 6, dof)]
                tip_out[2 * n + m] = join(*tip).astype(BF16)

    with jax.named_scope("w_barrier"):
        pl.semaphore_wait(barrier, awaited)
    for n, m in corners:
        pl.when(jnp.logical_and(to_s[n], to_p[m]))(lambda: tip_copy(n, m).start())
    for n in range(2):
        pl.when(to_s[n])(lambda: near_copy(n).start())
    for m in range(2):
        pl.when(to_p[m])(lambda: side_copy(m).start())
    for n in range(2):
        pl.when(to_far[n])(lambda: far_copy(n).start())
    if reaches:
        near_signal(0)
    ready(5)
    for j in range(1, patches):
        point_first(j).start()
    ready(7)
    pl.when(has_next_p)(lambda: d_up().start())
    pl.when(has_prev_p)(lambda: d_down().start())
    ready(6)
    for owner in range(patches):

        @pl.when(p == owner)
        def _():
            points[s, owner] = point_ref[0, :, owner * cap : (owner + 1) * cap]

    for owner in range(patches):
        elem = elem_ref[0, :, owner * cap : (owner + 1) * cap]
        for i in range(ex):
            line = lax.broadcasted_iota(jnp.int32, (wide_lanes, cap), 0)
            hit = (line + i * ey == elem) & (line < ey) & lives(owner)
            onehot_elem[owner, i] = jnp.where(hit, 1.0, 0.0).astype(BF16)
    if reaches:
        with jax.named_scope("w_reach"):
            near_wait(0)
        if len(reaches) > 1:
            near_signal(1)
    send_halos(0)
    scales = [column(scale_ref[i : i + 1, :]) for i in range(ex)]
    inverses = [1.0 / x for x in scales]

    def prelude(k):
        own = dot(vb[k].reshape(ex * ey, dof), matrix_ref[...]).reshape(ex, ey, dof)
        for i in range(ex):
            base_buf[i] = rhs_ref[i] - scales[i] * own[i]

    with jax.named_scope("shell"):
        shell()
    with jax.named_scope("prelude"):
        prelude(0)

    def halves(x):
        return jnp.where(low_half, x, 0.0), jnp.where(low_half, pltpu.roll(x, ey, 1), 0.0)

    span_rows = list(range(-ex, 2 * ex))

    def between(low, high):
        return (lane >= low) & (lane < high)

    def frame_mask(n, reach):
        right, left = has_next_p, has_prev_p
        if n is not None:
            right, left = jnp.logical_and(right, from_s[n]), jnp.logical_and(left, from_s[n])
        right, left = jnp.where(right, 1, 0), jnp.where(left, 1, 0)
        ahead, behind = between(ey, ey + reach), between(wide_lanes - reach, wide_lanes)
        return jnp.where(ahead, right, jnp.where(behind, left, 0)) > 0

    masks = {(n, reach): frame_mask(n, reach) for n in (None, 0, 1) for reach in range(1, SWEEPS + 1)}

    def framing(x, source, mask):
        return jnp.where(mask, pltpu.roll(x, (ey - source) % wide_lanes, 1), 0.0)

    with jax.named_scope("halves"):
        own_rows = list(zip(halves(own_v), halves(own_r)))
    with jax.named_scope("w_side"):
        for m in range(2):
            pl.when(from_p[m])(lambda: side_copy(m).wait_recv())
        for n, m in corners:
            pl.when(jnp.logical_and(from_s[n], from_p[m]))(lambda: tip_copy(n, m).wait_recv())
    for n in range(1, len(reaches)):
        with jax.named_scope("w_reach"):
            near_wait(n)
        if n + 1 < len(reaches):
            near_signal(n + 1)
    with jax.named_scope("w_pt1"):
        settle(points.at[s, pl.ds(0, patches - 1)], point_sem.at[1])
    for j in range(1, slabs):
        point_second(j).start()
    with jax.named_scope("place"):
        stack = rim[...]
        placed_v = dot_nt(words, stack)
        placed_r = dot_nt(rest, stack)

        def rim_row(base, at, ok):
            return jnp.where(ok, rim[base + at : base + at + 1, :wide_lanes].astype(F32), 0.0)

        def framed(middle, before, after):
            before, after = pltpu.roll(before, ey, 1), pltpu.roll(after, ey, 1)
            return jnp.where(low_half, middle, jnp.where(tail_half, after, before))

        w_rows = {}
        for i in range(ex):
            w_rows[i] = framed(
                w_own[i : i + 1],
                rim_row(side_base[0], i, has_prev_p),
                rim_row(side_base[1], side_w + i, has_next_p),
            )
        w_tips = [
            (
                rim_row(tip_base[n][0], 5, jnp.logical_and(from_s[n], has_prev_p)),
                rim_row(tip_base[n][1], 0, jnp.logical_and(from_s[n], has_next_p)),
            )
            for n in range(2)
        ]
        edges_v, edges_r = {}, {}
        for i in range(ex):
            edges_v[i] = framing(placed_v, SWEEPS * i, masks[None, SWEEPS])
            edges_r[i] = framing(placed_r, SWEEPS * ex + (SWEEPS - 1) * i, masks[None, SWEEPS - 1])
        for n in range(2):
            r1, r2 = (-1, -2) if n == 0 else (ex, ex + 1)
            base = tip_base[n][1]
            used = join(placed_v[:DEEP], placed_v[2 * DEEP : 5 * DEEP])
            edges_v[r1] = framing(used, base + 2, masks[n, 2])
            edges_v[r2] = framing(used, base + 4, masks[n, 1])
            edges_r[r1] = framing(placed_r[:DEEP], base + 5, masks[n, 1])

    with jax.named_scope("w_near"):
        for n in range(2):
            pl.when(from_far[n])(lambda: far_copy(n).wait_recv())
            pl.when(from_s[n])(lambda: near_copy(n).wait_recv())

    with jax.named_scope("stencil"):
        by_d, by_x, by_y, by_r2, by_r1, by_r0 = {}, {}, {}, {}, {}, {}
        for i, (v_half, r_half) in enumerate(own_rows):
            full, side = v_half + edges_v[i], r_half + edges_r[i]
            by_d[i], by_x[i], by_y[i] = (full[k * 2 * DEEP : (k + 1) * 2 * DEEP] for k in range(3))
            by_r2[i], by_r1[i], by_r0[i] = (
                side[: 2 * DEEP], side[2 * DEEP : 2 * DEEP + 3 * comps], side[3 * DEEP : 3 * DEEP + comps]
            )
        for n in range(2):
            got = jnp.where(from_s[n], near_in[n].astype(F32), 0.0)
            for i, half in enumerate(halves(got)):
                r = i - ex if n == 0 else i + ex
                edge = edges_v[r]
                by_d[r] = half[0:DEEP] + edge[0:DEEP]
                by_x[r] = half[DEEP : 3 * DEEP] + edge[DEEP : 3 * DEEP]
                by_y[r] = half[3 * DEEP : 4 * DEEP] + edge[3 * DEEP : 4 * DEEP]
                by_r2[r] = half[4 * DEEP : 5 * DEEP]
                if r in edges_r:
                    by_r2[r] = by_r2[r] + edges_r[r]
                by_r1[r] = half[3 * DEEP - comps - 1 : 3 * DEEP - 1]
                w_rows[r] = half[3 * DEEP - 1 : 3 * DEEP]
                if r in (-1, ex):
                    w_rows[r] = framed(w_rows[r], *w_tips[n])
            beyond = halves(jnp.where(from_far[n], far_in[n].astype(F32), 0.0))[1 - n]
            by_x[-ex - 1 if n == 0 else 2 * ex] = join(beyond, blank(DEEP - 8, wide_lanes))

        def turn(x):
            return pltpu.roll(x, 1, 1) + pltpu.roll(x, wide_lanes - 1, 1)

        one = {}
        for r in span_rows:
            n = 2 * DEEP if 0 <= r < ex else DEEP
            one[r] = by_d[r] + w_rows[r] * (by_x[r - 1][:n] + by_x[r + 1][:n] + turn(by_y[r]) + by_r2[r])
        two = {}
        for r in range(-1, ex + 1):
            if 0 <= r < ex:
                d_part = join(one[r][:comps], one[r][DEEP : DEEP + 2 * comps])
                y_part = join(one[r][4 * comps : 5 * comps], one[r][DEEP + 2 * comps : DEEP + 4 * comps])
                n = 3 * comps
            else:
                d_part, y_part = one[r][:comps], one[r][4 * comps : 5 * comps]
                n = comps
            x_part = one[r - 1][comps : comps + n] + one[r + 1][comps : comps + n]
            two[r] = d_part + w_rows[r] * (x_part + turn(y_part) + by_r1[r])
        drawn = []
        for r in range(ex):
            x_part = two[r - 1][:comps] + two[r + 1][:comps]
            drawn.append(
                two[r][comps : 2 * comps]
                + w_rows[r] * (x_part + turn(two[r][2 * comps : 3 * comps]) + by_r0[r])
            )
        tractions = [jnp.where(low_half, x, 0.0).astype(BF16) for x in drawn]
        for owner in range(patches):
            pull_out[owner] = sum(dot(tractions[i], onehot_elem[owner, i]) for i in range(ex)).astype(BF16)
    with jax.named_scope("s_pull"):
        for j in sorted(range(slabs), key=lambda j: -min(j, slabs - j)):
            for i in range(patches):
                if (j, i) != (0, 0):
                    pull_copy(j, i).start()
    for owner in range(patches):

        @pl.when(p == owner)
        def _():
            pulls[s, :, owner * cap : (owner + 1) * cap] = pull_out[owner]


    def sweep(k, v):
        rounded = vb[k]
        wide = rounded.astype(F32)
        with jax.named_scope("w_halo"):
            if k > 0:
                pl.when(has_prev_p)(lambda: y_up(k).wait_recv())
                pl.when(has_next_p)(lambda: y_down(k).wait_recv())
            pl.when(has_prev_s)(lambda: x_up(k).wait_recv())
            pl.when(has_next_s)(lambda: x_down(k).wait_recv())
        line = lax.broadcasted_iota(jnp.int32, (ey, dof), 0)
        along_y = []
        for i in range(ex):
            if k == 0:
                at = shift + side_v + SWEEPS * (i + 1) - 1
                before = rim[at : at + 1].astype(F32)
                after = rim[SWEEPS * i : SWEEPS * i + 1].astype(F32)
            else:
                before = halo_y[k, 0, i].astype(F32)[PACK - 1 : PACK]
                after = halo_y[k, 1, i].astype(F32)[0:1]
            before = jnp.where(has_prev_p, before, 0.0)
            after = jnp.where(has_next_p, after, 0.0)
            prev = jnp.where(line == 0, jnp.broadcast_to(before, (ey, dof)), pltpu.roll(wide[i], 1, 0))
            following = jnp.where(line == ey - 1, jnp.broadcast_to(after, (ey, dof)), pltpu.roll(wide[i], ey - 1, 0))
            along_y.append((prev + following).astype(BF16))
        side_y = dot(jnp.concatenate(along_y, axis=0), cy_ref[...])
        low = jnp.where(has_prev_s, halo_x[k, 0].astype(F32), 0.0)
        high = jnp.where(has_next_s, halo_x[k, 1].astype(F32), 0.0)
        along_x = []
        for i in range(ex):
            below = low if i == 0 else wide[i - 1]
            above = high if i == ex - 1 else wide[i + 1]
            along_x.append((below + above).astype(BF16))
        side_x = dot(jnp.concatenate(along_x, axis=0), cx_ref[...])
        side = (side_x + side_y).reshape(ex, ey, dof)
        residue = jnp.concatenate([(base_buf[i] + side[i]).astype(BF16) for i in range(ex)], axis=0)
        update = dot(residue, inverse_ref[...]).reshape(ex, ey, dof)
        return [v[i] + update[i] * inverses[i] for i in range(ex)]

    def keep(v, k):
        for i in range(ex):
            fluid_ref[i] = v[i]
            if k < SWEEPS:
                vb[k, i] = v[i].astype(BF16)

    with jax.named_scope("sweep0"):
        keep(sweep(0, state_ref), 1)
        send_halos(1)
        prelude(1)

    def scatter(slab, acc):
        hot = onehot_row[slab]
        value = pulls[slab]
        scaled = jnp.concatenate([hot * value[c : c + 1] for c in range(comps)], axis=0)
        return acc + dot_nt(scaled, onehot_col[slab])

    inner = jnp.minimum(s, slabs - 1 - s)

    def nearest(t):
        step = lax.div(t + 1, 2)
        alternate = jnp.where(lax.rem(t, 2) == 1, s + step, s - step)
        return jnp.where(t <= 2 * inner, alternate, jnp.where(s < slabs - 1 - s, t, slabs - 1 - t))

    def prepared(t, carry):
        slab = nearest(t)
        with jax.named_scope("w_point"):
            settle(points.at[slab], rp2.at[slab])
        build_points(slab)
        return carry

    def gathered(t, acc):
        slab = nearest(t)
        with jax.named_scope("w_pull"):
            settle(pulls.at[slab], rq.at[slab])
        return scatter(slab, acc)

    half = (slabs + 1) // 2
    build_points(s)
    with jax.named_scope("build1"):
        lax.fori_loop(1, half, prepared, 0)
    with jax.named_scope("w_own"):
        settle(pulls.at[s, :, pl.ds(0, (patches - 1) * cap)], rq.at[s])
    acc = scatter(s, jnp.zeros((comps * rows, cols), F32))
    with jax.named_scope("gather1"):
        acc = lax.fori_loop(1, half, gathered, acc)
    with jax.named_scope("sweep1"):
        keep(sweep(1, fluid_ref), 2)
        send_halos(2)
    with jax.named_scope("build2"):
        lax.fori_loop(half, slabs, prepared, 0)
    with jax.named_scope("gather2"):
        acc = lax.fori_loop(half, slabs, gathered, acc)
    loads = acc.reshape(comps, rows, cols)
    fresh = [rest_buf[c] + loads[c] * gain_buf[...] for c in range(comps)]
    narrow = jnp.concatenate([x.astype(BF16) for x in fresh], axis=0)
    for k in range(patches):
        span = pl.ds(k * cap, cap)
        spread = dot(narrow, onehot_col[s, :, span]).reshape(comps, rows, cap)
        hot = onehot_row[s, :, span].astype(F32)
        for c in range(comps):
            picks_out[k, c : c + 1] = jnp.sum(spread[c] * hot, axis=0, keepdims=True).astype(BF16)
    with jax.named_scope("s_pick"):
        for j in range(1, patches):
            pick_copy(j).start()
    picks_in[p] = picks_out[p]
    for c in range(comps):
        net_ref[c] = fresh[c]
    with jax.named_scope("sweep2"):
        prelude(2)
        keep(sweep(2, fluid_ref), SWEEPS)
    with jax.named_scope("w_pick"):
        settle(picks_in.at[pl.ds(0, patches - 1)], pick_sem.at[1])
    for k in range(patches):
        live = lives(k)
        for c in range(comps):
            wall_ref[c, 0, :, k * cap : (k + 1) * cap] = jnp.where(live, picks_in[k, c : c + 1].astype(F32), 0.0)

    with jax.named_scope("drain"):
        halo_sends(SWEEPS - 1, lambda copy: copy.wait_send())
        pl.when(has_next_p)(lambda: d_up().wait_send())
        pl.when(has_prev_p)(lambda: d_down().wait_send())
        for n in range(2):
            pl.when(to_far[n])(lambda: far_copy(n).wait_send())
        for n, m in corners:
            pl.when(jnp.logical_and(to_s[n], to_p[m]))(lambda: tip_copy(n, m).wait_send())
        settle(points.at[s, pl.ds(0, patches - 1)], point_sem.at[0])
        settle(points.at[pl.ds(0, slabs - 1)], point_sem.at[2])
        settle(pulls.at[pl.ds(0, slabs - 1)], pull_sem.at[0])
        settle(pulls.at[s, :, pl.ds(0, (patches - 1) * cap)], pull_sem.at[1])
        settle(picks_in.at[pl.ds(0, patches - 1)], pick_sem.at[0])


def deliver(*refs):
    copies = [pltpu.make_async_copy(refs[n], refs[n + 3], refs[6].at[n]) for n in range(3)]
    for copy in copies:
        copy.start()
    for copy in copies:
        copy.wait()


def shards(slabs, patches, *args):
    state, disp, elem = args[0], args[11], args[8]
    ex, ey, dof = state.shape
    comps, rows, cols = disp.shape
    cap = elem.shape[2] // patches
    sem = pltpu.SemaphoreType.DMA
    vmem = pl.BlockSpec(memory_space=pltpu.VMEM)
    hot_bytes = slabs * patches * cap * (rows + cols) * 2
    outs = pl.pallas_call(
        functools.partial(kernel, slabs, patches, len(args)),
        out_shape=(
            pltpu.VMEM(state.shape, F32),
            pltpu.VMEM(disp.shape, F32),
            pltpu.VMEM((comps, 1, 1, elem.shape[2]), F32),
        ),
        in_specs=[pl.BlockSpec(memory_space=pltpu.HBM)] * len(args),
        out_specs=(vmem, vmem, vmem),
        scratch_shapes=[pltpu.VMEM(x.shape, x.dtype) for x in args[:3]]
        + [
            pltpu.VMEM((4,) + args[3].shape, BF16),
            pltpu.VMEM(args[7].shape, BF16),
            pltpu.VMEM((2,) + elem.shape, jnp.int32),
            pltpu.VMEM(args[10].shape, jnp.int32),
            pltpu.VMEM((comps + 1, rows, cols), F32),
            pltpu.VMEM((SWEEPS, ex, ey, dof), BF16),
            pltpu.VMEM((SWEEPS, 2, ey, dof), BF16),
            pltpu.VMEM((SWEEPS, 2, ex, PACK, dof), BF16),
            pltpu.VMEM((2, comps, EDGE, cols), F32),
            pltpu.VMEM((slabs, patches, 1, cap), jnp.int32),
            pltpu.VMEM((slabs, comps, patches * cap), BF16),
            pltpu.VMEM((patches, comps, cap), BF16),
            pltpu.VMEM((patches, comps, cap), BF16),
            pltpu.VMEM((patches, comps, cap), BF16),
            pltpu.VMEM((patches, ex, ex * ey, cap), BF16),
            pltpu.VMEM((slabs, rows, patches * cap), BF16),
            pltpu.VMEM((slabs, cols, patches * cap), BF16),
            pltpu.VMEM((comps, rows, cols), F32),
            pltpu.VMEM((rows, cols), F32),
            pltpu.VMEM(state.shape, F32),
            pltpu.VMEM((5 * DEEP, ex * ey), BF16),
            pltpu.VMEM((2, 5 * DEEP, ex * ey), BF16),
            pltpu.VMEM((8, ex * ey), BF16),
            pltpu.VMEM((2, 8, ex * ey), BF16),
            pltpu.VMEM((2, DEEP, dof), BF16),
            pltpu.VMEM((4, TIP, dof), BF16),
            pltpu.VMEM((ex * ey, dof), BF16),
            sem((8,)),
            sem((2, 2)),
            sem((2, 2)),
            sem((2,)),
            sem((2,)),
            sem((3,)),
            sem((slabs,)),
            sem((2,)),
            sem((slabs,)),
            sem((2,)),
            sem((2,)),
            sem((2,)),
            sem((2,)),
            sem((2,)),
            sem((2,)),
            sem((2,)),
            sem((4,)),
            sem((4,)),
            pltpu.SemaphoreType.REGULAR((max(slabs.bit_length() - 2, 1),)),
        ],
        compiler_params=pltpu.CompilerParams(collective_id=0, has_side_effects=True),
    )(*args)
    return pl.pallas_call(
        deliver,
        out_shape=tuple(jax.ShapeDtypeStruct(x.shape, x.dtype) for x in outs),
        in_specs=[vmem] * 3,
        out_specs=(pl.BlockSpec(memory_space=pltpu.HBM),) * 3,
        scratch_shapes=[sem((3,))],
    )(*[pltpu.with_memory_space_constraint(x, pltpu.VMEM) for x in outs])


def solution(mesh):
    return jax.shard_map(
        functools.partial(shards, mesh.shape["slab"], mesh.shape["patch"]),
        mesh=mesh,
        in_specs=(
            P("slab", "patch", None),
            P("slab", "patch", None),
            P("slab", "patch"),
            P(),
            P(),
            P(),
            P(),
            P(),
            P("slab", "patch", None),
            P("slab", "patch", None),
            P("slab", "patch", None),
            P(None, "patch", None),
            P("patch", None),
        ),
        out_specs=(
            P("slab", "patch", None),
            P(None, "patch", None),
            P(None, "slab", "patch", None),
        ),
        check_vma=False,
    )
```

```python
import functools

import jax
import jax.numpy as jnp
from jax import lax
from jax.experimental import pallas as pl
from jax.experimental.pallas import tpu as pltpu
from jax.sharding import PartitionSpec as P

SWEEPS = 3
PACK = 16
EDGE = 8
SPARE = 8 * 2**20
DEEP = 16
TIP = 8
LOAD_ORDER = (7, 6, 3, 4, 5, 0, 1, 2, 9, 8, 10, 11, 12)
MESH = pl.DeviceIdType.MESH
F32 = jnp.float32
BF16 = jnp.bfloat16


def dot(a, b):
    return jnp.dot(a, b, preferred_element_type=F32)


def dot_nt(a, b):
    return lax.dot_general(a, b, (((1,), (1,)), ((), ())), preferred_element_type=F32)


def split_point(point, cols):
    if cols & (cols - 1) == 0:
        return lax.shift_right_logical(point, cols.bit_length() - 1), point & (cols - 1)
    row = lax.div(point, cols)
    return row, point - row * cols


def column(row_vector):
    n = row_vector.shape[1]
    shape = (n, n)
    eye = lax.broadcasted_iota(jnp.int32, shape, 0) == lax.broadcasted_iota(jnp.int32, shape, 1)
    return jnp.sum(jnp.where(eye, jnp.broadcast_to(row_vector, shape), 0.0), axis=1, keepdims=True)


def laplace(x):
    rows, cols = x.shape
    lane = lax.broadcasted_iota(jnp.int32, x.shape, 1)
    left = jnp.where(lane == 0, 0.0, pltpu.roll(x, 1, 1))
    right = jnp.where(lane == cols - 1, 0.0, pltpu.roll(x, cols - 1, 1))
    return 4.0 * x - (pltpu.roll(x, 1, 0) + pltpu.roll(x, rows - 1, 0) + left + right)


def join(*parts):
    return jnp.concatenate(parts, axis=0)


def blank(rows, cols):
    return jnp.zeros((rows, cols), F32)


def first_words(base0, traction, matrix, couple_x, couple_y):
    low = base0.astype(BF16)
    return join(dot_nt(low, couple_x), traction.astype(F32) - dot_nt(low, matrix), dot_nt(low, couple_y))


def second_words(base1, one, comps, matrix, couple_x, couple_y):
    low = base1.astype(BF16)
    by_x, by_y = dot_nt(low, couple_x), dot_nt(low, couple_y)
    by_d = one - dot_nt(low, matrix)
    dof = one.shape[1]
    return join(
        by_d[:comps], by_x, by_y[:comps], blank(DEEP - 5 * comps, dof),
        by_d[comps:], by_y[comps:], blank(DEEP - 4 * comps, dof),
    )


def third_words(base2, two, matrix, couple_x, couple_y):
    low = base2.astype(BF16)
    return join(two - dot_nt(low, matrix), dot_nt(low, couple_x), dot_nt(low, couple_y)).astype(BF16)


def stacked(two, one, none):
    comps, dof = none.shape
    return join(two, one, blank(DEEP - 3 * comps, dof), none, blank(DEEP - comps, dof)).astype(BF16)


def kernel(slabs, patches, args, *refs):
    hbm, refs = refs[:args], refs[args:]
    (fluid_ref, net_ref, wall_ref), refs = refs[:3], refs[3:]
    (state_ref, rhs_ref, scale_ref, matrices, traction_ref, slots, count_ref, nets, inverse_ref) = refs[:9]
    refs = refs[9:]
    cx_ref, cy_ref, matrix_ref = (matrices.at[n] for n in range(3))
    elem_ref, point_ref = slots.at[0], slots.at[1]
    (vb, halo_x, halo_y, halo_d, points, pulls, pull_out, picks_out, picks_in) = refs[:9]
    (onehot_elem, onehot_row, onehot_col, rest_buf, gain_buf, base_buf) = refs[9:15]
    (near_out, near_in, far_out, far_in, side_out, tip_out, rim) = refs[15:22]
    (load_sem, rx, ry, rd, point_sem, rp2, pull_sem, rq, pick_sem) = refs[22:31]
    (r_near, s_far, r_far, r_side, r_tip, near_sem) = refs[31:]
    s_near, s_side, s_tip = load_sem.at[pl.ds(0, 2)], load_sem.at[pl.ds(2, 2)], load_sem.at[pl.ds(4, 4)]
    sx, sy, sd = s_near, s_side, s_far
    comps = nets.shape[0] - 1
    disp_ref, stiff_ref = nets.at[pl.ds(0, comps)], nets.at[comps]
    homes = (
        (state_ref, 0), (rhs_ref, 1), (scale_ref, 2), (matrix_ref, 3), (cx_ref, 3), (cy_ref, 3), (inverse_ref, 8),
        (traction_ref, 4), (elem_ref, 5), (point_ref, 5), (count_ref, 6), (disp_ref, 7), (stiff_ref, 7),
    )

    loads_in = [pltpu.make_async_copy(hbm[n], homes[n][0], load_sem.at[homes[n][1]]) for n in range(args)]
    for n in LOAD_ORDER:
        loads_in[n].start()
    groups = (state_ref, rhs_ref, scale_ref, matrices, traction_ref, slots, count_ref, nets, inverse_ref)

    def ready(*names):
        for n in names:
            pltpu.make_async_copy(groups[n], groups[n], load_sem.at[n]).wait()

    s = lax.axis_index("slab")
    p = lax.axis_index("patch")
    ex, ey, dof = state_ref.shape
    rows, cols = stiff_ref.shape
    cap = elem_ref.shape[2] // patches
    wide_lanes = ex * ey

    def slab_peer(j):
        return lax.rem(s + j, slabs)

    def patch_peer(j):
        return lax.rem(p + j, patches)

    def slab_sides(reach, semaphore):
        @pl.when(s >= reach)
        def _():
            pl.semaphore_signal(semaphore, inc=1, device_id=(s - reach, p), device_id_type=MESH)

        @pl.when(s + reach < slabs)
        def _():
            pl.semaphore_signal(semaphore, inc=1, device_id=(s + reach, p), device_id_type=MESH)

    def slab_count(reach):
        return jnp.where(s >= reach, 1, 0) + jnp.where(s + reach < slabs, 1, 0)

    reaches = []
    while 2 ** (len(reaches) + 1) < slabs - 1:
        reaches.append(2 ** (len(reaches) + 1))

    def near_signal(n):
        slab_sides(reaches[n], near_sem.at[n])

    def near_wait(n):
        pl.semaphore_wait(near_sem.at[n], slab_count(reaches[n]))

    has_prev_s, has_next_s = s > 0, s < slabs - 1
    has_prev_p, has_next_p = p > 0, p < patches - 1
    has_far_prev, has_far_next = s > 1, s < slabs - 2

    barrier = pltpu.get_barrier_semaphore()
    for j in range(1, patches):
        pl.semaphore_signal(barrier, inc=1, device_id=(s, patch_peer(j)), device_id_type=MESH)
    for reach in (1, 2):

        @pl.when(s >= reach)
        def _():
            for j in range(patches):
                pl.semaphore_signal(barrier, inc=1, device_id=(s - reach, patch_peer(j)), device_id_type=MESH)

        @pl.when(s + reach < slabs)
        def _():
            for j in range(patches):
                pl.semaphore_signal(barrier, inc=1, device_id=(s + reach, patch_peer(j)), device_id_type=MESH)

    awaited = patches - 1 + patches * (slab_count(1) + slab_count(2))

    def remote(src, dst, send, recv, target):
        return pltpu.make_async_remote_copy(
            src_ref=src, dst_ref=dst, send_sem=send, recv_sem=recv, device_id=target, device_id_type=MESH
        )

    def slab_at(step):
        return jnp.clip(s + step, 0, slabs - 1)

    def patch_at(step):
        return jnp.clip(p + step, 0, patches - 1)

    def x_up(k):
        return remote(vb.at[k, ex - 1], halo_x.at[k, 0], sx.at[0], rx.at[k % 2, 0], (slab_at(1), p))

    def x_down(k):
        return remote(vb.at[k, 0], halo_x.at[k, 1], sx.at[1], rx.at[k % 2, 1], (slab_at(-1), p))

    def y_up(k):
        return remote(
            vb.at[k, :, pl.ds(ey - PACK, PACK)], halo_y.at[k, 0], sy.at[0], ry.at[k % 2, 0], (s, patch_at(1))
        )

    def y_down(k):
        return remote(vb.at[k, :, pl.ds(0, PACK)], halo_y.at[k, 1], sy.at[1], ry.at[k % 2, 1], (s, patch_at(-1)))

    def d_up():
        return remote(disp_ref.at[:, pl.ds(rows - EDGE, EDGE)], halo_d.at[0], sd.at[0], rd.at[0], (s, patch_at(1)))

    def d_down():
        return remote(disp_ref.at[:, pl.ds(0, EDGE)], halo_d.at[1], sd.at[1], rd.at[1], (s, patch_at(-1)))

    shift = ey - TIP
    side_base = (shift, 0)
    tip_base = [(DEEP + TIP * n + ey, DEEP + TIP * n) for n in range(2)]

    side_w = ex * (2 * SWEEPS - 1)
    side_v = SWEEPS + 2

    def near_copy(n):
        return remote(near_out, near_in.at[n], s_near.at[n], r_near.at[n], (slab_at(1 - 2 * n), p))

    def far_copy(n):
        return remote(far_out, far_in.at[n], s_far.at[n], r_far.at[n], (slab_at(2 - 4 * n), p))

    def side_copy(n):
        return remote(side_out.at[n], rim.at[pl.ds(side_base[n], DEEP)], s_side.at[n], r_side.at[n], (s, patch_at(1 - 2 * n)))

    def tip_copy(n, m):
        q = 2 * n + m
        return remote(tip_out.at[q], rim.at[pl.ds(tip_base[n][m], TIP)], s_tip.at[q], r_tip.at[q], (slab_at(1 - 2 * n), patch_at(1 - 2 * m)))

    to_s, from_s = (has_next_s, has_prev_s), (has_prev_s, has_next_s)
    to_p, from_p = (has_next_p, has_prev_p), (has_prev_p, has_next_p)
    to_far, from_far = (has_far_next, has_far_prev), (has_far_prev, has_far_next)
    corners = [(n, m) for n in range(2) for m in range(2)]
    def point_first(j):
        peer = patch_peer(j)
        src = point_ref.at[0, :, pl.ds(pl.multiple_of(peer * cap, cap), cap)]
        return remote(src, points.at[s, p], point_sem.at[0], point_sem.at[1], (s, peer))

    def point_second(j):
        return remote(points.at[s], points.at[s], point_sem.at[2], rp2.at[s], (slab_peer(j), p))

    def pull_copy(j, i):
        to = (slab_peer(j), patch_peer(i))
        here = pl.ds(pl.multiple_of(p * cap, cap), cap)
        return remote(pull_out.at[to[1]], pulls.at[s, :, here], pull_sem.at[0 if j else 1], rq.at[s], to)

    def pick_copy(j):
        peer = patch_peer(j)
        return remote(picks_out.at[peer], picks_in.at[p], pick_sem.at[0], pick_sem.at[1], (s, peer))

    def settle(ref, semaphore):
        pltpu.make_async_copy(ref, ref, semaphore).wait()

    def halo_sends(k, act):
        pl.when(has_next_s)(lambda: act(x_up(k)))
        pl.when(has_prev_s)(lambda: act(x_down(k)))
        if k > 0:
            pl.when(has_next_p)(lambda: act(y_up(k)))
            pl.when(has_prev_p)(lambda: act(y_down(k)))

    def send_halos(k):
        if k == 0:
            for n in range(2):
                pl.when(to_s[n])(lambda: near_copy(n).wait_send())
        else:
            halo_sends(k - 1, lambda copy: copy.wait_send())
        if k == 1:
            for n in range(2):
                pl.when(to_p[n])(lambda: side_copy(n).wait_send())
        halo_sends(k, lambda copy: copy.start())

    def build_points(slab):
        for k in range(patches):
            row, col = split_point(points[slab, k], cols)
            span = pl.ds(k * cap, cap)
            onehot_row[slab, :, span] = jnp.where(
                lax.broadcasted_iota(jnp.int32, (rows, cap), 0) == row, 1.0, 0.0
            ).astype(BF16)
            onehot_col[slab, :, span] = jnp.where(
                lax.broadcasted_iota(jnp.int32, (cols, cap), 0) == col, 1.0, 0.0
            ).astype(BF16)

    def lives(k):
        lane = lax.broadcasted_iota(jnp.int32, (1, cap), 1)
        return lane < count_ref[0, :, k : k + 1]

    def shell():
        pl.when(has_prev_p)(lambda: d_up().wait_recv())
        pl.when(has_next_p)(lambda: d_down().wait_recv())
        total = rows + 2 * EDGE
        line = lax.broadcasted_iota(jnp.int32, (total, cols), 0)
        first = jnp.where(has_prev_p, 0, EDGE)
        last = jnp.where(has_next_p, total, EDGE + rows)
        valid = (line >= first) & (line < last)
        gain = 1.0 / (36.0 * stiff_ref[...])
        gain_buf[...] = gain
        for c in range(comps):
            field = jnp.concatenate([halo_d[0, c], disp_ref[c], halo_d[1, c]], axis=0)
            field = jnp.where(valid, field, 0.0)
            bend = jnp.where(valid, laplace(field), 0.0)
            full = (laplace(bend) + 4.0 * bend)[EDGE : EDGE + rows]
            rest_buf[c] = disp_ref[c] - stiff_ref[...] * full * gain

    with jax.named_scope("w_mat"):
        ready(4, 8)
        base0 = dot_nt(traction_ref[...], inverse_ref[...])
        ready(3, 0, 1, 2)
    rounded0 = state_ref[...].astype(BF16)
    vb[0] = rounded0
    wet = rhs_ref[...].astype(BF16)
    flat = 1.0 / scale_ref[...]
    w_own = jnp.concatenate([flat, blank(ex, wide_lanes - ey)], axis=1)
    lane = lax.broadcasted_iota(jnp.int32, (1, wide_lanes), 1)
    low_half = lane < ey
    tail_half = lane < ey + ey // 2
    w_lines = jnp.concatenate([w_own] + [blank(ex, wide_lanes)] * (dof // wide_lanes - 1), axis=1)
    with jax.named_scope("project"):
        couples = (matrix_ref[...], cx_ref[...], cy_ref[...])
        one = first_words(base0, traction_ref[...], *couples)
        base1 = dot_nt(one.astype(BF16), inverse_ref[...])
        two = second_words(base1, one, comps, *couples)
        flow = rounded0.reshape(wide_lanes, dof)
        passed = join(*[dot(flow, couple) for couple in couples]).astype(BF16)
        mapped = dot(join(passed, wet.reshape(wide_lanes, dof)), inverse_ref[...])
        turned = join(flow.astype(F32) - mapped[:wide_lanes], mapped[wide_lanes:]).astype(BF16)
        both = dot_nt(stacked(two, one, traction_ref[...].astype(F32)), turned)
        own_v = join(*[both[: 2 * DEEP, n * wide_lanes : (n + 1) * wide_lanes] for n in range(3)])
        own_r = both[:, 3 * wide_lanes :]
        packed = jnp.where(low_half, w_own[0:1], pltpu.roll(w_own[1:2], ey, 1))
        spare = join(
            blank(2 * DEEP - comps - 1, wide_lanes), own_r[2 * DEEP : 2 * DEEP + comps], packed
        )
        near_out[...] = join(
            own_v[0:DEEP], own_v[2 * DEEP : 4 * DEEP] + spare, own_v[4 * DEEP : 5 * DEEP], own_r[0:DEEP]
        ).astype(BF16)
        far_out[...] = own_v[2 * DEEP : 2 * DEEP + 8].astype(BF16)

        def state_at(i, c):
            return state_ref[i, c : c + 1]

        def rhs_at(i, c):
            return rhs_ref[i, c : c + 1]

        for m in range(2):
            close = [ey - 1 - j if m == 0 else j for j in range(SWEEPS)]
            if m == 1:
                side = [state_at(i, c) for i in range(ex) for c in close]
                side += [rhs_at(i, c) for i in range(ex) for c in close[: SWEEPS - 1]]
                side += [w_lines, blank(DEEP - side_w - ex, dof)]
            else:
                side = [w_lines, blank(side_v - ex, dof)]
                side += [state_at(i, c) for i in range(ex) for c in close[::-1]]
                side += [blank(1, dof)]
                side += [rhs_at(i, c) for i in range(ex) for c in close[: SWEEPS - 1][::-1]]
            side_out[m] = join(*side).astype(BF16)
            for n in range(2):
                r1, r2 = (ex - 1, ex - 2) if n == 0 else (0, 1)
                near2 = [state_at(r1, close[0]), state_at(r1, close[1])]
                last = [state_at(r2, close[0]), rhs_at(r1, close[0])]
                weigh = w_lines[r1 : r1 + 1]
                if m == 1:
                    tip = [weigh, blank(1, dof), *near2, *last, blank(TIP - 6, dof)]
                else:
                    tip = [*near2[::-1], blank(1, dof), *last, weigh, blank(TIP - 6, dof)]
                tip_out[2 * n + m] = join(*tip).astype(BF16)

    ready(5, 6, 7)
    with jax.named_scope("w_barrier"):
        pl.semaphore_wait(barrier, awaited)
    for n, m in corners:
        pl.when(jnp.logical_and(to_s[n], to_p[m]))(lambda: tip_copy(n, m).start())
    for n in range(2):
        pl.when(to_s[n])(lambda: near_copy(n).start())
    for m in range(2):
        pl.when(to_p[m])(lambda: side_copy(m).start())
    for n in range(2):
        pl.when(to_far[n])(lambda: far_copy(n).start())
    if reaches:
        near_signal(0)
    for j in range(1, patches):
        point_first(j).start()
    for owner in range(patches):

        @pl.when(p == owner)
        def _():
            points[s, owner] = point_ref[0, :, owner * cap : (owner + 1) * cap]

    for owner in range(patches):
        elem = elem_ref[0, :, owner * cap : (owner + 1) * cap]
        for i in range(ex):
            line = lax.broadcasted_iota(jnp.int32, (wide_lanes, cap), 0)
            hit = (line + i * ey == elem) & (line < ey) & lives(owner)
            onehot_elem[owner, i] = jnp.where(hit, 1.0, 0.0).astype(BF16)
    if reaches:
        with jax.named_scope("w_reach"):
            near_wait(0)
        if len(reaches) > 1:
            near_signal(1)
    send_halos(0)
    scales = [column(scale_ref[i : i + 1, :]) for i in range(ex)]
    inverses = [1.0 / x for x in scales]

    def prelude(k):
        own = dot(vb[k].reshape(ex * ey, dof), matrix_ref[...]).reshape(ex, ey, dof)
        for i in range(ex):
            base_buf[i] = rhs_ref[i] - scales[i] * own[i]

    for n in range(2):
        pl.when(to_far[n])(lambda: far_copy(n).wait_send())
    pl.when(has_next_p)(lambda: d_up().start())
    pl.when(has_prev_p)(lambda: d_down().start())
    with jax.named_scope("late_words"):
        base2 = dot_nt(two.astype(BF16), inverse_ref[...])
        words = third_words(base2, two, matrix_ref[...], cx_ref[...], cy_ref[...])
        rest = stacked(base2, base1, base0)
    with jax.named_scope("prelude"):
        prelude(0)

    def halves(x):
        return jnp.where(low_half, x, 0.0), jnp.where(low_half, pltpu.roll(x, ey, 1), 0.0)

    span_rows = list(range(-ex, 2 * ex))

    def between(low, high):
        return (lane >= low) & (lane < high)

    def frame_mask(n, reach):
        right, left = has_next_p, has_prev_p
        if n is not None:
            right, left = jnp.logical_and(right, from_s[n]), jnp.logical_and(left, from_s[n])
        right, left = jnp.where(right, 1, 0), jnp.where(left, 1, 0)
        ahead, behind = between(ey, ey + reach), between(wide_lanes - reach, wide_lanes)
        return jnp.where(ahead, right, jnp.where(behind, left, 0)) > 0

    masks = {(n, reach): frame_mask(n, reach) for n in (None, 0, 1) for reach in range(1, SWEEPS + 1)}

    def framing(x, source, mask):
        return jnp.where(mask, pltpu.roll(x, (ey - source) % wide_lanes, 1), 0.0)

    with jax.named_scope("halves"):
        own_rows = list(zip(halves(own_v), halves(own_r)))
    with jax.named_scope("w_side"):
        for m in range(2):
            pl.when(from_p[m])(lambda: side_copy(m).wait_recv())
        for n, m in corners:
            pl.when(jnp.logical_and(from_s[n], from_p[m]))(lambda: tip_copy(n, m).wait_recv())
    for n in range(1, len(reaches)):
        with jax.named_scope("w_reach"):
            near_wait(n)
        if n + 1 < len(reaches):
            near_signal(n + 1)
    with jax.named_scope("w_pt1"):
        settle(points.at[s, pl.ds(0, patches - 1)], point_sem.at[1])
    for j in range(1, slabs):
        point_second(j).start()
    with jax.named_scope("place"):
        stack = rim[...]
        placed_v = dot_nt(words, stack)
        placed_r = dot_nt(rest, stack)

        def rim_row(base, at, ok):
            return jnp.where(ok, rim[base + at : base + at + 1, :wide_lanes].astype(F32), 0.0)

        def framed(middle, before, after):
            before, after = pltpu.roll(before, ey, 1), pltpu.roll(after, ey, 1)
            return jnp.where(low_half, middle, jnp.where(tail_half, after, before))

        w_rows = {}
        for i in range(ex):
            w_rows[i] = framed(
                w_own[i : i + 1],
                rim_row(side_base[0], i, has_prev_p),
                rim_row(side_base[1], side_w + i, has_next_p),
            )
        w_tips = [
            (
                rim_row(tip_base[n][0], 5, jnp.logical_and(from_s[n], has_prev_p)),
                rim_row(tip_base[n][1], 0, jnp.logical_and(from_s[n], has_next_p)),
            )
            for n in range(2)
        ]
        edges_v, edges_r = {}, {}
        for i in range(ex):
            edges_v[i] = framing(placed_v, SWEEPS * i, masks[None, SWEEPS])
            edges_r[i] = framing(placed_r, SWEEPS * ex + (SWEEPS - 1) * i, masks[None, SWEEPS - 1])
        for n in range(2):
            r1, r2 = (-1, -2) if n == 0 else (ex, ex + 1)
            base = tip_base[n][1]
            used = join(placed_v[:DEEP], placed_v[2 * DEEP : 5 * DEEP])
            edges_v[r1] = framing(used, base + 2, masks[n, 2])
            edges_v[r2] = framing(used, base + 4, masks[n, 1])
            edges_r[r1] = framing(placed_r[:DEEP], base + 5, masks[n, 1])

    with jax.named_scope("w_near"):
        for n in range(2):
            pl.when(from_far[n])(lambda: far_copy(n).wait_recv())
            pl.when(from_s[n])(lambda: near_copy(n).wait_recv())

    with jax.named_scope("stencil"):
        by_d, by_x, by_y, by_r2, by_r1, by_r0 = {}, {}, {}, {}, {}, {}
        for i, (v_half, r_half) in enumerate(own_rows):
            full, side = v_half + edges_v[i], r_half + edges_r[i]
            by_d[i], by_x[i], by_y[i] = (full[k * 2 * DEEP : (k + 1) * 2 * DEEP] for k in range(3))
            by_r2[i], by_r1[i], by_r0[i] = (
                side[: 2 * DEEP], side[2 * DEEP : 2 * DEEP + 3 * comps], side[3 * DEEP : 3 * DEEP + comps]
            )
        for n in range(2):
            got = jnp.where(from_s[n], near_in[n].astype(F32), 0.0)
            for i, half in enumerate(halves(got)):
                r = i - ex if n == 0 else i + ex
                edge = edges_v[r]
                by_d[r] = half[0:DEEP] + edge[0:DEEP]
                by_x[r] = half[DEEP : 3 * DEEP] + edge[DEEP : 3 * DEEP]
                by_y[r] = half[3 * DEEP : 4 * DEEP] + edge[3 * DEEP : 4 * DEEP]
                by_r2[r] = half[4 * DEEP : 5 * DEEP]
                if r in edges_r:
                    by_r2[r] = by_r2[r] + edges_r[r]
                by_r1[r] = half[3 * DEEP - comps - 1 : 3 * DEEP - 1]
                w_rows[r] = half[3 * DEEP - 1 : 3 * DEEP]
                if r in (-1, ex):
                    w_rows[r] = framed(w_rows[r], *w_tips[n])
            beyond = halves(jnp.where(from_far[n], far_in[n].astype(F32), 0.0))[1 - n]
            by_x[-ex - 1 if n == 0 else 2 * ex] = join(beyond, blank(DEEP - 8, wide_lanes))

        def turn(x):
            return pltpu.roll(x, 1, 1) + pltpu.roll(x, wide_lanes - 1, 1)

        one = {}
        for r in span_rows:
            n = 2 * DEEP if 0 <= r < ex else DEEP
            one[r] = by_d[r] + w_rows[r] * (by_x[r - 1][:n] + by_x[r + 1][:n] + turn(by_y[r]) + by_r2[r])
        two = {}
        for r in range(-1, ex + 1):
            if 0 <= r < ex:
                d_part = join(one[r][:comps], one[r][DEEP : DEEP + 2 * comps])
                y_part = join(one[r][4 * comps : 5 * comps], one[r][DEEP + 2 * comps : DEEP + 4 * comps])
                n = 3 * comps
            else:
                d_part, y_part = one[r][:comps], one[r][4 * comps : 5 * comps]
                n = comps
            x_part = one[r - 1][comps : comps + n] + one[r + 1][comps : comps + n]
            two[r] = d_part + w_rows[r] * (x_part + turn(y_part) + by_r1[r])
        drawn = []
        for r in range(ex):
            x_part = two[r - 1][:comps] + two[r + 1][:comps]
            drawn.append(
                two[r][comps : 2 * comps]
                + w_rows[r] * (x_part + turn(two[r][2 * comps : 3 * comps]) + by_r0[r])
            )
        tractions = [jnp.where(low_half, x, 0.0).astype(BF16) for x in drawn]
        for owner in range(patches):
            pull_out[owner] = sum(dot(tractions[i], onehot_elem[owner, i]) for i in range(ex)).astype(BF16)
    with jax.named_scope("s_pull"):
        for j in sorted(range(slabs), key=lambda j: -min(j, slabs - j)):
            for i in range(patches):
                if (j, i) != (0, 0):
                    pull_copy(j, i).start()
    for owner in range(patches):

        @pl.when(p == owner)
        def _():
            pulls[s, :, owner * cap : (owner + 1) * cap] = pull_out[owner]


    def sweep(k, v):
        rounded = vb[k]
        wide = rounded.astype(F32)
        with jax.named_scope("w_halo"):
            if k > 0:
                pl.when(has_prev_p)(lambda: y_up(k).wait_recv())
                pl.when(has_next_p)(lambda: y_down(k).wait_recv())
            pl.when(has_prev_s)(lambda: x_up(k).wait_recv())
            pl.when(has_next_s)(lambda: x_down(k).wait_recv())
        line = lax.broadcasted_iota(jnp.int32, (ey, dof), 0)
        along_y = []
        for i in range(ex):
            if k == 0:
                at = shift + side_v + SWEEPS * (i + 1) - 1
                before = rim[at : at + 1].astype(F32)
                after = rim[SWEEPS * i : SWEEPS * i + 1].astype(F32)
            else:
                before = halo_y[k, 0, i].astype(F32)[PACK - 1 : PACK]
                after = halo_y[k, 1, i].astype(F32)[0:1]
            before = jnp.where(has_prev_p, before, 0.0)
            after = jnp.where(has_next_p, after, 0.0)
            prev = jnp.where(line == 0, jnp.broadcast_to(before, (ey, dof)), pltpu.roll(wide[i], 1, 0))
            following = jnp.where(line == ey - 1, jnp.broadcast_to(after, (ey, dof)), pltpu.roll(wide[i], ey - 1, 0))
            along_y.append((prev + following).astype(BF16))
        side_y = dot(jnp.concatenate(along_y, axis=0), cy_ref[...])
        low = jnp.where(has_prev_s, halo_x[k, 0].astype(F32), 0.0)
        high = jnp.where(has_next_s, halo_x[k, 1].astype(F32), 0.0)
        along_x = []
        for i in range(ex):
            below = low if i == 0 else wide[i - 1]
            above = high if i == ex - 1 else wide[i + 1]
            along_x.append((below + above).astype(BF16))
        side_x = dot(jnp.concatenate(along_x, axis=0), cx_ref[...])
        side = (side_x + side_y).reshape(ex, ey, dof)
        residue = jnp.concatenate([(base_buf[i] + side[i]).astype(BF16) for i in range(ex)], axis=0)
        update = dot(residue, inverse_ref[...]).reshape(ex, ey, dof)
        return [v[i] + update[i] * inverses[i] for i in range(ex)]

    def keep(v, k):
        for i in range(ex):
            fluid_ref[i] = v[i]
            if k < SWEEPS:
                vb[k, i] = v[i].astype(BF16)

    with jax.named_scope("sweep0"):
        keep(sweep(0, state_ref), 1)
        send_halos(1)
        prelude(1)

    def scatter(slab, acc):
        hot = onehot_row[slab]
        value = pulls[slab]
        scaled = jnp.concatenate([hot * value[c : c + 1] for c in range(comps)], axis=0)
        return acc + dot_nt(scaled, onehot_col[slab])

    inner = jnp.minimum(s, slabs - 1 - s)

    def nearest(t):
        step = lax.div(t + 1, 2)
        alternate = jnp.where(lax.rem(t, 2) == 1, s + step, s - step)
        return jnp.where(t <= 2 * inner, alternate, jnp.where(s < slabs - 1 - s, t, slabs - 1 - t))

    def prepared(t, carry):
        slab = nearest(t)
        with jax.named_scope("w_point"):
            settle(points.at[slab], rp2.at[slab])
        build_points(slab)
        return carry

    def gathered(t, acc):
        slab = nearest(t)
        with jax.named_scope("w_pull"):
            settle(pulls.at[slab], rq.at[slab])
        return scatter(slab, acc)

    half = (slabs + 1) // 2
    build_points(s)
    with jax.named_scope("shell"):
        shell()
    with jax.named_scope("build1"):
        lax.fori_loop(1, half, prepared, 0)
    with jax.named_scope("w_own"):
        settle(pulls.at[s, :, pl.ds(0, (patches - 1) * cap)], rq.at[s])
    acc = scatter(s, jnp.zeros((comps * rows, cols), F32))
    with jax.named_scope("gather1"):
        acc = lax.fori_loop(1, half, gathered, acc)
    with jax.named_scope("sweep1"):
        keep(sweep(1, fluid_ref), 2)
        send_halos(2)
    with jax.named_scope("build2"):
        lax.fori_loop(half, slabs, prepared, 0)
    with jax.named_scope("gather2"):
        acc = lax.fori_loop(half, slabs, gathered, acc)
    loads = acc.reshape(comps, rows, cols)
    fresh = [rest_buf[c] + loads[c] * gain_buf[...] for c in range(comps)]
    narrow = jnp.concatenate([x.astype(BF16) for x in fresh], axis=0)
    for k in range(patches):
        span = pl.ds(k * cap, cap)
        spread = dot(narrow, onehot_col[s, :, span]).reshape(comps, rows, cap)
        hot = onehot_row[s, :, span].astype(F32)
        for c in range(comps):
            picks_out[k, c : c + 1] = jnp.sum(spread[c] * hot, axis=0, keepdims=True).astype(BF16)
    with jax.named_scope("s_pick"):
        for j in range(1, patches):
            pick_copy(j).start()
    picks_in[p] = picks_out[p]
    for c in range(comps):
        net_ref[c] = fresh[c]
    with jax.named_scope("sweep2"):
        prelude(2)
        keep(sweep(2, fluid_ref), SWEEPS)
    with jax.named_scope("w_pick"):
        settle(picks_in.at[pl.ds(0, patches - 1)], pick_sem.at[1])
    for k in range(patches):
        live = lives(k)
        for c in range(comps):
            wall_ref[c, 0, :, k * cap : (k + 1) * cap] = jnp.where(live, picks_in[k, c : c + 1].astype(F32), 0.0)

    with jax.named_scope("drain"):
        halo_sends(SWEEPS - 1, lambda copy: copy.wait_send())
        pl.when(has_next_p)(lambda: d_up().wait_send())
        pl.when(has_prev_p)(lambda: d_down().wait_send())
        for n, m in corners:
            pl.when(jnp.logical_and(to_s[n], to_p[m]))(lambda: tip_copy(n, m).wait_send())
        settle(points.at[s, pl.ds(0, patches - 1)], point_sem.at[0])
        settle(points.at[pl.ds(0, slabs - 1)], point_sem.at[2])
        settle(pulls.at[pl.ds(0, slabs - 1)], pull_sem.at[0])
        settle(pulls.at[s, :, pl.ds(0, (patches - 1) * cap)], pull_sem.at[1])
        settle(picks_in.at[pl.ds(0, patches - 1)], pick_sem.at[0])


def deliver(*refs):
    copies = [pltpu.make_async_copy(refs[n], refs[n + 3], refs[6].at[n]) for n in range(3)]
    for copy in copies:
        copy.start()
    for copy in copies:
        copy.wait()


def shards(slabs, patches, *args):
    state, disp, elem = args[0], args[11], args[8]
    ex, ey, dof = state.shape
    comps, rows, cols = disp.shape
    cap = elem.shape[2] // patches
    sem = pltpu.SemaphoreType.DMA
    vmem = pl.BlockSpec(memory_space=pltpu.VMEM)
    hot_bytes = slabs * patches * cap * (rows + cols) * 2
    outs = pl.pallas_call(
        functools.partial(kernel, slabs, patches, len(args)),
        out_shape=(
            pltpu.VMEM(state.shape, F32),
            pltpu.VMEM(disp.shape, F32),
            pltpu.VMEM((comps, 1, 1, elem.shape[2]), F32),
        ),
        in_specs=[pl.BlockSpec(memory_space=pltpu.HBM)] * len(args),
        out_specs=(vmem, vmem, vmem),
        scratch_shapes=[pltpu.VMEM(x.shape, x.dtype) for x in args[:3]]
        + [
            pltpu.VMEM((3,) + args[3].shape, BF16),
            pltpu.VMEM(args[7].shape, BF16),
            pltpu.VMEM((2,) + elem.shape, jnp.int32),
            pltpu.VMEM(args[10].shape, jnp.int32),
            pltpu.VMEM((comps + 1, rows, cols), F32),
            pltpu.VMEM(args[6].shape, BF16),
            pltpu.VMEM((SWEEPS, ex, ey, dof), BF16),
            pltpu.VMEM((SWEEPS, 2, ey, dof), BF16),
            pltpu.VMEM((SWEEPS, 2, ex, PACK, dof), BF16),
            pltpu.VMEM((2, comps, EDGE, cols), F32),
            pltpu.VMEM((slabs, patches, 1, cap), jnp.int32),
            pltpu.VMEM((slabs, comps, patches * cap), BF16),
            pltpu.VMEM((patches, comps, cap), BF16),
            pltpu.VMEM((patches, comps, cap), BF16),
            pltpu.VMEM((patches, comps, cap), BF16),
            pltpu.VMEM((patches, ex, ex * ey, cap), BF16),
            pltpu.VMEM((slabs, rows, patches * cap), BF16),
            pltpu.VMEM((slabs, cols, patches * cap), BF16),
            pltpu.VMEM((comps, rows, cols), F32),
            pltpu.VMEM((rows, cols), F32),
            pltpu.VMEM(state.shape, F32),
            pltpu.VMEM((5 * DEEP, ex * ey), BF16),
            pltpu.VMEM((2, 5 * DEEP, ex * ey), BF16),
            pltpu.VMEM((8, ex * ey), BF16),
            pltpu.VMEM((2, 8, ex * ey), BF16),
            pltpu.VMEM((2, DEEP, dof), BF16),
            pltpu.VMEM((4, TIP, dof), BF16),
            pltpu.VMEM((ex * ey, dof), BF16),
            sem((9,)),
            sem((2, 2)),
            sem((2, 2)),
            sem((2,)),
            sem((3,)),
            sem((slabs,)),
            sem((2,)),
            sem((slabs,)),
            sem((2,)),
            sem((2,)),
            sem((2,)),
            sem((2,)),
            sem((2,)),
            sem((4,)),
            pltpu.SemaphoreType.REGULAR((max(slabs.bit_length() - 2, 1),)),
        ],
        compiler_params=pltpu.CompilerParams(collective_id=0, has_side_effects=True),
    )(*args)
    return pl.pallas_call(
        deliver,
        out_shape=tuple(jax.ShapeDtypeStruct(x.shape, x.dtype) for x in outs),
        in_specs=[vmem] * 3,
        out_specs=(pl.BlockSpec(memory_space=pltpu.HBM),) * 3,
        scratch_shapes=[sem((3,))],
    )(*[pltpu.with_memory_space_constraint(x, pltpu.VMEM) for x in outs])


def solution(mesh):
    return jax.shard_map(
        functools.partial(shards, mesh.shape["slab"], mesh.shape["patch"]),
        mesh=mesh,
        in_specs=(
            P("slab", "patch", None),
            P("slab", "patch", None),
            P("slab", "patch"),
            P(),
            P(),
            P(),
            P(),
            P(),
            P("slab", "patch", None),
            P("slab", "patch", None),
            P("slab", "patch", None),
            P(None, "patch", None),
            P("patch", None),
        ),
        out_specs=(
            P("slab", "patch", None),
            P(None, "patch", None),
            P(None, "slab", "patch", None),
        ),
        check_vma=False,
    )
```

```python
import functools

import jax
import jax.numpy as jnp
from jax import lax
from jax.experimental import pallas as pl
from jax.experimental.pallas import tpu as pltpu
from jax.sharding import PartitionSpec as P

SWEEPS = 3
PACK = 16
EDGE = 8
SPARE = 8 * 2**20
DEEP = 16
TIP = 8
LOAD_ORDER = (7, 6, 3, 4, 5, 0, 1, 2, 9, 8, 10, 11, 12)
MESH = pl.DeviceIdType.MESH
F32 = jnp.float32
BF16 = jnp.bfloat16


def dot(a, b):
    return jnp.dot(a, b, preferred_element_type=F32)


def dot_nt(a, b):
    return lax.dot_general(a, b, (((1,), (1,)), ((), ())), preferred_element_type=F32)


def split_point(point, cols):
    if cols & (cols - 1) == 0:
        return lax.shift_right_logical(point, cols.bit_length() - 1), point & (cols - 1)
    row = lax.div(point, cols)
    return row, point - row * cols


def column(row_vector):
    n = row_vector.shape[1]
    shape = (n, n)
    eye = lax.broadcasted_iota(jnp.int32, shape, 0) == lax.broadcasted_iota(jnp.int32, shape, 1)
    return jnp.sum(jnp.where(eye, jnp.broadcast_to(row_vector, shape), 0.0), axis=1, keepdims=True)


def laplace(x):
    rows, cols = x.shape
    lane = lax.broadcasted_iota(jnp.int32, x.shape, 1)
    left = jnp.where(lane == 0, 0.0, pltpu.roll(x, 1, 1))
    right = jnp.where(lane == cols - 1, 0.0, pltpu.roll(x, cols - 1, 1))
    return 4.0 * x - (pltpu.roll(x, 1, 0) + pltpu.roll(x, rows - 1, 0) + left + right)


def join(*parts):
    return jnp.concatenate(parts, axis=0)


def blank(rows, cols):
    return jnp.zeros((rows, cols), F32)


def first_words(base0, traction, matrix, couple_x, couple_y):
    low = base0.astype(BF16)
    return join(dot_nt(low, couple_x), traction.astype(F32) - dot_nt(low, matrix), dot_nt(low, couple_y))


def second_words(base1, one, comps, matrix, couple_x, couple_y):
    low = base1.astype(BF16)
    by_x, by_y = dot_nt(low, couple_x), dot_nt(low, couple_y)
    by_d = one - dot_nt(low, matrix)
    dof = one.shape[1]
    return join(
        by_d[:comps], by_x, by_y[:comps], blank(DEEP - 5 * comps, dof),
        by_d[comps:], by_y[comps:], blank(DEEP - 4 * comps, dof),
    )


def third_words(base2, two, matrix, couple_x, couple_y):
    low = base2.astype(BF16)
    return join(two - dot_nt(low, matrix), dot_nt(low, couple_x), dot_nt(low, couple_y)).astype(BF16)


def stacked(two, one, none):
    comps, dof = none.shape
    return join(two, one, blank(DEEP - 3 * comps, dof), none, blank(DEEP - comps, dof)).astype(BF16)


def kernel(slabs, patches, args, *refs):
    hbm, refs = refs[:args], refs[args:]
    (fluid_ref, net_ref, wall_ref), refs = refs[:3], refs[3:]
    (state_ref, rhs_ref, scale_ref, matrices, traction_ref, slots, count_ref, nets, inverse_ref) = refs[:9]
    refs = refs[9:]
    cx_ref, cy_ref, matrix_ref = (matrices.at[n] for n in range(3))
    elem_ref, point_ref = slots.at[0], slots.at[1]
    (vb, halo_x, halo_y, halo_d, points, pulls, pull_out, picks_out, picks_in) = refs[:9]
    (onehot_elem, onehot_row, onehot_col, rest_buf, gain_buf, base_buf) = refs[9:15]
    (near_out, near_in, far_out, far_in, side_out, tip_out, rim) = refs[15:22]
    (load_sem, rx, ry, rd, point_sem, rp2, pull_sem, rq, pick_sem) = refs[22:31]
    (r_near, s_far, r_far, r_side, r_tip, near_sem) = refs[31:]
    s_near, s_side, s_tip = load_sem.at[pl.ds(0, 2)], load_sem.at[pl.ds(2, 2)], load_sem.at[pl.ds(4, 4)]
    sx, sy, sd = s_near, s_side, s_far
    comps = nets.shape[0] - 1
    disp_ref, stiff_ref = nets.at[pl.ds(0, comps)], nets.at[comps]
    homes = (
        (state_ref, 0), (rhs_ref, 1), (scale_ref, 2), (matrix_ref, 3), (cx_ref, 3), (cy_ref, 3), (inverse_ref, 8),
        (traction_ref, 4), (elem_ref, 5), (point_ref, 5), (count_ref, 6), (disp_ref, 7), (stiff_ref, 7),
    )

    loads_in = [pltpu.make_async_copy(hbm[n], homes[n][0], load_sem.at[homes[n][1]]) for n in range(args)]
    for n in LOAD_ORDER:
        loads_in[n].start()
    groups = (state_ref, rhs_ref, scale_ref, matrices, traction_ref, slots, count_ref, nets, inverse_ref)

    def ready(*names):
        for n in names:
            pltpu.make_async_copy(groups[n], groups[n], load_sem.at[n]).wait()

    s = lax.axis_index("slab")
    p = lax.axis_index("patch")
    ex, ey, dof = state_ref.shape
    rows, cols = stiff_ref.shape
    cap = elem_ref.shape[2] // patches
    wide_lanes = ex * ey

    def slab_peer(j):
        return lax.rem(s + j, slabs)

    def patch_peer(j):
        return lax.rem(p + j, patches)

    def slab_sides(reach, semaphore):
        @pl.when(s >= reach)
        def _():
            pl.semaphore_signal(semaphore, inc=1, device_id=(s - reach, p), device_id_type=MESH)

        @pl.when(s + reach < slabs)
        def _():
            pl.semaphore_signal(semaphore, inc=1, device_id=(s + reach, p), device_id_type=MESH)

    def slab_count(reach):
        return jnp.where(s >= reach, 1, 0) + jnp.where(s + reach < slabs, 1, 0)

    reaches = []
    while 2 ** (len(reaches) + 1) < slabs - 1:
        reaches.append(2 ** (len(reaches) + 1))

    def near_signal(n):
        slab_sides(reaches[n], near_sem.at[n])

    def near_wait(n):
        pl.semaphore_wait(near_sem.at[n], slab_count(reaches[n]))

    has_prev_s, has_next_s = s > 0, s < slabs - 1
    has_prev_p, has_next_p = p > 0, p < patches - 1
    has_far_prev, has_far_next = s > 1, s < slabs - 2

    barrier = pltpu.get_barrier_semaphore()
    for j in range(1, patches):
        pl.semaphore_signal(barrier, inc=1, device_id=(s, patch_peer(j)), device_id_type=MESH)
    for reach in (1, 2):

        @pl.when(s >= reach)
        def _():
            for j in range(patches):
                pl.semaphore_signal(barrier, inc=1, device_id=(s - reach, patch_peer(j)), device_id_type=MESH)

        @pl.when(s + reach < slabs)
        def _():
            for j in range(patches):
                pl.semaphore_signal(barrier, inc=1, device_id=(s + reach, patch_peer(j)), device_id_type=MESH)

    awaited = patches - 1 + patches * (slab_count(1) + slab_count(2))

    def remote(src, dst, send, recv, target):
        return pltpu.make_async_remote_copy(
            src_ref=src, dst_ref=dst, send_sem=send, recv_sem=recv, device_id=target, device_id_type=MESH
        )

    def slab_at(step):
        return jnp.clip(s + step, 0, slabs - 1)

    def patch_at(step):
        return jnp.clip(p + step, 0, patches - 1)

    def x_up(k):
        return remote(vb.at[k, ex - 1], halo_x.at[k, 0], sx.at[0], rx.at[k % 2, 0], (slab_at(1), p))

    def x_down(k):
        return remote(vb.at[k, 0], halo_x.at[k, 1], sx.at[1], rx.at[k % 2, 1], (slab_at(-1), p))

    def y_up(k):
        return remote(
            vb.at[k, :, pl.ds(ey - PACK, PACK)], halo_y.at[k, 0], sy.at[0], ry.at[k % 2, 0], (s, patch_at(1))
        )

    def y_down(k):
        return remote(vb.at[k, :, pl.ds(0, PACK)], halo_y.at[k, 1], sy.at[1], ry.at[k % 2, 1], (s, patch_at(-1)))

    def d_up():
        return remote(disp_ref.at[:, pl.ds(rows - EDGE, EDGE)], halo_d.at[0], sd.at[0], rd.at[0], (s, patch_at(1)))

    def d_down():
        return remote(disp_ref.at[:, pl.ds(0, EDGE)], halo_d.at[1], sd.at[1], rd.at[1], (s, patch_at(-1)))

    shift = ey - TIP
    side_base = (shift, 0)
    tip_base = [(DEEP + TIP * n + ey, DEEP + TIP * n) for n in range(2)]

    side_w = ex * (2 * SWEEPS - 1)
    side_v = SWEEPS + 2

    def near_copy(n):
        return remote(near_out, near_in.at[n], s_near.at[n], r_near.at[n], (slab_at(1 - 2 * n), p))

    def far_copy(n):
        return remote(far_out, far_in.at[n], s_far.at[n], r_far.at[n], (slab_at(2 - 4 * n), p))

    def side_copy(n):
        return remote(side_out.at[n], rim.at[pl.ds(side_base[n], DEEP)], s_side.at[n], r_side.at[n], (s, patch_at(1 - 2 * n)))

    def tip_copy(n, m):
        q = 2 * n + m
        return remote(tip_out.at[q], rim.at[pl.ds(tip_base[n][m], TIP)], s_tip.at[q], r_tip.at[q], (slab_at(1 - 2 * n), patch_at(1 - 2 * m)))

    to_s, from_s = (has_next_s, has_prev_s), (has_prev_s, has_next_s)
    to_p, from_p = (has_next_p, has_prev_p), (has_prev_p, has_next_p)
    to_far, from_far = (has_far_next, has_far_prev), (has_far_prev, has_far_next)
    corners = [(n, m) for n in range(2) for m in range(2)]
    def point_first(j):
        peer = patch_peer(j)
        src = point_ref.at[0, :, pl.ds(pl.multiple_of(peer * cap, cap), cap)]
        return remote(src, points.at[s, p], point_sem.at[0], point_sem.at[1], (s, peer))

    def point_second(j):
        return remote(points.at[s], points.at[s], point_sem.at[2], rp2.at[s], (slab_peer(j), p))

    def pull_copy(j, i):
        to = (slab_peer(j), patch_peer(i))
        here = pl.ds(pl.multiple_of(p * cap, cap), cap)
        return remote(pull_out.at[to[1]], pulls.at[s, :, here], pull_sem.at[0 if j else 1], rq.at[s], to)

    def pick_copy(j):
        peer = patch_peer(j)
        return remote(picks_out.at[peer], picks_in.at[p], pick_sem.at[0], pick_sem.at[1], (s, peer))

    def settle(ref, semaphore):
        pltpu.make_async_copy(ref, ref, semaphore).wait()

    def halo_sends(k, act):
        pl.when(has_next_s)(lambda: act(x_up(k)))
        pl.when(has_prev_s)(lambda: act(x_down(k)))
        if k > 0:
            pl.when(has_next_p)(lambda: act(y_up(k)))
            pl.when(has_prev_p)(lambda: act(y_down(k)))

    def send_halos(k):
        if k == 0:
            for n in range(2):
                pl.when(to_s[n])(lambda: near_copy(n).wait_send())
        else:
            halo_sends(k - 1, lambda copy: copy.wait_send())
        if k == 1:
            for n in range(2):
                pl.when(to_p[n])(lambda: side_copy(n).wait_send())
        halo_sends(k, lambda copy: copy.start())

    def build_points(slab):
        for k in range(patches):
            row, col = split_point(points[slab, k], cols)
            span = pl.ds(k * cap, cap)
            onehot_row[slab, :, span] = jnp.where(
                lax.broadcasted_iota(jnp.int32, (rows, cap), 0) == row, 1.0, 0.0
            ).astype(BF16)
            onehot_col[slab, :, span] = jnp.where(
                lax.broadcasted_iota(jnp.int32, (cols, cap), 0) == col, 1.0, 0.0
            ).astype(BF16)

    def lives(k):
        lane = lax.broadcasted_iota(jnp.int32, (1, cap), 1)
        return lane < count_ref[0, :, k : k + 1]

    def shell():
        pl.when(has_prev_p)(lambda: d_up().wait_recv())
        pl.when(has_next_p)(lambda: d_down().wait_recv())
        total = rows + 2 * EDGE
        line = lax.broadcasted_iota(jnp.int32, (total, cols), 0)
        first = jnp.where(has_prev_p, 0, EDGE)
        last = jnp.where(has_next_p, total, EDGE + rows)
        valid = (line >= first) & (line < last)
        gain = 1.0 / (36.0 * stiff_ref[...])
        gain_buf[...] = gain
        for c in range(comps):
            field = jnp.concatenate([halo_d[0, c], disp_ref[c], halo_d[1, c]], axis=0)
            field = jnp.where(valid, field, 0.0)
            bend = jnp.where(valid, laplace(field), 0.0)
            full = (laplace(bend) + 4.0 * bend)[EDGE : EDGE + rows]
            rest_buf[c] = disp_ref[c] - stiff_ref[...] * full * gain

    with jax.named_scope("w_mat"):
        ready(4, 8)
        base0 = dot_nt(traction_ref[...], inverse_ref[...])
        ready(3)
    couples = (matrix_ref[...], cx_ref[...], cy_ref[...])
    with jax.named_scope("words"):
        one = first_words(base0, traction_ref[...], *couples)
        base1 = dot_nt(one.astype(BF16), inverse_ref[...])
    with jax.named_scope("w_state"):
        ready(0, 1, 2)
    rounded0 = state_ref[...].astype(BF16)
    vb[0] = rounded0
    wet = rhs_ref[...].astype(BF16)
    flat = 1.0 / scale_ref[...]
    w_own = jnp.concatenate([flat, blank(ex, wide_lanes - ey)], axis=1)
    lane = lax.broadcasted_iota(jnp.int32, (1, wide_lanes), 1)
    low_half = lane < ey
    tail_half = lane < ey + ey // 2
    w_lines = jnp.concatenate([w_own] + [blank(ex, wide_lanes)] * (dof // wide_lanes - 1), axis=1)
    with jax.named_scope("project"):
        two = second_words(base1, one, comps, *couples)
        flow = rounded0.reshape(wide_lanes, dof)
        passed = join(*[dot(flow, couple) for couple in couples]).astype(BF16)
        mapped = dot(join(passed, wet.reshape(wide_lanes, dof)), inverse_ref[...])
        turned = join(flow.astype(F32) - mapped[:wide_lanes], mapped[wide_lanes:]).astype(BF16)
        both = dot_nt(stacked(two, one, traction_ref[...].astype(F32)), turned)
        own_v = join(*[both[: 2 * DEEP, n * wide_lanes : (n + 1) * wide_lanes] for n in range(3)])
        own_r = both[:, 3 * wide_lanes :]
        packed = jnp.where(low_half, w_own[0:1], pltpu.roll(w_own[1:2], ey, 1))
        spare = join(
            blank(2 * DEEP - comps - 1, wide_lanes), own_r[2 * DEEP : 2 * DEEP + comps], packed
        )
        near_out[...] = join(
            own_v[0:DEEP], own_v[2 * DEEP : 4 * DEEP] + spare, own_v[4 * DEEP : 5 * DEEP], own_r[0:DEEP]
        ).astype(BF16)
        far_out[...] = own_v[2 * DEEP : 2 * DEEP + 8].astype(BF16)

        def state_at(i, c):
            return state_ref[i, c : c + 1]

        def rhs_at(i, c):
            return rhs_ref[i, c : c + 1]

        for m in range(2):
            close = [ey - 1 - j if m == 0 else j for j in range(SWEEPS)]
            if m == 1:
                side = [state_at(i, c) for i in range(ex) for c in close]
                side += [rhs_at(i, c) for i in range(ex) for c in close[: SWEEPS - 1]]
                side += [w_lines, blank(DEEP - side_w - ex, dof)]
            else:
                side = [w_lines, blank(side_v - ex, dof)]
                side += [state_at(i, c) for i in range(ex) for c in close[::-1]]
                side += [blank(1, dof)]
                side += [rhs_at(i, c) for i in range(ex) for c in close[: SWEEPS - 1][::-1]]
            side_out[m] = join(*side).astype(BF16)
            for n in range(2):
                r1, r2 = (ex - 1, ex - 2) if n == 0 else (0, 1)
                near2 = [state_at(r1, close[0]), state_at(r1, close[1])]
                last = [state_at(r2, close[0]), rhs_at(r1, close[0])]
                weigh = w_lines[r1 : r1 + 1]
                if m == 1:
                    tip = [weigh, blank(1, dof), *near2, *last, blank(TIP - 6, dof)]
                else:
                    tip = [*near2[::-1], blank(1, dof), *last, weigh, blank(TIP - 6, dof)]
                tip_out[2 * n + m] = join(*tip).astype(BF16)

    ready(5, 6, 7)
    with jax.named_scope("w_barrier"):
        pl.semaphore_wait(barrier, awaited)
    for n, m in corners:
        pl.when(jnp.logical_and(to_s[n], to_p[m]))(lambda: tip_copy(n, m).start())
    for n in range(2):
        pl.when(to_s[n])(lambda: near_copy(n).start())
    for m in range(2):
        pl.when(to_p[m])(lambda: side_copy(m).start())
    for n in range(2):
        pl.when(to_far[n])(lambda: far_copy(n).start())
    if reaches:
        near_signal(0)
    for j in range(1, patches):
        point_first(j).start()
    for owner in range(patches):

        @pl.when(p == owner)
        def _():
            points[s, owner] = point_ref[0, :, owner * cap : (owner + 1) * cap]

    for owner in range(patches):
        elem = elem_ref[0, :, owner * cap : (owner + 1) * cap]
        for i in range(ex):
            line = lax.broadcasted_iota(jnp.int32, (wide_lanes, cap), 0)
            hit = (line + i * ey == elem) & (line < ey) & lives(owner)
            onehot_elem[owner, i] = jnp.where(hit, 1.0, 0.0).astype(BF16)
    if reaches:
        with jax.named_scope("w_reach"):
            near_wait(0)
        if len(reaches) > 1:
            near_signal(1)
    send_halos(0)
    scales = [column(scale_ref[i : i + 1, :]) for i in range(ex)]
    inverses = [1.0 / x for x in scales]

    def prelude(k):
        own = dot(vb[k].reshape(ex * ey, dof), matrix_ref[...]).reshape(ex, ey, dof)
        for i in range(ex):
            base_buf[i] = rhs_ref[i] - scales[i] * own[i]

    for n in range(2):
        pl.when(to_far[n])(lambda: far_copy(n).wait_send())
    pl.when(has_next_p)(lambda: d_up().start())
    pl.when(has_prev_p)(lambda: d_down().start())
    with jax.named_scope("late_words"):
        base2 = dot_nt(two.astype(BF16), inverse_ref[...])
        words = third_words(base2, two, matrix_ref[...], cx_ref[...], cy_ref[...])
        rest = stacked(base2, base1, base0)
    with jax.named_scope("prelude"):
        prelude(0)

    def halves(x):
        return jnp.where(low_half, x, 0.0), jnp.where(low_half, pltpu.roll(x, ey, 1), 0.0)

    span_rows = list(range(-ex, 2 * ex))

    def between(low, high):
        return (lane >= low) & (lane < high)

    def frame_mask(n, reach):
        right, left = has_next_p, has_prev_p
        if n is not None:
            right, left = jnp.logical_and(right, from_s[n]), jnp.logical_and(left, from_s[n])
        right, left = jnp.where(right, 1, 0), jnp.where(left, 1, 0)
        ahead, behind = between(ey, ey + reach), between(wide_lanes - reach, wide_lanes)
        return jnp.where(ahead, right, jnp.where(behind, left, 0)) > 0

    masks = {(n, reach): frame_mask(n, reach) for n in (None, 0, 1) for reach in range(1, SWEEPS + 1)}

    def framing(x, source, mask):
        return jnp.where(mask, pltpu.roll(x, (ey - source) % wide_lanes, 1), 0.0)

    with jax.named_scope("halves"):
        own_rows = list(zip(halves(own_v), halves(own_r)))
    with jax.named_scope("w_side"):
        for m in range(2):
            pl.when(from_p[m])(lambda: side_copy(m).wait_recv())
        for n, m in corners:
            pl.when(jnp.logical_and(from_s[n], from_p[m]))(lambda: tip_copy(n, m).wait_recv())
    early = s < slabs // 2
    known = 4

    def far_off(j):
        peer = slab_peer(j)
        return jnp.maximum(peer - s, s - peer) > known

    def learn_all():
        for n in range(1, len(reaches)):
            with jax.named_scope("w_reach"):
                near_wait(n)
            if n + 1 < len(reaches):
                near_signal(n + 1)

    with jax.named_scope("w_pt1"):
        settle(points.at[s, pl.ds(0, patches - 1)], point_sem.at[1])

    @pl.when(early)
    def _():
        for j in range(1, slabs):
            pl.when(jnp.logical_not(far_off(j)))(lambda: point_second(j).start())

    @pl.when(jnp.logical_not(early))
    def _():
        learn_all()
        for j in range(1, slabs):
            point_second(j).start()

    with jax.named_scope("place"):
        stack = rim[...]
        placed_v = dot_nt(words, stack)
        placed_r = dot_nt(rest, stack)

        def rim_row(base, at, ok):
            return jnp.where(ok, rim[base + at : base + at + 1, :wide_lanes].astype(F32), 0.0)

        def framed(middle, before, after):
            before, after = pltpu.roll(before, ey, 1), pltpu.roll(after, ey, 1)
            return jnp.where(low_half, middle, jnp.where(tail_half, after, before))

        w_rows = {}
        for i in range(ex):
            w_rows[i] = framed(
                w_own[i : i + 1],
                rim_row(side_base[0], i, has_prev_p),
                rim_row(side_base[1], side_w + i, has_next_p),
            )
        w_tips = [
            (
                rim_row(tip_base[n][0], 5, jnp.logical_and(from_s[n], has_prev_p)),
                rim_row(tip_base[n][1], 0, jnp.logical_and(from_s[n], has_next_p)),
            )
            for n in range(2)
        ]
        edges_v, edges_r = {}, {}
        for i in range(ex):
            edges_v[i] = framing(placed_v, SWEEPS * i, masks[None, SWEEPS])
            edges_r[i] = framing(placed_r, SWEEPS * ex + (SWEEPS - 1) * i, masks[None, SWEEPS - 1])
        for n in range(2):
            r1, r2 = (-1, -2) if n == 0 else (ex, ex + 1)
            base = tip_base[n][1]
            used = join(placed_v[:DEEP], placed_v[2 * DEEP : 5 * DEEP])
            edges_v[r1] = framing(used, base + 2, masks[n, 2])
            edges_v[r2] = framing(used, base + 4, masks[n, 1])
            edges_r[r1] = framing(placed_r[:DEEP], base + 5, masks[n, 1])

    with jax.named_scope("w_near"):
        for n in range(2):
            pl.when(from_far[n])(lambda: far_copy(n).wait_recv())
            pl.when(from_s[n])(lambda: near_copy(n).wait_recv())

    with jax.named_scope("stencil"):
        by_d, by_x, by_y, by_r2, by_r1, by_r0 = {}, {}, {}, {}, {}, {}
        for i, (v_half, r_half) in enumerate(own_rows):
            full, side = v_half + edges_v[i], r_half + edges_r[i]
            by_d[i], by_x[i], by_y[i] = (full[k * 2 * DEEP : (k + 1) * 2 * DEEP] for k in range(3))
            by_r2[i], by_r1[i], by_r0[i] = (
                side[: 2 * DEEP], side[2 * DEEP : 2 * DEEP + 3 * comps], side[3 * DEEP : 3 * DEEP + comps]
            )
        for n in range(2):
            got = jnp.where(from_s[n], near_in[n].astype(F32), 0.0)
            for i, half in enumerate(halves(got)):
                r = i - ex if n == 0 else i + ex
                edge = edges_v[r]
                by_d[r] = half[0:DEEP] + edge[0:DEEP]
                by_x[r] = half[DEEP : 3 * DEEP] + edge[DEEP : 3 * DEEP]
                by_y[r] = half[3 * DEEP : 4 * DEEP] + edge[3 * DEEP : 4 * DEEP]
                by_r2[r] = half[4 * DEEP : 5 * DEEP]
                if r in edges_r:
                    by_r2[r] = by_r2[r] + edges_r[r]
                by_r1[r] = half[3 * DEEP - comps - 1 : 3 * DEEP - 1]
                w_rows[r] = half[3 * DEEP - 1 : 3 * DEEP]
                if r in (-1, ex):
                    w_rows[r] = framed(w_rows[r], *w_tips[n])
            beyond = halves(jnp.where(from_far[n], far_in[n].astype(F32), 0.0))[1 - n]
            by_x[-ex - 1 if n == 0 else 2 * ex] = join(beyond, blank(DEEP - 8, wide_lanes))

        def turn(x):
            return pltpu.roll(x, 1, 1) + pltpu.roll(x, wide_lanes - 1, 1)

        one = {}
        for r in span_rows:
            n = 2 * DEEP if 0 <= r < ex else DEEP
            one[r] = by_d[r] + w_rows[r] * (by_x[r - 1][:n] + by_x[r + 1][:n] + turn(by_y[r]) + by_r2[r])
        two = {}
        for r in range(-1, ex + 1):
            if 0 <= r < ex:
                d_part = join(one[r][:comps], one[r][DEEP : DEEP + 2 * comps])
                y_part = join(one[r][4 * comps : 5 * comps], one[r][DEEP + 2 * comps : DEEP + 4 * comps])
                n = 3 * comps
            else:
                d_part, y_part = one[r][:comps], one[r][4 * comps : 5 * comps]
                n = comps
            x_part = one[r - 1][comps : comps + n] + one[r + 1][comps : comps + n]
            two[r] = d_part + w_rows[r] * (x_part + turn(y_part) + by_r1[r])
        drawn = []
        for r in range(ex):
            x_part = two[r - 1][:comps] + two[r + 1][:comps]
            drawn.append(
                two[r][comps : 2 * comps]
                + w_rows[r] * (x_part + turn(two[r][2 * comps : 3 * comps]) + by_r0[r])
            )
        tractions = [jnp.where(low_half, x, 0.0).astype(BF16) for x in drawn]
        for owner in range(patches):
            pull_out[owner] = sum(dot(tractions[i], onehot_elem[owner, i]) for i in range(ex)).astype(BF16)
    order = sorted(range(slabs), key=lambda j: -min(j, slabs - j))

    def send_pulls(j):
        for i in range(patches):
            if (j, i) != (0, 0):
                pull_copy(j, i).start()

    with jax.named_scope("s_pull"):

        @pl.when(early)
        def _():
            for j in order:
                pl.when(jnp.logical_not(far_off(j)))(lambda: send_pulls(j))
        @pl.when(jnp.logical_not(early))
        def _():
            for j in range(1, slabs):
                pl.when(far_off(j))(lambda: send_pulls(j))
            for j in order:
                pl.when(jnp.logical_not(far_off(j)))(lambda: send_pulls(j))

    for owner in range(patches):

        @pl.when(p == owner)
        def _():
            pulls[s, :, owner * cap : (owner + 1) * cap] = pull_out[owner]


    def sweep(k, v):
        rounded = vb[k]
        wide = rounded.astype(F32)
        with jax.named_scope("w_halo"):
            if k > 0:
                pl.when(has_prev_p)(lambda: y_up(k).wait_recv())
                pl.when(has_next_p)(lambda: y_down(k).wait_recv())
            pl.when(has_prev_s)(lambda: x_up(k).wait_recv())
            pl.when(has_next_s)(lambda: x_down(k).wait_recv())
        line = lax.broadcasted_iota(jnp.int32, (ey, dof), 0)
        along_y = []
        for i in range(ex):
            if k == 0:
                at = shift + side_v + SWEEPS * (i + 1) - 1
                before = rim[at : at + 1].astype(F32)
                after = rim[SWEEPS * i : SWEEPS * i + 1].astype(F32)
            else:
                before = halo_y[k, 0, i].astype(F32)[PACK - 1 : PACK]
                after = halo_y[k, 1, i].astype(F32)[0:1]
            before = jnp.where(has_prev_p, before, 0.0)
            after = jnp.where(has_next_p, after, 0.0)
            prev = jnp.where(line == 0, jnp.broadcast_to(before, (ey, dof)), pltpu.roll(wide[i], 1, 0))
            following = jnp.where(line == ey - 1, jnp.broadcast_to(after, (ey, dof)), pltpu.roll(wide[i], ey - 1, 0))
            along_y.append((prev + following).astype(BF16))
        side_y = dot(jnp.concatenate(along_y, axis=0), cy_ref[...])
        low = jnp.where(has_prev_s, halo_x[k, 0].astype(F32), 0.0)
        high = jnp.where(has_next_s, halo_x[k, 1].astype(F32), 0.0)
        along_x = []
        for i in range(ex):
            below = low if i == 0 else wide[i - 1]
            above = high if i == ex - 1 else wide[i + 1]
            along_x.append((below + above).astype(BF16))
        side_x = dot(jnp.concatenate(along_x, axis=0), cx_ref[...])
        side = (side_x + side_y).reshape(ex, ey, dof)
        residue = jnp.concatenate([(base_buf[i] + side[i]).astype(BF16) for i in range(ex)], axis=0)
        update = dot(residue, inverse_ref[...]).reshape(ex, ey, dof)
        return [v[i] + update[i] * inverses[i] for i in range(ex)]

    def keep(v, k):
        for i in range(ex):
            fluid_ref[i] = v[i]
            if k < SWEEPS:
                vb[k, i] = v[i].astype(BF16)

    with jax.named_scope("sweep0"):
        keep(sweep(0, state_ref), 1)
        send_halos(1)
        prelude(1)

    @pl.when(early)
    def _():
        learn_all()
        for j in order[:-1]:

            @pl.when(far_off(j))
            def _():
                point_second(j).start()
                send_pulls(j)


    def scatter(slab, acc):
        hot = onehot_row[slab]
        value = pulls[slab]
        scaled = jnp.concatenate([hot * value[c : c + 1] for c in range(comps)], axis=0)
        return acc + dot_nt(scaled, onehot_col[slab])

    inner = jnp.minimum(s, slabs - 1 - s)

    def nearest(t):
        step = lax.div(t + 1, 2)
        alternate = jnp.where(lax.rem(t, 2) == 1, s + step, s - step)
        return jnp.where(t <= 2 * inner, alternate, jnp.where(s < slabs - 1 - s, t, slabs - 1 - t))

    def settle_points(t):
        with jax.named_scope("w_point"):
            settle(points.at[nearest(t)], rp2.at[nearest(t)])

    def settle_pulls(t):
        with jax.named_scope("w_pull"):
            settle(pulls.at[nearest(t)], rq.at[nearest(t)])

    def prepared(t, carry):
        settle_points(t)
        build_points(nearest(t))
        return carry

    def gathered(t, acc):
        settle_pulls(t)
        return scatter(nearest(t), acc)

    def gathered_ahead(t, acc):
        settle_points(t + half - 1)
        settle_pulls(t)
        acc = scatter(nearest(t), acc)
        build_points(nearest(t + half - 1))
        return acc

    half = (slabs + 1) // 2
    build_points(s)
    with jax.named_scope("shell"):
        shell()
    with jax.named_scope("build1"):
        lax.fori_loop(1, half, prepared, 0)
    with jax.named_scope("w_own"):
        settle(pulls.at[s, :, pl.ds(0, (patches - 1) * cap)], rq.at[s])
    acc = scatter(s, jnp.zeros((comps * rows, cols), F32))
    last = slabs - half + 1
    with jax.named_scope("gather1"):
        acc = lax.fori_loop(1, half, gathered_ahead, acc)
    with jax.named_scope("sweep1"):
        keep(sweep(1, fluid_ref), 2)
        send_halos(2)
    with jax.named_scope("gather2"):
        acc = lax.fori_loop(half, last, gathered_ahead, acc)
        acc = lax.fori_loop(last, slabs, gathered, acc)
    loads = acc.reshape(comps, rows, cols)
    fresh = [rest_buf[c] + loads[c] * gain_buf[...] for c in range(comps)]
    narrow = jnp.concatenate([x.astype(BF16) for x in fresh], axis=0)
    def picks_for(j):
        k = patch_peer(j)
        span = pl.ds(pl.multiple_of(k * cap, cap), cap)
        spread = dot(narrow, onehot_col[s, :, span]).reshape(comps, rows, cap)
        hot = onehot_row[s, :, span].astype(F32)
        for c in range(comps):
            picks_out[k, c : c + 1] = jnp.sum(spread[c] * hot, axis=0, keepdims=True).astype(BF16)

    far_first = sorted(range(1, patches), key=lambda j: -min(j, patches - j))
    with jax.named_scope("s_pick"):
        for j in far_first:
            picks_for(j)
            pick_copy(j).start()
    picks_for(0)
    picks_in[p] = picks_out[p]
    for c in range(comps):
        net_ref[c] = fresh[c]
    with jax.named_scope("sweep2"):
        prelude(2)
        keep(sweep(2, fluid_ref), SWEEPS)
    with jax.named_scope("w_pick"):
        settle(picks_in.at[pl.ds(0, patches - 1)], pick_sem.at[1])
    for k in range(patches):
        live = lives(k)
        for c in range(comps):
            wall_ref[c, 0, :, k * cap : (k + 1) * cap] = jnp.where(live, picks_in[k, c : c + 1].astype(F32), 0.0)

    with jax.named_scope("drain"):
        halo_sends(SWEEPS - 1, lambda copy: copy.wait_send())
        pl.when(has_next_p)(lambda: d_up().wait_send())
        pl.when(has_prev_p)(lambda: d_down().wait_send())
        for n, m in corners:
            pl.when(jnp.logical_and(to_s[n], to_p[m]))(lambda: tip_copy(n, m).wait_send())
        settle(points.at[s, pl.ds(0, patches - 1)], point_sem.at[0])
        settle(points.at[pl.ds(0, slabs - 1)], point_sem.at[2])
        settle(pulls.at[pl.ds(0, slabs - 1)], pull_sem.at[0])
        settle(pulls.at[s, :, pl.ds(0, (patches - 1) * cap)], pull_sem.at[1])
        settle(picks_in.at[pl.ds(0, patches - 1)], pick_sem.at[0])


def deliver(*refs):
    copies = [pltpu.make_async_copy(refs[n], refs[n + 3], refs[6].at[n]) for n in range(3)]
    for copy in copies:
        copy.start()
    for copy in copies:
        copy.wait()


def shards(slabs, patches, *args):
    state, disp, elem = args[0], args[11], args[8]
    ex, ey, dof = state.shape
    comps, rows, cols = disp.shape
    cap = elem.shape[2] // patches
    sem = pltpu.SemaphoreType.DMA
    vmem = pl.BlockSpec(memory_space=pltpu.VMEM)
    hot_bytes = slabs * patches * cap * (rows + cols) * 2
    outs = pl.pallas_call(
        functools.partial(kernel, slabs, patches, len(args)),
        out_shape=(
            pltpu.VMEM(state.shape, F32),
            pltpu.VMEM(disp.shape, F32),
            pltpu.VMEM((comps, 1, 1, elem.shape[2]), F32),
        ),
        in_specs=[pl.BlockSpec(memory_space=pltpu.HBM)] * len(args),
        out_specs=(vmem, vmem, vmem),
        scratch_shapes=[pltpu.VMEM(x.shape, x.dtype) for x in args[:3]]
        + [
            pltpu.VMEM((3,) + args[3].shape, BF16),
            pltpu.VMEM(args[7].shape, BF16),
            pltpu.VMEM((2,) + elem.shape, jnp.int32),
            pltpu.VMEM(args[10].shape, jnp.int32),
            pltpu.VMEM((comps + 1, rows, cols), F32),
            pltpu.VMEM(args[6].shape, BF16),
            pltpu.VMEM((SWEEPS, ex, ey, dof), BF16),
            pltpu.VMEM((SWEEPS, 2, ey, dof), BF16),
            pltpu.VMEM((SWEEPS, 2, ex, PACK, dof), BF16),
            pltpu.VMEM((2, comps, EDGE, cols), F32),
            pltpu.VMEM((slabs, patches, 1, cap), jnp.int32),
            pltpu.VMEM((slabs, comps, patches * cap), BF16),
            pltpu.VMEM((patches, comps, cap), BF16),
            pltpu.VMEM((patches, comps, cap), BF16),
            pltpu.VMEM((patches, comps, cap), BF16),
            pltpu.VMEM((patches, ex, ex * ey, cap), BF16),
            pltpu.VMEM((slabs, rows, patches * cap), BF16),
            pltpu.VMEM((slabs, cols, patches * cap), BF16),
            pltpu.VMEM((comps, rows, cols), F32),
            pltpu.VMEM((rows, cols), F32),
            pltpu.VMEM(state.shape, F32),
            pltpu.VMEM((5 * DEEP, ex * ey), BF16),
            pltpu.VMEM((2, 5 * DEEP, ex * ey), BF16),
            pltpu.VMEM((8, ex * ey), BF16),
            pltpu.VMEM((2, 8, ex * ey), BF16),
            pltpu.VMEM((2, DEEP, dof), BF16),
            pltpu.VMEM((4, TIP, dof), BF16),
            pltpu.VMEM((ex * ey, dof), BF16),
            sem((9,)),
            sem((2, 2)),
            sem((2, 2)),
            sem((2,)),
            sem((3,)),
            sem((slabs,)),
            sem((2,)),
            sem((slabs,)),
            sem((2,)),
            sem((2,)),
            sem((2,)),
            sem((2,)),
            sem((2,)),
            sem((4,)),
            pltpu.SemaphoreType.REGULAR((max(slabs.bit_length() - 2, 1),)),
        ],
        compiler_params=pltpu.CompilerParams(collective_id=0, has_side_effects=True),
    )(*args)
    return pl.pallas_call(
        deliver,
        out_shape=tuple(jax.ShapeDtypeStruct(x.shape, x.dtype) for x in outs),
        in_specs=[vmem] * 3,
        out_specs=(pl.BlockSpec(memory_space=pltpu.HBM),) * 3,
        scratch_shapes=[sem((3,))],
    )(*[pltpu.with_memory_space_constraint(x, pltpu.VMEM) for x in outs])


def solution(mesh):
    return jax.shard_map(
        functools.partial(shards, mesh.shape["slab"], mesh.shape["patch"]),
        mesh=mesh,
        in_specs=(
            P("slab", "patch", None),
            P("slab", "patch", None),
            P("slab", "patch"),
            P(),
            P(),
            P(),
            P(),
            P(),
            P("slab", "patch", None),
            P("slab", "patch", None),
            P("slab", "patch", None),
            P(None, "patch", None),
            P("patch", None),
        ),
        out_specs=(
            P("slab", "patch", None),
            P(None, "patch", None),
            P(None, "slab", "patch", None),
        ),
        check_vma=False,
    )
```

```python
import functools

import jax
import jax.numpy as jnp
from jax import lax
from jax.experimental import pallas as pl
from jax.experimental.pallas import tpu as pltpu
from jax.sharding import PartitionSpec as P

SWEEPS = 3
PACK = 16
EDGE = 8
SPARE = 8 * 2**20
DEEP = 16
TIP = 8
LOAD_ORDER = (7, 6, 3, 4, 5, 0, 1, 2, 9, 8, 10, 11, 12)
MESH = pl.DeviceIdType.MESH
F32 = jnp.float32
BF16 = jnp.bfloat16


def dot(a, b):
    return jnp.dot(a, b, preferred_element_type=F32)


def dot_nt(a, b):
    return lax.dot_general(a, b, (((1,), (1,)), ((), ())), preferred_element_type=F32)


def split_point(point, cols):
    if cols & (cols - 1) == 0:
        return lax.shift_right_logical(point, cols.bit_length() - 1), point & (cols - 1)
    row = lax.div(point, cols)
    return row, point - row * cols


def column(row_vector):
    n = row_vector.shape[1]
    shape = (n, n)
    eye = lax.broadcasted_iota(jnp.int32, shape, 0) == lax.broadcasted_iota(jnp.int32, shape, 1)
    return jnp.sum(jnp.where(eye, jnp.broadcast_to(row_vector, shape), 0.0), axis=1, keepdims=True)


def laplace(x):
    rows, cols = x.shape
    lane = lax.broadcasted_iota(jnp.int32, x.shape, 1)
    left = jnp.where(lane == 0, 0.0, pltpu.roll(x, 1, 1))
    right = jnp.where(lane == cols - 1, 0.0, pltpu.roll(x, cols - 1, 1))
    return 4.0 * x - (pltpu.roll(x, 1, 0) + pltpu.roll(x, rows - 1, 0) + left + right)


def join(*parts):
    return jnp.concatenate(parts, axis=0)


def blank(rows, cols):
    return jnp.zeros((rows, cols), F32)


def first_words(base0, traction, matrix, couple_x, couple_y):
    low = base0.astype(BF16)
    return join(dot_nt(low, couple_x), traction.astype(F32) - dot_nt(low, matrix), dot_nt(low, couple_y))


def second_words(base1, one, comps, matrix, couple_x, couple_y):
    low = base1.astype(BF16)
    by_x, by_y = dot_nt(low, couple_x), dot_nt(low, couple_y)
    by_d = one - dot_nt(low, matrix)
    dof = one.shape[1]
    return join(
        by_d[:comps], by_x, by_y[:comps], blank(DEEP - 5 * comps, dof),
        by_d[comps:], by_y[comps:], blank(DEEP - 4 * comps, dof),
    )


def third_words(base2, two, matrix, couple_x, couple_y):
    low = base2.astype(BF16)
    return join(two - dot_nt(low, matrix), dot_nt(low, couple_x), dot_nt(low, couple_y)).astype(BF16)


def stacked(two, one, none):
    comps, dof = none.shape
    return join(two, one, blank(DEEP - 3 * comps, dof), none, blank(DEEP - comps, dof)).astype(BF16)


def kernel(slabs, patches, args, *refs):
    hbm, refs = refs[:args], refs[args:]
    (fluid_ref, net_ref, wall_ref), refs = refs[:3], refs[3:]
    (state_ref, rhs_ref, scale_ref, matrices, traction_ref, slots, count_ref, nets, inverse_ref) = refs[:9]
    refs = refs[9:]
    cx_ref, cy_ref, matrix_ref = (matrices.at[n] for n in range(3))
    elem_ref, point_ref = slots.at[0], slots.at[1]
    (vb, halo_x, halo_y, halo_d, points, pulls, pull_out, picks_out, picks_in) = refs[:9]
    (onehot_elem, onehot_row, onehot_col, rest_buf, gain_buf, base_buf) = refs[9:15]
    (near_out, near_in, far_out, far_in, side_out, tip_out, rim) = refs[15:22]
    (load_sem, rx, ry, rd, point_sem, rp2, pull_sem, rq, pick_sem) = refs[22:31]
    (r_near, s_far, r_far, r_side, r_tip, near_sem) = refs[31:]
    s_near, s_side, s_tip = load_sem.at[pl.ds(0, 2)], load_sem.at[pl.ds(2, 2)], load_sem.at[pl.ds(4, 4)]
    sx, sy, sd = s_near, s_side, s_far
    comps = nets.shape[0] - 1
    disp_ref, stiff_ref = nets.at[pl.ds(0, comps)], nets.at[comps]
    homes = (
        (state_ref, 0), (rhs_ref, 1), (scale_ref, 2), (matrix_ref, 3), (cx_ref, 3), (cy_ref, 3), (inverse_ref, 8),
        (traction_ref, 4), (elem_ref, 5), (point_ref, 5), (count_ref, 6), (disp_ref, 7), (stiff_ref, 7),
    )

    loads_in = [pltpu.make_async_copy(hbm[n], homes[n][0], load_sem.at[homes[n][1]]) for n in range(args)]
    for n in LOAD_ORDER:
        loads_in[n].start()
    groups = (state_ref, rhs_ref, scale_ref, matrices, traction_ref, slots, count_ref, nets, inverse_ref)

    def ready(*names):
        for n in names:
            pltpu.make_async_copy(groups[n], groups[n], load_sem.at[n]).wait()

    s = lax.axis_index("slab")
    p = lax.axis_index("patch")
    ex, ey, dof = state_ref.shape
    rows, cols = stiff_ref.shape
    cap = elem_ref.shape[2] // patches
    wide_lanes = ex * ey

    def slab_peer(j):
        return lax.rem(s + j, slabs)

    def patch_peer(j):
        return lax.rem(p + j, patches)

    def slab_sides(reach, semaphore):
        @pl.when(s >= reach)
        def _():
            pl.semaphore_signal(semaphore, inc=1, device_id=(s - reach, p), device_id_type=MESH)

        @pl.when(s + reach < slabs)
        def _():
            pl.semaphore_signal(semaphore, inc=1, device_id=(s + reach, p), device_id_type=MESH)

    def slab_count(reach):
        return jnp.where(s >= reach, 1, 0) + jnp.where(s + reach < slabs, 1, 0)

    reaches = []
    while 2 ** (len(reaches) + 1) < slabs - 1:
        reaches.append(2 ** (len(reaches) + 1))

    def near_signal(n):
        slab_sides(reaches[n], near_sem.at[n])

    def near_wait(n):
        pl.semaphore_wait(near_sem.at[n], slab_count(reaches[n]))

    has_prev_s, has_next_s = s > 0, s < slabs - 1
    has_prev_p, has_next_p = p > 0, p < patches - 1
    has_far_prev, has_far_next = s > 1, s < slabs - 2

    barrier = pltpu.get_barrier_semaphore()
    for j in range(1, patches):
        pl.semaphore_signal(barrier, inc=1, device_id=(s, patch_peer(j)), device_id_type=MESH)
    for reach in (1, 2):

        @pl.when(s >= reach)
        def _():
            for j in range(patches):
                pl.semaphore_signal(barrier, inc=1, device_id=(s - reach, patch_peer(j)), device_id_type=MESH)

        @pl.when(s + reach < slabs)
        def _():
            for j in range(patches):
                pl.semaphore_signal(barrier, inc=1, device_id=(s + reach, patch_peer(j)), device_id_type=MESH)

    awaited = patches - 1 + patches * (slab_count(1) + slab_count(2))

    def remote(src, dst, send, recv, target):
        return pltpu.make_async_remote_copy(
            src_ref=src, dst_ref=dst, send_sem=send, recv_sem=recv, device_id=target, device_id_type=MESH
        )

    def slab_at(step):
        return jnp.clip(s + step, 0, slabs - 1)

    def patch_at(step):
        return jnp.clip(p + step, 0, patches - 1)

    def x_up(k):
        return remote(vb.at[k, ex - 1], halo_x.at[k, 0], sx.at[0], rx.at[k % 2, 0], (slab_at(1), p))

    def x_down(k):
        return remote(vb.at[k, 0], halo_x.at[k, 1], sx.at[1], rx.at[k % 2, 1], (slab_at(-1), p))

    def y_up(k):
        return remote(
            vb.at[k, :, pl.ds(ey - PACK, PACK)], halo_y.at[k, 0], sy.at[0], ry.at[k % 2, 0], (s, patch_at(1))
        )

    def y_down(k):
        return remote(vb.at[k, :, pl.ds(0, PACK)], halo_y.at[k, 1], sy.at[1], ry.at[k % 2, 1], (s, patch_at(-1)))

    def d_up():
        return remote(disp_ref.at[:, pl.ds(rows - EDGE, EDGE)], halo_d.at[0], sd.at[0], rd.at[0], (s, patch_at(1)))

    def d_down():
        return remote(disp_ref.at[:, pl.ds(0, EDGE)], halo_d.at[1], sd.at[1], rd.at[1], (s, patch_at(-1)))

    shift = ey - TIP
    side_base = (shift, 0)
    tip_base = [(DEEP + TIP * n + ey, DEEP + TIP * n) for n in range(2)]

    side_w = ex * (2 * SWEEPS - 1)
    side_v = SWEEPS + 2

    def near_copy(n):
        return remote(near_out, near_in.at[n], s_near.at[n], r_near.at[n], (slab_at(1 - 2 * n), p))

    def far_copy(n):
        return remote(far_out, far_in.at[n], s_far.at[n], r_far.at[n], (slab_at(2 - 4 * n), p))

    def side_copy(n):
        return remote(side_out.at[n], rim.at[pl.ds(side_base[n], DEEP)], s_side.at[n], r_side.at[n], (s, patch_at(1 - 2 * n)))

    def tip_copy(n, m):
        q = 2 * n + m
        return remote(tip_out.at[q], rim.at[pl.ds(tip_base[n][m], TIP)], s_tip.at[q], r_tip.at[q], (slab_at(1 - 2 * n), patch_at(1 - 2 * m)))

    to_s, from_s = (has_next_s, has_prev_s), (has_prev_s, has_next_s)
    to_p, from_p = (has_next_p, has_prev_p), (has_prev_p, has_next_p)
    to_far, from_far = (has_far_next, has_far_prev), (has_far_prev, has_far_next)
    corners = [(n, m) for n in range(2) for m in range(2)]
    def point_first(j):
        peer = patch_peer(j)
        src = point_ref.at[0, :, pl.ds(pl.multiple_of(peer * cap, cap), cap)]
        return remote(src, points.at[s, p], point_sem.at[0], point_sem.at[1], (s, peer))

    def point_second(j):
        return remote(points.at[s], points.at[s], point_sem.at[2], rp2.at[s], (slab_peer(j), p))

    def pull_copy(j, i):
        to = (slab_peer(j), patch_peer(i))
        here = pl.ds(pl.multiple_of(p * cap, cap), cap)
        return remote(pull_out.at[to[1]], pulls.at[s, :, here], pull_sem.at[0 if j else 1], rq.at[s], to)

    def pick_copy(j):
        peer = patch_peer(j)
        return remote(picks_out.at[peer], picks_in.at[p], pick_sem.at[0], pick_sem.at[1], (s, peer))

    def settle(ref, semaphore):
        pltpu.make_async_copy(ref, ref, semaphore).wait()

    def halo_sends(k, act):
        pl.when(has_next_s)(lambda: act(x_up(k)))
        pl.when(has_prev_s)(lambda: act(x_down(k)))
        if k > 0:
            pl.when(has_next_p)(lambda: act(y_up(k)))
            pl.when(has_prev_p)(lambda: act(y_down(k)))

    def send_halos(k):
        if k == 0:
            for n in range(2):
                pl.when(to_s[n])(lambda: near_copy(n).wait_send())
        else:
            halo_sends(k - 1, lambda copy: copy.wait_send())
        if k == 1:
            for n in range(2):
                pl.when(to_p[n])(lambda: side_copy(n).wait_send())
        halo_sends(k, lambda copy: copy.start())

    def build_points(slab):
        for k in range(patches):
            row, col = split_point(points[slab, k], cols)
            span = pl.ds(k * cap, cap)
            onehot_row[slab, :, span] = jnp.where(
                lax.broadcasted_iota(jnp.int32, (rows, cap), 0) == row, 1.0, 0.0
            ).astype(BF16)
            onehot_col[slab, :, span] = jnp.where(
                lax.broadcasted_iota(jnp.int32, (cols, cap), 0) == col, 1.0, 0.0
            ).astype(BF16)

    def lives(k):
        lane = lax.broadcasted_iota(jnp.int32, (1, cap), 1)
        return lane < count_ref[0, :, k : k + 1]

    def shell():
        pl.when(has_prev_p)(lambda: d_up().wait_recv())
        pl.when(has_next_p)(lambda: d_down().wait_recv())
        total = rows + 2 * EDGE
        line = lax.broadcasted_iota(jnp.int32, (total, cols), 0)
        first = jnp.where(has_prev_p, 0, EDGE)
        last = jnp.where(has_next_p, total, EDGE + rows)
        valid = (line >= first) & (line < last)
        gain = 1.0 / (36.0 * stiff_ref[...])
        gain_buf[...] = gain
        for c in range(comps):
            field = jnp.concatenate([halo_d[0, c], disp_ref[c], halo_d[1, c]], axis=0)
            field = jnp.where(valid, field, 0.0)
            bend = jnp.where(valid, laplace(field), 0.0)
            full = (laplace(bend) + 4.0 * bend)[EDGE : EDGE + rows]
            rest_buf[c] = disp_ref[c] - stiff_ref[...] * full * gain

    with jax.named_scope("w_mat"):
        ready(4, 8)
        base0 = dot_nt(traction_ref[...], inverse_ref[...])
        ready(3)
    couples = (matrix_ref[...], cx_ref[...], cy_ref[...])
    with jax.named_scope("words"):
        one = first_words(base0, traction_ref[...], *couples)
        base1 = dot_nt(one.astype(BF16), inverse_ref[...])
    with jax.named_scope("w_state"):
        ready(0, 1, 2)
    rounded0 = state_ref[...].astype(BF16)
    vb[0] = rounded0
    wet = rhs_ref[...].astype(BF16)
    flat = 1.0 / scale_ref[...]
    w_own = jnp.concatenate([flat, blank(ex, wide_lanes - ey)], axis=1)
    lane = lax.broadcasted_iota(jnp.int32, (1, wide_lanes), 1)
    low_half = lane < ey
    tail_half = lane < ey + ey // 2
    w_lines = jnp.concatenate([w_own] + [blank(ex, wide_lanes)] * (dof // wide_lanes - 1), axis=1)
    with jax.named_scope("project"):
        two = second_words(base1, one, comps, *couples)
        flow = rounded0.reshape(wide_lanes, dof)
        passed = join(*[dot(flow, couple) for couple in couples]).astype(BF16)
        mapped = dot(join(passed, wet.reshape(wide_lanes, dof)), inverse_ref[...])
        turned = join(flow.astype(F32) - mapped[:wide_lanes], mapped[wide_lanes:]).astype(BF16)
        both = dot_nt(stacked(two, one, traction_ref[...].astype(F32)), turned)
        own_v = join(*[both[: 2 * DEEP, n * wide_lanes : (n + 1) * wide_lanes] for n in range(3)])
        own_r = both[:, 3 * wide_lanes :]
        packed = jnp.where(low_half, w_own[0:1], pltpu.roll(w_own[1:2], ey, 1))
        spare = join(
            blank(2 * DEEP - comps - 1, wide_lanes), own_r[2 * DEEP : 2 * DEEP + comps], packed
        )
        near_out[...] = join(
            own_v[0:DEEP], own_v[2 * DEEP : 4 * DEEP] + spare, own_v[4 * DEEP : 5 * DEEP], own_r[0:DEEP]
        ).astype(BF16)
        far_out[...] = own_v[2 * DEEP : 2 * DEEP + 8].astype(BF16)

        def state_at(i, c):
            return state_ref[i, c : c + 1]

        def rhs_at(i, c):
            return rhs_ref[i, c : c + 1]

        for m in range(2):
            close = [ey - 1 - j if m == 0 else j for j in range(SWEEPS)]
            if m == 1:
                side = [state_at(i, c) for i in range(ex) for c in close]
                side += [rhs_at(i, c) for i in range(ex) for c in close[: SWEEPS - 1]]
                side += [w_lines, blank(DEEP - side_w - ex, dof)]
            else:
                side = [w_lines, blank(side_v - ex, dof)]
                side += [state_at(i, c) for i in range(ex) for c in close[::-1]]
                side += [blank(1, dof)]
                side += [rhs_at(i, c) for i in range(ex) for c in close[: SWEEPS - 1][::-1]]
            side_out[m] = join(*side).astype(BF16)
            for n in range(2):
                r1, r2 = (ex - 1, ex - 2) if n == 0 else (0, 1)
                near2 = [state_at(r1, close[0]), state_at(r1, close[1])]
                last = [state_at(r2, close[0]), rhs_at(r1, close[0])]
                weigh = w_lines[r1 : r1 + 1]
                if m == 1:
                    tip = [weigh, blank(1, dof), *near2, *last, blank(TIP - 6, dof)]
                else:
                    tip = [*near2[::-1], blank(1, dof), *last, weigh, blank(TIP - 6, dof)]
                tip_out[2 * n + m] = join(*tip).astype(BF16)

    ready(5, 6, 7)
    with jax.named_scope("w_barrier"):
        pl.semaphore_wait(barrier, awaited)
    for n, m in corners:
        pl.when(jnp.logical_and(to_s[n], to_p[m]))(lambda: tip_copy(n, m).start())
    for n in range(2):
        pl.when(to_s[n])(lambda: near_copy(n).start())
    for m in range(2):
        pl.when(to_p[m])(lambda: side_copy(m).start())
    for n in range(2):
        pl.when(to_far[n])(lambda: far_copy(n).start())
    if reaches:
        near_signal(0)
    for j in range(1, patches):
        point_first(j).start()
    for owner in range(patches):

        @pl.when(p == owner)
        def _():
            points[s, owner] = point_ref[0, :, owner * cap : (owner + 1) * cap]

    for owner in range(patches):
        elem = elem_ref[0, :, owner * cap : (owner + 1) * cap]
        for i in range(ex):
            line = lax.broadcasted_iota(jnp.int32, (wide_lanes, cap), 0)
            hit = (line + i * ey == elem) & (line < ey) & lives(owner)
            onehot_elem[owner, i] = jnp.where(hit, 1.0, 0.0).astype(BF16)
    if reaches:
        with jax.named_scope("w_reach"):
            near_wait(0)
        if len(reaches) > 1:
            near_signal(1)
    send_halos(0)
    scales = [column(scale_ref[i : i + 1, :]) for i in range(ex)]
    inverses = [1.0 / x for x in scales]

    def prelude(k):
        own = dot(vb[k].reshape(ex * ey, dof), matrix_ref[...]).reshape(ex, ey, dof)
        for i in range(ex):
            base_buf[i] = rhs_ref[i] - scales[i] * own[i]

    for n in range(2):
        pl.when(to_far[n])(lambda: far_copy(n).wait_send())
    pl.when(has_next_p)(lambda: d_up().start())
    pl.when(has_prev_p)(lambda: d_down().start())
    with jax.named_scope("late_words"):
        base2 = dot_nt(two.astype(BF16), inverse_ref[...])
        words = third_words(base2, two, matrix_ref[...], cx_ref[...], cy_ref[...])
        rest = stacked(base2, base1, base0)
    with jax.named_scope("prelude"):
        prelude(0)

    def halves(x):
        return jnp.where(low_half, x, 0.0), jnp.where(low_half, pltpu.roll(x, ey, 1), 0.0)

    span_rows = list(range(-ex, 2 * ex))

    def between(low, high):
        return (lane >= low) & (lane < high)

    def frame_mask(n, reach):
        right, left = has_next_p, has_prev_p
        if n is not None:
            right, left = jnp.logical_and(right, from_s[n]), jnp.logical_and(left, from_s[n])
        right, left = jnp.where(right, 1, 0), jnp.where(left, 1, 0)
        ahead, behind = between(ey, ey + reach), between(wide_lanes - reach, wide_lanes)
        return jnp.where(ahead, right, jnp.where(behind, left, 0)) > 0

    masks = {(n, reach): frame_mask(n, reach) for n in (None, 0, 1) for reach in range(1, SWEEPS + 1)}

    def framing(x, source, mask):
        return jnp.where(mask, pltpu.roll(x, (ey - source) % wide_lanes, 1), 0.0)

    with jax.named_scope("halves"):
        own_rows = list(zip(halves(own_v), halves(own_r)))
    with jax.named_scope("w_side"):
        for m in range(2):
            pl.when(from_p[m])(lambda: side_copy(m).wait_recv())
        for n, m in corners:
            pl.when(jnp.logical_and(from_s[n], from_p[m]))(lambda: tip_copy(n, m).wait_recv())
    early = s < slabs // 2
    known = 4

    def far_off(j):
        peer = slab_peer(j)
        return jnp.maximum(peer - s, s - peer) > known

    def learn_all():
        for n in range(1, len(reaches)):
            with jax.named_scope("w_reach"):
                near_wait(n)
            if n + 1 < len(reaches):
                near_signal(n + 1)

    with jax.named_scope("w_pt1"):
        settle(points.at[s, pl.ds(0, patches - 1)], point_sem.at[1])

    @pl.when(early)
    def _():
        for j in range(1, slabs):
            pl.when(jnp.logical_not(far_off(j)))(lambda: point_second(j).start())

    @pl.when(jnp.logical_not(early))
    def _():
        learn_all()
        for j in range(1, slabs):
            point_second(j).start()

    with jax.named_scope("place"):
        stack = rim[...]
        placed_v = dot_nt(words, stack)
        placed_r = dot_nt(rest, stack)

        def rim_row(base, at, ok):
            return jnp.where(ok, rim[base + at : base + at + 1, :wide_lanes].astype(F32), 0.0)

        def framed(middle, before, after):
            before, after = pltpu.roll(before, ey, 1), pltpu.roll(after, ey, 1)
            return jnp.where(low_half, middle, jnp.where(tail_half, after, before))

        w_rows = {}
        for i in range(ex):
            w_rows[i] = framed(
                w_own[i : i + 1],
                rim_row(side_base[0], i, has_prev_p),
                rim_row(side_base[1], side_w + i, has_next_p),
            )
        w_tips = [
            (
                rim_row(tip_base[n][0], 5, jnp.logical_and(from_s[n], has_prev_p)),
                rim_row(tip_base[n][1], 0, jnp.logical_and(from_s[n], has_next_p)),
            )
            for n in range(2)
        ]
        edges_v, edges_r = {}, {}
        for i in range(ex):
            edges_v[i] = framing(placed_v, SWEEPS * i, masks[None, SWEEPS])
            edges_r[i] = framing(placed_r, SWEEPS * ex + (SWEEPS - 1) * i, masks[None, SWEEPS - 1])
        for n in range(2):
            r1, r2 = (-1, -2) if n == 0 else (ex, ex + 1)
            base = tip_base[n][1]
            used = join(placed_v[:DEEP], placed_v[2 * DEEP : 5 * DEEP])
            edges_v[r1] = framing(used, base + 2, masks[n, 2])
            edges_v[r2] = framing(used, base + 4, masks[n, 1])
            edges_r[r1] = framing(placed_r[:DEEP], base + 5, masks[n, 1])

    def across(k, wide):
        line = lax.broadcasted_iota(jnp.int32, (ey, dof), 0)
        along_y = []
        for i in range(ex):
            if k == 0:
                at = shift + side_v + SWEEPS * (i + 1) - 1
                before = rim[at : at + 1].astype(F32)
                after = rim[SWEEPS * i : SWEEPS * i + 1].astype(F32)
            else:
                before = halo_y[k, 0, i].astype(F32)[PACK - 1 : PACK]
                after = halo_y[k, 1, i].astype(F32)[0:1]
            before = jnp.where(has_prev_p, before, 0.0)
            after = jnp.where(has_next_p, after, 0.0)
            prev = jnp.where(line == 0, jnp.broadcast_to(before, (ey, dof)), pltpu.roll(wide[i], 1, 0))
            following = jnp.where(line == ey - 1, jnp.broadcast_to(after, (ey, dof)), pltpu.roll(wide[i], ey - 1, 0))
            along_y.append((prev + following).astype(BF16))
        return dot(jnp.concatenate(along_y, axis=0), cy_ref[...])

    with jax.named_scope("w_near"):
        for n in range(2):
            pl.when(from_far[n])(lambda: far_copy(n).wait_recv())
            pl.when(from_s[n])(lambda: near_copy(n).wait_recv())

    with jax.named_scope("stencil"):
        by_d, by_x, by_y, by_r2, by_r1, by_r0 = {}, {}, {}, {}, {}, {}
        for i, (v_half, r_half) in enumerate(own_rows):
            full, side = v_half + edges_v[i], r_half + edges_r[i]
            by_d[i], by_x[i], by_y[i] = (full[k * 2 * DEEP : (k + 1) * 2 * DEEP] for k in range(3))
            by_r2[i], by_r1[i], by_r0[i] = (
                side[: 2 * DEEP], side[2 * DEEP : 2 * DEEP + 3 * comps], side[3 * DEEP : 3 * DEEP + comps]
            )
        for n in range(2):
            got = jnp.where(from_s[n], near_in[n].astype(F32), 0.0)
            for i, half in enumerate(halves(got)):
                r = i - ex if n == 0 else i + ex
                edge = edges_v[r]
                by_d[r] = half[0:DEEP] + edge[0:DEEP]
                by_x[r] = half[DEEP : 3 * DEEP] + edge[DEEP : 3 * DEEP]
                by_y[r] = half[3 * DEEP : 4 * DEEP] + edge[3 * DEEP : 4 * DEEP]
                by_r2[r] = half[4 * DEEP : 5 * DEEP]
                if r in edges_r:
                    by_r2[r] = by_r2[r] + edges_r[r]
                by_r1[r] = half[3 * DEEP - comps - 1 : 3 * DEEP - 1]
                w_rows[r] = half[3 * DEEP - 1 : 3 * DEEP]
                if r in (-1, ex):
                    w_rows[r] = framed(w_rows[r], *w_tips[n])
            beyond = halves(jnp.where(from_far[n], far_in[n].astype(F32), 0.0))[1 - n]
            by_x[-ex - 1 if n == 0 else 2 * ex] = join(beyond, blank(DEEP - 8, wide_lanes))

        def turn(x):
            return pltpu.roll(x, 1, 1) + pltpu.roll(x, wide_lanes - 1, 1)

        one = {}
        for r in span_rows:
            n = 2 * DEEP if 0 <= r < ex else DEEP
            one[r] = by_d[r] + w_rows[r] * (by_x[r - 1][:n] + by_x[r + 1][:n] + turn(by_y[r]) + by_r2[r])
        two = {}
        for r in range(-1, ex + 1):
            if 0 <= r < ex:
                d_part = join(one[r][:comps], one[r][DEEP : DEEP + 2 * comps])
                y_part = join(one[r][4 * comps : 5 * comps], one[r][DEEP + 2 * comps : DEEP + 4 * comps])
                n = 3 * comps
            else:
                d_part, y_part = one[r][:comps], one[r][4 * comps : 5 * comps]
                n = comps
            x_part = one[r - 1][comps : comps + n] + one[r + 1][comps : comps + n]
            two[r] = d_part + w_rows[r] * (x_part + turn(y_part) + by_r1[r])
        drawn = []
        for r in range(ex):
            x_part = two[r - 1][:comps] + two[r + 1][:comps]
            drawn.append(
                two[r][comps : 2 * comps]
                + w_rows[r] * (x_part + turn(two[r][2 * comps : 3 * comps]) + by_r0[r])
            )
        tractions = [jnp.where(low_half, x, 0.0).astype(BF16) for x in drawn]
        for owner in range(patches):
            pull_out[owner] = sum(dot(tractions[i], onehot_elem[owner, i]) for i in range(ex)).astype(BF16)
        crossed = across(0, vb[0].astype(F32)).reshape(ex, ey, dof)
        for i in range(ex):
            base_buf[i] = base_buf[i] + crossed[i]
    order = sorted(range(slabs), key=lambda j: -min(j, slabs - j))

    def send_pulls(j):
        for i in range(patches):
            if (j, i) != (0, 0):
                pull_copy(j, i).start()

    with jax.named_scope("s_pull"):

        @pl.when(early)
        def _():
            for j in order:
                pl.when(jnp.logical_not(far_off(j)))(lambda: send_pulls(j))
        @pl.when(jnp.logical_not(early))
        def _():
            for j in range(1, slabs):
                pl.when(far_off(j))(lambda: send_pulls(j))
            for j in order:
                pl.when(jnp.logical_not(far_off(j)))(lambda: send_pulls(j))

    for owner in range(patches):

        @pl.when(p == owner)
        def _():
            pulls[s, :, owner * cap : (owner + 1) * cap] = pull_out[owner]


    def sweep(k, v):
        rounded = vb[k]
        wide = rounded.astype(F32)
        with jax.named_scope("w_halo"):
            if k > 0:
                pl.when(has_prev_p)(lambda: y_up(k).wait_recv())
                pl.when(has_next_p)(lambda: y_down(k).wait_recv())
            pl.when(has_prev_s)(lambda: x_up(k).wait_recv())
            pl.when(has_next_s)(lambda: x_down(k).wait_recv())
        side_y = across(k, wide) if k > 0 else 0.0
        low = jnp.where(has_prev_s, halo_x[k, 0].astype(F32), 0.0)
        high = jnp.where(has_next_s, halo_x[k, 1].astype(F32), 0.0)
        along_x = []
        for i in range(ex):
            below = low if i == 0 else wide[i - 1]
            above = high if i == ex - 1 else wide[i + 1]
            along_x.append((below + above).astype(BF16))
        side_x = dot(jnp.concatenate(along_x, axis=0), cx_ref[...])
        side = (side_x + side_y).reshape(ex, ey, dof)
        residue = jnp.concatenate([(base_buf[i] + side[i]).astype(BF16) for i in range(ex)], axis=0)
        update = dot(residue, inverse_ref[...]).reshape(ex, ey, dof)
        return [v[i] + update[i] * inverses[i] for i in range(ex)]

    def keep(v, k):
        for i in range(ex):
            fluid_ref[i] = v[i]
            if k < SWEEPS:
                vb[k, i] = v[i].astype(BF16)

    with jax.named_scope("sweep0"):
        keep(sweep(0, state_ref), 1)
        send_halos(1)
        prelude(1)

    @pl.when(early)
    def _():
        learn_all()
        for j in order[:-1]:

            @pl.when(far_off(j))
            def _():
                point_second(j).start()
                send_pulls(j)


    def scatter(slab, acc):
        hot = onehot_row[slab]
        value = pulls[slab]
        scaled = jnp.concatenate([hot * value[c : c + 1] for c in range(comps)], axis=0)
        return acc + dot_nt(scaled, onehot_col[slab])

    inner = jnp.minimum(s, slabs - 1 - s)

    def nearest(t):
        step = lax.div(t + 1, 2)
        alternate = jnp.where(lax.rem(t, 2) == 1, s + step, s - step)
        return jnp.where(t <= 2 * inner, alternate, jnp.where(s < slabs - 1 - s, t, slabs - 1 - t))

    def settle_points(t):
        with jax.named_scope("w_point"):
            settle(points.at[nearest(t)], rp2.at[nearest(t)])

    def settle_pulls(t):
        with jax.named_scope("w_pull"):
            settle(pulls.at[nearest(t)], rq.at[nearest(t)])

    def prepared(t, carry):
        settle_points(t)
        build_points(nearest(t))
        return carry

    def gathered(t, acc):
        settle_pulls(t)
        return scatter(nearest(t), acc)

    def gathered_ahead(t, acc):
        settle_points(t + half - 1)
        settle_pulls(t)
        acc = scatter(nearest(t), acc)
        build_points(nearest(t + half - 1))
        return acc

    half = (slabs + 1) // 2
    build_points(s)
    with jax.named_scope("shell"):
        shell()
    with jax.named_scope("build1"):
        lax.fori_loop(1, half, prepared, 0)
    with jax.named_scope("w_own"):
        settle(pulls.at[s, :, pl.ds(0, (patches - 1) * cap)], rq.at[s])
    acc = scatter(s, jnp.zeros((comps * rows, cols), F32))
    last = slabs - half + 1
    with jax.named_scope("gather1"):
        acc = lax.fori_loop(1, half, gathered_ahead, acc)
    with jax.named_scope("sweep1"):
        keep(sweep(1, fluid_ref), 2)
        send_halos(2)
    with jax.named_scope("gather2"):
        acc = lax.fori_loop(half, last, gathered_ahead, acc)
        acc = lax.fori_loop(last, slabs, gathered, acc)
    loads = acc.reshape(comps, rows, cols)
    fresh = [rest_buf[c] + loads[c] * gain_buf[...] for c in range(comps)]
    narrow = jnp.concatenate([x.astype(BF16) for x in fresh], axis=0)
    def picks_for(j):
        k = patch_peer(j)
        span = pl.ds(pl.multiple_of(k * cap, cap), cap)
        spread = dot(narrow, onehot_col[s, :, span]).reshape(comps, rows, cap)
        hot = onehot_row[s, :, span].astype(F32)
        for c in range(comps):
            picks_out[k, c : c + 1] = jnp.sum(spread[c] * hot, axis=0, keepdims=True).astype(BF16)

    far_first = sorted(range(1, patches), key=lambda j: -min(j, patches - j))
    with jax.named_scope("s_pick"):
        for j in far_first:
            picks_for(j)
            pick_copy(j).start()
    picks_for(0)
    picks_in[p] = picks_out[p]
    for c in range(comps):
        net_ref[c] = fresh[c]
    with jax.named_scope("sweep2"):
        prelude(2)
        keep(sweep(2, fluid_ref), SWEEPS)
    with jax.named_scope("w_pick"):
        settle(picks_in.at[pl.ds(0, patches - 1)], pick_sem.at[1])
    for k in range(patches):
        live = lives(k)
        for c in range(comps):
            wall_ref[c, 0, :, k * cap : (k + 1) * cap] = jnp.where(live, picks_in[k, c : c + 1].astype(F32), 0.0)

    with jax.named_scope("drain"):
        halo_sends(SWEEPS - 1, lambda copy: copy.wait_send())
        pl.when(has_next_p)(lambda: d_up().wait_send())
        pl.when(has_prev_p)(lambda: d_down().wait_send())
        for n, m in corners:
            pl.when(jnp.logical_and(to_s[n], to_p[m]))(lambda: tip_copy(n, m).wait_send())
        settle(points.at[s, pl.ds(0, patches - 1)], point_sem.at[0])
        settle(points.at[pl.ds(0, slabs - 1)], point_sem.at[2])
        settle(pulls.at[pl.ds(0, slabs - 1)], pull_sem.at[0])
        settle(pulls.at[s, :, pl.ds(0, (patches - 1) * cap)], pull_sem.at[1])
        settle(picks_in.at[pl.ds(0, patches - 1)], pick_sem.at[0])


def deliver(*refs):
    copies = [pltpu.make_async_copy(refs[n], refs[n + 3], refs[6].at[n]) for n in range(3)]
    for copy in copies:
        copy.start()
    for copy in copies:
        copy.wait()


def shards(slabs, patches, *args):
    state, disp, elem = args[0], args[11], args[8]
    ex, ey, dof = state.shape
    comps, rows, cols = disp.shape
    cap = elem.shape[2] // patches
    sem = pltpu.SemaphoreType.DMA
    vmem = pl.BlockSpec(memory_space=pltpu.VMEM)
    hot_bytes = slabs * patches * cap * (rows + cols) * 2
    outs = pl.pallas_call(
        functools.partial(kernel, slabs, patches, len(args)),
        out_shape=(
            pltpu.VMEM(state.shape, F32),
            pltpu.VMEM(disp.shape, F32),
            pltpu.VMEM((comps, 1, 1, elem.shape[2]), F32),
        ),
        in_specs=[pl.BlockSpec(memory_space=pltpu.HBM)] * len(args),
        out_specs=(vmem, vmem, vmem),
        scratch_shapes=[pltpu.VMEM(x.shape, x.dtype) for x in args[:3]]
        + [
            pltpu.VMEM((3,) + args[3].shape, BF16),
            pltpu.VMEM(args[7].shape, BF16),
            pltpu.VMEM((2,) + elem.shape, jnp.int32),
            pltpu.VMEM(args[10].shape, jnp.int32),
            pltpu.VMEM((comps + 1, rows, cols), F32),
            pltpu.VMEM(args[6].shape, BF16),
            pltpu.VMEM((SWEEPS, ex, ey, dof), BF16),
            pltpu.VMEM((SWEEPS, 2, ey, dof), BF16),
            pltpu.VMEM((SWEEPS, 2, ex, PACK, dof), BF16),
            pltpu.VMEM((2, comps, EDGE, cols), F32),
            pltpu.VMEM((slabs, patches, 1, cap), jnp.int32),
            pltpu.VMEM((slabs, comps, patches * cap), BF16),
            pltpu.VMEM((patches, comps, cap), BF16),
            pltpu.VMEM((patches, comps, cap), BF16),
            pltpu.VMEM((patches, comps, cap), BF16),
            pltpu.VMEM((patches, ex, ex * ey, cap), BF16),
            pltpu.VMEM((slabs, rows, patches * cap), BF16),
            pltpu.VMEM((slabs, cols, patches * cap), BF16),
            pltpu.VMEM((comps, rows, cols), F32),
            pltpu.VMEM((rows, cols), F32),
            pltpu.VMEM(state.shape, F32),
            pltpu.VMEM((5 * DEEP, ex * ey), BF16),
            pltpu.VMEM((2, 5 * DEEP, ex * ey), BF16),
            pltpu.VMEM((8, ex * ey), BF16),
            pltpu.VMEM((2, 8, ex * ey), BF16),
            pltpu.VMEM((2, DEEP, dof), BF16),
            pltpu.VMEM((4, TIP, dof), BF16),
            pltpu.VMEM((ex * ey, dof), BF16),
            sem((9,)),
            sem((2, 2)),
            sem((2, 2)),
            sem((2,)),
            sem((3,)),
            sem((slabs,)),
            sem((2,)),
            sem((slabs,)),
            sem((2,)),
            sem((2,)),
            sem((2,)),
            sem((2,)),
            sem((2,)),
            sem((4,)),
            pltpu.SemaphoreType.REGULAR((max(slabs.bit_length() - 2, 1),)),
        ],
        compiler_params=pltpu.CompilerParams(collective_id=0, has_side_effects=True),
    )(*args)
    return pl.pallas_call(
        deliver,
        out_shape=tuple(jax.ShapeDtypeStruct(x.shape, x.dtype) for x in outs),
        in_specs=[vmem] * 3,
        out_specs=(pl.BlockSpec(memory_space=pltpu.HBM),) * 3,
        scratch_shapes=[sem((3,))],
    )(*[pltpu.with_memory_space_constraint(x, pltpu.VMEM) for x in outs])


def solution(mesh):
    return jax.shard_map(
        functools.partial(shards, mesh.shape["slab"], mesh.shape["patch"]),
        mesh=mesh,
        in_specs=(
            P("slab", "patch", None),
            P("slab", "patch", None),
            P("slab", "patch"),
            P(),
            P(),
            P(),
            P(),
            P(),
            P("slab", "patch", None),
            P("slab", "patch", None),
            P("slab", "patch", None),
            P(None, "patch", None),
            P("patch", None),
        ),
        out_specs=(
            P("slab", "patch", None),
            P(None, "patch", None),
            P(None, "slab", "patch", None),
        ),
        check_vma=False,
    )
```

```python
import functools

import jax
import jax.numpy as jnp
from jax import lax
from jax.experimental import pallas as pl
from jax.experimental.pallas import tpu as pltpu
from jax.sharding import PartitionSpec as P

SWEEPS = 3
PACK = 16
EDGE = 8
SPARE = 8 * 2**20
DEEP = 16
TIP = 8
LOAD_ORDER = (7, 6, 3, 4, 5, 0, 1, 2, 9, 8, 10, 11, 12)
MESH = pl.DeviceIdType.MESH
F32 = jnp.float32
BF16 = jnp.bfloat16


def dot(a, b):
    return jnp.dot(a, b, preferred_element_type=F32)


def dot_nt(a, b):
    return lax.dot_general(a, b, (((1,), (1,)), ((), ())), preferred_element_type=F32)


def split_point(point, cols):
    if cols & (cols - 1) == 0:
        return lax.shift_right_logical(point, cols.bit_length() - 1), point & (cols - 1)
    row = lax.div(point, cols)
    return row, point - row * cols


def column(row_vector):
    n = row_vector.shape[1]
    shape = (n, n)
    eye = lax.broadcasted_iota(jnp.int32, shape, 0) == lax.broadcasted_iota(jnp.int32, shape, 1)
    return jnp.sum(jnp.where(eye, jnp.broadcast_to(row_vector, shape), 0.0), axis=1, keepdims=True)


def laplace(x):
    rows, cols = x.shape
    lane = lax.broadcasted_iota(jnp.int32, x.shape, 1)
    left = jnp.where(lane == 0, 0.0, pltpu.roll(x, 1, 1))
    right = jnp.where(lane == cols - 1, 0.0, pltpu.roll(x, cols - 1, 1))
    return 4.0 * x - (pltpu.roll(x, 1, 0) + pltpu.roll(x, rows - 1, 0) + left + right)


def join(*parts):
    return jnp.concatenate(parts, axis=0)


def blank(rows, cols):
    return jnp.zeros((rows, cols), F32)


def first_words(base0, traction, matrix, couple_x, couple_y):
    low = base0.astype(BF16)
    return join(dot_nt(low, couple_x), traction.astype(F32) - dot_nt(low, matrix), dot_nt(low, couple_y))


def second_words(base1, one, comps, matrix, couple_x, couple_y):
    low = base1.astype(BF16)
    by_x, by_y = dot_nt(low, couple_x), dot_nt(low, couple_y)
    by_d = one - dot_nt(low, matrix)
    dof = one.shape[1]
    return join(
        by_d[:comps], by_x, by_y[:comps], blank(DEEP - 5 * comps, dof),
        by_d[comps:], by_y[comps:], blank(DEEP - 4 * comps, dof),
    )


def third_words(base2, two, matrix, couple_x, couple_y):
    low = base2.astype(BF16)
    return join(two - dot_nt(low, matrix), dot_nt(low, couple_x), dot_nt(low, couple_y)).astype(BF16)


def stacked(two, one, none):
    comps, dof = none.shape
    return join(two, one, blank(DEEP - 3 * comps, dof), none, blank(DEEP - comps, dof)).astype(BF16)


def kernel(slabs, patches, args, *refs):
    hbm, refs = refs[:args], refs[args:]
    (fluid_ref, net_ref, wall_ref), refs = refs[:3], refs[3:]
    (state_ref, rhs_ref, scale_ref, matrices, traction_ref, slots, count_ref, nets, inverse_ref) = refs[:9]
    refs = refs[9:]
    cx_ref, cy_ref, matrix_ref = (matrices.at[n] for n in range(3))
    elem_ref, point_ref = slots.at[0], slots.at[1]
    (vb, halo_x, halo_y, halo_d, points, pulls, pull_out, picks_out, picks_in) = refs[:9]
    (onehot_elem, onehot_row, onehot_col, rest_buf, gain_buf, base_buf) = refs[9:15]
    (near_out, near_in, far_out, far_in, side_out, tip_out, rim) = refs[15:22]
    (load_sem, rx, ry, rd, point_sem, rp2, pull_sem, rq, pick_sem) = refs[22:31]
    (r_near, s_far, r_far, r_side, r_tip, near_sem) = refs[31:]
    s_near, s_side, s_tip = load_sem.at[pl.ds(0, 2)], load_sem.at[pl.ds(2, 2)], load_sem.at[pl.ds(4, 4)]
    sx, sy, sd = s_near, s_side, s_far
    comps = nets.shape[0] - 1
    disp_ref, stiff_ref = nets.at[pl.ds(0, comps)], nets.at[comps]
    homes = (
        (state_ref, 0), (rhs_ref, 1), (scale_ref, 2), (matrix_ref, 3), (cx_ref, 3), (cy_ref, 3), (inverse_ref, 8),
        (traction_ref, 4), (elem_ref, 5), (point_ref, 5), (count_ref, 6), (disp_ref, 7), (stiff_ref, 7),
    )

    loads_in = [pltpu.make_async_copy(hbm[n], homes[n][0], load_sem.at[homes[n][1]]) for n in range(args)]
    for n in LOAD_ORDER:
        loads_in[n].start()
    groups = (state_ref, rhs_ref, scale_ref, matrices, traction_ref, slots, count_ref, nets, inverse_ref)

    def ready(*names):
        for n in names:
            pltpu.make_async_copy(groups[n], groups[n], load_sem.at[n]).wait()

    s = lax.axis_index("slab")
    p = lax.axis_index("patch")
    ex, ey, dof = state_ref.shape
    rows, cols = stiff_ref.shape
    cap = elem_ref.shape[2] // patches
    wide_lanes = ex * ey

    def slab_peer(j):
        return lax.rem(s + j, slabs)

    def patch_peer(j):
        return lax.rem(p + j, patches)

    def slab_sides(reach, semaphore):
        @pl.when(s >= reach)
        def _():
            pl.semaphore_signal(semaphore, inc=1, device_id=(s - reach, p), device_id_type=MESH)

        @pl.when(s + reach < slabs)
        def _():
            pl.semaphore_signal(semaphore, inc=1, device_id=(s + reach, p), device_id_type=MESH)

    def slab_count(reach):
        return jnp.where(s >= reach, 1, 0) + jnp.where(s + reach < slabs, 1, 0)

    reaches = []
    while 2 ** (len(reaches) + 1) < slabs - 1:
        reaches.append(2 ** (len(reaches) + 1))

    def near_signal(n):
        slab_sides(reaches[n], near_sem.at[n])

    def near_wait(n):
        pl.semaphore_wait(near_sem.at[n], slab_count(reaches[n]))

    has_prev_s, has_next_s = s > 0, s < slabs - 1
    has_prev_p, has_next_p = p > 0, p < patches - 1
    has_far_prev, has_far_next = s > 1, s < slabs - 2

    barrier = pltpu.get_barrier_semaphore()
    for j in range(1, patches):
        pl.semaphore_signal(barrier, inc=1, device_id=(s, patch_peer(j)), device_id_type=MESH)
    for reach in (1, 2):

        @pl.when(s >= reach)
        def _():
            for j in range(patches):
                pl.semaphore_signal(barrier, inc=1, device_id=(s - reach, patch_peer(j)), device_id_type=MESH)

        @pl.when(s + reach < slabs)
        def _():
            for j in range(patches):
                pl.semaphore_signal(barrier, inc=1, device_id=(s + reach, patch_peer(j)), device_id_type=MESH)

    awaited = patches - 1 + patches * (slab_count(1) + slab_count(2))

    def remote(src, dst, send, recv, target):
        return pltpu.make_async_remote_copy(
            src_ref=src, dst_ref=dst, send_sem=send, recv_sem=recv, device_id=target, device_id_type=MESH
        )

    def slab_at(step):
        return jnp.clip(s + step, 0, slabs - 1)

    def patch_at(step):
        return jnp.clip(p + step, 0, patches - 1)

    def x_up(k):
        return remote(vb.at[k, ex - 1], halo_x.at[k, 0], sx.at[0], rx.at[k % 2, 0], (slab_at(1), p))

    def x_down(k):
        return remote(vb.at[k, 0], halo_x.at[k, 1], sx.at[1], rx.at[k % 2, 1], (slab_at(-1), p))

    def y_up(k):
        return remote(
            vb.at[k, :, pl.ds(ey - PACK, PACK)], halo_y.at[k, 0], sy.at[0], ry.at[k % 2, 0], (s, patch_at(1))
        )

    def y_down(k):
        return remote(vb.at[k, :, pl.ds(0, PACK)], halo_y.at[k, 1], sy.at[1], ry.at[k % 2, 1], (s, patch_at(-1)))

    def d_up():
        return remote(disp_ref.at[:, pl.ds(rows - EDGE, EDGE)], halo_d.at[0], sd.at[0], rd.at[0], (s, patch_at(1)))

    def d_down():
        return remote(disp_ref.at[:, pl.ds(0, EDGE)], halo_d.at[1], sd.at[1], rd.at[1], (s, patch_at(-1)))

    shift = ey - TIP
    side_base = (shift, 0)
    tip_base = [(DEEP + TIP * n + ey, DEEP + TIP * n) for n in range(2)]

    side_w = ex * (2 * SWEEPS - 1)
    side_v = SWEEPS + 2

    def near_copy(n):
        return remote(near_out, near_in.at[n], s_near.at[n], r_near.at[n], (slab_at(1 - 2 * n), p))

    def far_copy(n):
        return remote(far_out, far_in.at[n], s_far.at[n], r_far.at[n], (slab_at(2 - 4 * n), p))

    def side_copy(n):
        return remote(side_out.at[n], rim.at[pl.ds(side_base[n], DEEP)], s_side.at[n], r_side.at[n], (s, patch_at(1 - 2 * n)))

    def tip_copy(n, m):
        q = 2 * n + m
        return remote(tip_out.at[q], rim.at[pl.ds(tip_base[n][m], TIP)], s_tip.at[q], r_tip.at[q], (slab_at(1 - 2 * n), patch_at(1 - 2 * m)))

    to_s, from_s = (has_next_s, has_prev_s), (has_prev_s, has_next_s)
    to_p, from_p = (has_next_p, has_prev_p), (has_prev_p, has_next_p)
    to_far, from_far = (has_far_next, has_far_prev), (has_far_prev, has_far_next)
    corners = [(n, m) for n in range(2) for m in range(2)]
    def point_first(j):
        peer = patch_peer(j)
        src = point_ref.at[0, :, pl.ds(pl.multiple_of(peer * cap, cap), cap)]
        return remote(src, points.at[s, p], point_sem.at[0], point_sem.at[1], (s, peer))

    def point_second(j):
        return remote(points.at[s], points.at[s], point_sem.at[2], rp2.at[s], (slab_peer(j), p))

    def pull_copy(j, i):
        to = (slab_peer(j), patch_peer(i))
        here = pl.ds(pl.multiple_of(p * cap, cap), cap)
        return remote(pull_out.at[to[1]], pulls.at[s, :, here], pull_sem.at[0 if j else 1], rq.at[s], to)

    def pick_copy(j):
        peer = patch_peer(j)
        return remote(picks_out.at[peer], picks_in.at[p], pick_sem.at[0], pick_sem.at[1], (s, peer))

    def settle(ref, semaphore):
        pltpu.make_async_copy(ref, ref, semaphore).wait()

    def halo_sends(k, act):
        pl.when(has_next_s)(lambda: act(x_up(k)))
        pl.when(has_prev_s)(lambda: act(x_down(k)))
        if k > 0:
            pl.when(has_next_p)(lambda: act(y_up(k)))
            pl.when(has_prev_p)(lambda: act(y_down(k)))

    def send_halos(k):
        if k == 0:
            for n in range(2):
                pl.when(to_s[n])(lambda: near_copy(n).wait_send())
        else:
            halo_sends(k - 1, lambda copy: copy.wait_send())
        if k == 1:
            for n in range(2):
                pl.when(to_p[n])(lambda: side_copy(n).wait_send())
        halo_sends(k, lambda copy: copy.start())

    def build_points(slab):
        for k in range(patches):
            row, col = split_point(points[slab, k], cols)
            span = pl.ds(k * cap, cap)
            onehot_row[slab, :, span] = jnp.where(
                lax.broadcasted_iota(jnp.int32, (rows, cap), 0) == row, 1.0, 0.0
            ).astype(BF16)
            onehot_col[slab, :, span] = jnp.where(
                lax.broadcasted_iota(jnp.int32, (cols, cap), 0) == col, 1.0, 0.0
            ).astype(BF16)

    def lives(k):
        lane = lax.broadcasted_iota(jnp.int32, (1, cap), 1)
        return lane < count_ref[0, :, k : k + 1]

    def shell():
        pl.when(has_prev_p)(lambda: d_up().wait_recv())
        pl.when(has_next_p)(lambda: d_down().wait_recv())
        total = rows + 2 * EDGE
        line = lax.broadcasted_iota(jnp.int32, (total, cols), 0)
        first = jnp.where(has_prev_p, 0, EDGE)
        last = jnp.where(has_next_p, total, EDGE + rows)
        valid = (line >= first) & (line < last)
        gain = 1.0 / (36.0 * stiff_ref[...])
        gain_buf[...] = gain
        for c in range(comps):
            field = jnp.concatenate([halo_d[0, c], disp_ref[c], halo_d[1, c]], axis=0)
            field = jnp.where(valid, field, 0.0)
            bend = jnp.where(valid, laplace(field), 0.0)
            full = (laplace(bend) + 4.0 * bend)[EDGE : EDGE + rows]
            rest_buf[c] = disp_ref[c] - stiff_ref[...] * full * gain

    with jax.named_scope("w_mat"):
        ready(4, 8)
        base0 = dot_nt(traction_ref[...], inverse_ref[...])
        ready(3)
    couples = (matrix_ref[...], cx_ref[...], cy_ref[...])
    with jax.named_scope("words"):
        one = first_words(base0, traction_ref[...], *couples)
        base1 = dot_nt(one.astype(BF16), inverse_ref[...])
    with jax.named_scope("w_state"):
        ready(0, 1, 2)
    rounded0 = state_ref[...].astype(BF16)
    vb[0] = rounded0
    wet = rhs_ref[...].astype(BF16)
    flat = 1.0 / scale_ref[...]
    w_own = jnp.concatenate([flat, blank(ex, wide_lanes - ey)], axis=1)
    lane = lax.broadcasted_iota(jnp.int32, (1, wide_lanes), 1)
    low_half = lane < ey
    tail_half = lane < ey + ey // 2
    w_lines = jnp.concatenate([w_own] + [blank(ex, wide_lanes)] * (dof // wide_lanes - 1), axis=1)
    with jax.named_scope("project"):
        two = second_words(base1, one, comps, *couples)
        flow = rounded0.reshape(wide_lanes, dof)
        passed = join(*[dot(flow, couple) for couple in couples]).astype(BF16)
        mapped = dot(join(passed, wet.reshape(wide_lanes, dof)), inverse_ref[...])
        turned = join(flow.astype(F32) - mapped[:wide_lanes], mapped[wide_lanes:]).astype(BF16)
        both = dot_nt(stacked(two, one, traction_ref[...].astype(F32)), turned)
        own_v = join(*[both[: 2 * DEEP, n * wide_lanes : (n + 1) * wide_lanes] for n in range(3)])
        own_r = both[:, 3 * wide_lanes :]
        packed = jnp.where(low_half, w_own[0:1], pltpu.roll(w_own[1:2], ey, 1))
        spare = join(
            blank(2 * DEEP - comps - 1, wide_lanes), own_r[2 * DEEP : 2 * DEEP + comps], packed
        )
        near_out[...] = join(
            own_v[0:DEEP], own_v[2 * DEEP : 4 * DEEP] + spare, own_v[4 * DEEP : 5 * DEEP], own_r[0:DEEP]
        ).astype(BF16)
        far_out[...] = own_v[2 * DEEP : 2 * DEEP + 8].astype(BF16)

        def state_at(i, c):
            return state_ref[i, c : c + 1]

        def rhs_at(i, c):
            return rhs_ref[i, c : c + 1]

        for m in range(2):
            close = [ey - 1 - j if m == 0 else j for j in range(SWEEPS)]
            if m == 1:
                side = [state_at(i, c) for i in range(ex) for c in close]
                side += [rhs_at(i, c) for i in range(ex) for c in close[: SWEEPS - 1]]
                side += [w_lines, blank(DEEP - side_w - ex, dof)]
            else:
                side = [w_lines, blank(side_v - ex, dof)]
                side += [state_at(i, c) for i in range(ex) for c in close[::-1]]
                side += [blank(1, dof)]
                side += [rhs_at(i, c) for i in range(ex) for c in close[: SWEEPS - 1][::-1]]
            side_out[m] = join(*side).astype(BF16)
            for n in range(2):
                r1, r2 = (ex - 1, ex - 2) if n == 0 else (0, 1)
                near2 = [state_at(r1, close[0]), state_at(r1, close[1])]
                last = [state_at(r2, close[0]), rhs_at(r1, close[0])]
                weigh = w_lines[r1 : r1 + 1]
                if m == 1:
                    tip = [weigh, blank(1, dof), *near2, *last, blank(TIP - 6, dof)]
                else:
                    tip = [*near2[::-1], blank(1, dof), *last, weigh, blank(TIP - 6, dof)]
                tip_out[2 * n + m] = join(*tip).astype(BF16)

    ready(5, 6, 7)
    with jax.named_scope("w_barrier"):
        pl.semaphore_wait(barrier, awaited)
    for n, m in corners:
        pl.when(jnp.logical_and(to_s[n], to_p[m]))(lambda: tip_copy(n, m).start())
    for n in range(2):
        pl.when(to_s[n])(lambda: near_copy(n).start())
    for m in range(2):
        pl.when(to_p[m])(lambda: side_copy(m).start())
    for n in range(2):
        pl.when(to_far[n])(lambda: far_copy(n).start())
    if reaches:
        near_signal(0)
    for j in range(1, patches):
        point_first(j).start()
    for owner in range(patches):

        @pl.when(p == owner)
        def _():
            points[s, owner] = point_ref[0, :, owner * cap : (owner + 1) * cap]

    for owner in range(patches):
        elem = elem_ref[0, :, owner * cap : (owner + 1) * cap]
        for i in range(ex):
            line = lax.broadcasted_iota(jnp.int32, (wide_lanes, cap), 0)
            hit = (line + i * ey == elem) & (line < ey) & lives(owner)
            onehot_elem[owner, i] = jnp.where(hit, 1.0, 0.0).astype(BF16)
    if reaches:
        with jax.named_scope("w_reach"):
            near_wait(0)
        if len(reaches) > 1:
            near_signal(1)
    send_halos(0)
    scales = [column(scale_ref[i : i + 1, :]) for i in range(ex)]
    inverses = [1.0 / x for x in scales]

    def prelude(k):
        own = dot(vb[k].reshape(ex * ey, dof), matrix_ref[...]).reshape(ex, ey, dof)
        for i in range(ex):
            base_buf[i] = rhs_ref[i] - scales[i] * own[i]

    for n in range(2):
        pl.when(to_far[n])(lambda: far_copy(n).wait_send())
    pl.when(has_next_p)(lambda: d_up().start())
    pl.when(has_prev_p)(lambda: d_down().start())
    with jax.named_scope("late_words"):
        base2 = dot_nt(two.astype(BF16), inverse_ref[...])
        words = third_words(base2, two, matrix_ref[...], cx_ref[...], cy_ref[...])
        rest = stacked(base2, base1, base0)
    with jax.named_scope("prelude"):
        prelude(0)

    def halves(x):
        return jnp.where(low_half, x, 0.0), jnp.where(low_half, pltpu.roll(x, ey, 1), 0.0)

    span_rows = list(range(-ex, 2 * ex))

    def between(low, high):
        return (lane >= low) & (lane < high)

    def frame_mask(n, reach):
        right, left = has_next_p, has_prev_p
        if n is not None:
            right, left = jnp.logical_and(right, from_s[n]), jnp.logical_and(left, from_s[n])
        right, left = jnp.where(right, 1, 0), jnp.where(left, 1, 0)
        ahead, behind = between(ey, ey + reach), between(wide_lanes - reach, wide_lanes)
        return jnp.where(ahead, right, jnp.where(behind, left, 0)) > 0

    masks = {(n, reach): frame_mask(n, reach) for n in (None, 0, 1) for reach in range(1, SWEEPS + 1)}

    def framing(x, source, mask):
        return jnp.where(mask, pltpu.roll(x, (ey - source) % wide_lanes, 1), 0.0)

    with jax.named_scope("halves"):
        own_rows = list(zip(halves(own_v), halves(own_r)))
    with jax.named_scope("w_side"):
        for m in range(2):
            pl.when(from_p[m])(lambda: side_copy(m).wait_recv())
        for n, m in corners:
            pl.when(jnp.logical_and(from_s[n], from_p[m]))(lambda: tip_copy(n, m).wait_recv())
    early = s < slabs // 2
    known = 4

    def far_off(j):
        peer = slab_peer(j)
        return jnp.maximum(peer - s, s - peer) > known

    def learn_all():
        for n in range(1, len(reaches)):
            with jax.named_scope("w_reach"):
                near_wait(n)
            if n + 1 < len(reaches):
                near_signal(n + 1)

    with jax.named_scope("w_pt1"):
        settle(points.at[s, pl.ds(0, patches - 1)], point_sem.at[1])

    @pl.when(early)
    def _():
        for j in range(1, slabs):
            pl.when(jnp.logical_not(far_off(j)))(lambda: point_second(j).start())

    @pl.when(jnp.logical_not(early))
    def _():
        learn_all()
        for j in range(1, slabs):
            point_second(j).start()

    with jax.named_scope("place"):
        stack = rim[...]
        placed_v = dot_nt(words, stack)
        placed_r = dot_nt(rest, stack)

        def rim_row(base, at, ok):
            return jnp.where(ok, rim[base + at : base + at + 1, :wide_lanes].astype(F32), 0.0)

        def framed(middle, before, after):
            before, after = pltpu.roll(before, ey, 1), pltpu.roll(after, ey, 1)
            return jnp.where(low_half, middle, jnp.where(tail_half, after, before))

        w_rows = {}
        for i in range(ex):
            w_rows[i] = framed(
                w_own[i : i + 1],
                rim_row(side_base[0], i, has_prev_p),
                rim_row(side_base[1], side_w + i, has_next_p),
            )
        w_tips = [
            (
                rim_row(tip_base[n][0], 5, jnp.logical_and(from_s[n], has_prev_p)),
                rim_row(tip_base[n][1], 0, jnp.logical_and(from_s[n], has_next_p)),
            )
            for n in range(2)
        ]
        edges_v, edges_r = {}, {}
        for i in range(ex):
            edges_v[i] = framing(placed_v, SWEEPS * i, masks[None, SWEEPS])
            edges_r[i] = framing(placed_r, SWEEPS * ex + (SWEEPS - 1) * i, masks[None, SWEEPS - 1])
        for n in range(2):
            r1, r2 = (-1, -2) if n == 0 else (ex, ex + 1)
            base = tip_base[n][1]
            used = join(placed_v[:DEEP], placed_v[2 * DEEP : 5 * DEEP])
            edges_v[r1] = framing(used, base + 2, masks[n, 2])
            edges_v[r2] = framing(used, base + 4, masks[n, 1])
            edges_r[r1] = framing(placed_r[:DEEP], base + 5, masks[n, 1])

    def across(k, wide):
        line = lax.broadcasted_iota(jnp.int32, (ey, dof), 0)
        along_y = []
        for i in range(ex):
            if k == 0:
                at = shift + side_v + SWEEPS * (i + 1) - 1
                before = rim[at : at + 1].astype(F32)
                after = rim[SWEEPS * i : SWEEPS * i + 1].astype(F32)
            else:
                before = halo_y[k, 0, i].astype(F32)[PACK - 1 : PACK]
                after = halo_y[k, 1, i].astype(F32)[0:1]
            before = jnp.where(has_prev_p, before, 0.0)
            after = jnp.where(has_next_p, after, 0.0)
            prev = jnp.where(line == 0, jnp.broadcast_to(before, (ey, dof)), pltpu.roll(wide[i], 1, 0))
            following = jnp.where(line == ey - 1, jnp.broadcast_to(after, (ey, dof)), pltpu.roll(wide[i], ey - 1, 0))
            along_y.append((prev + following).astype(BF16))
        return dot(jnp.concatenate(along_y, axis=0), cy_ref[...])

    with jax.named_scope("w_near"):
        for n in range(2):
            pl.when(from_far[n])(lambda: far_copy(n).wait_recv())
            pl.when(from_s[n])(lambda: near_copy(n).wait_recv())

    with jax.named_scope("stencil"):
        by_d, by_x, by_y, by_r2, by_r1, by_r0 = {}, {}, {}, {}, {}, {}
        for i, (v_half, r_half) in enumerate(own_rows):
            full, side = v_half + edges_v[i], r_half + edges_r[i]
            by_d[i], by_x[i], by_y[i] = (full[k * 2 * DEEP : (k + 1) * 2 * DEEP] for k in range(3))
            by_r2[i], by_r1[i], by_r0[i] = (
                side[: 2 * DEEP], side[2 * DEEP : 2 * DEEP + 3 * comps], side[3 * DEEP : 3 * DEEP + comps]
            )
        for n in range(2):
            got = jnp.where(from_s[n], near_in[n].astype(F32), 0.0)
            for i, half in enumerate(halves(got)):
                r = i - ex if n == 0 else i + ex
                edge = edges_v[r]
                by_d[r] = half[0:DEEP] + edge[0:DEEP]
                by_x[r] = half[DEEP : 3 * DEEP] + edge[DEEP : 3 * DEEP]
                by_y[r] = half[3 * DEEP : 4 * DEEP] + edge[3 * DEEP : 4 * DEEP]
                by_r2[r] = half[4 * DEEP : 5 * DEEP]
                if r in edges_r:
                    by_r2[r] = by_r2[r] + edges_r[r]
                by_r1[r] = half[3 * DEEP - comps - 1 : 3 * DEEP - 1]
                w_rows[r] = half[3 * DEEP - 1 : 3 * DEEP]
                if r in (-1, ex):
                    w_rows[r] = framed(w_rows[r], *w_tips[n])
            beyond = halves(jnp.where(from_far[n], far_in[n].astype(F32), 0.0))[1 - n]
            by_x[-ex - 1 if n == 0 else 2 * ex] = join(beyond, blank(DEEP - 8, wide_lanes))

        def turn(x):
            return pltpu.roll(x, 1, 1) + pltpu.roll(x, wide_lanes - 1, 1)

        one = {}
        for r in span_rows:
            n = 2 * DEEP if 0 <= r < ex else DEEP
            one[r] = by_d[r] + w_rows[r] * (by_x[r - 1][:n] + by_x[r + 1][:n] + turn(by_y[r]) + by_r2[r])
        two = {}
        for r in range(-1, ex + 1):
            if 0 <= r < ex:
                d_part = join(one[r][:comps], one[r][DEEP : DEEP + 2 * comps])
                y_part = join(one[r][4 * comps : 5 * comps], one[r][DEEP + 2 * comps : DEEP + 4 * comps])
                n = 3 * comps
            else:
                d_part, y_part = one[r][:comps], one[r][4 * comps : 5 * comps]
                n = comps
            x_part = one[r - 1][comps : comps + n] + one[r + 1][comps : comps + n]
            two[r] = d_part + w_rows[r] * (x_part + turn(y_part) + by_r1[r])
        drawn = []
        for r in range(ex):
            x_part = two[r - 1][:comps] + two[r + 1][:comps]
            drawn.append(
                two[r][comps : 2 * comps]
                + w_rows[r] * (x_part + turn(two[r][2 * comps : 3 * comps]) + by_r0[r])
            )
        tractions = [jnp.where(low_half, x, 0.0).astype(BF16) for x in drawn]
        for owner in range(patches):
            pull_out[owner] = sum(dot(tractions[i], onehot_elem[owner, i]) for i in range(ex)).astype(BF16)
        crossed = across(0, vb[0].astype(F32)).reshape(ex, ey, dof)
        for i in range(ex):
            base_buf[i] = base_buf[i] + crossed[i]
    order = sorted(range(slabs), key=lambda j: -min(j, slabs - j))

    def send_pulls(j):
        for i in range(patches):
            if (j, i) != (0, 0):
                pull_copy(j, i).start()

    with jax.named_scope("s_pull"):

        @pl.when(early)
        def _():
            for j in order:
                pl.when(jnp.logical_not(far_off(j)))(lambda: send_pulls(j))
        @pl.when(jnp.logical_not(early))
        def _():
            for j in range(1, slabs):
                pl.when(far_off(j))(lambda: send_pulls(j))
            for j in order:
                pl.when(jnp.logical_not(far_off(j)))(lambda: send_pulls(j))

    for owner in range(patches):

        @pl.when(p == owner)
        def _():
            pulls[s, :, owner * cap : (owner + 1) * cap] = pull_out[owner]


    def sweep(k, v):
        rounded = vb[k]
        wide = rounded.astype(F32)
        with jax.named_scope("w_halo"):
            if k > 0:
                pl.when(has_prev_p)(lambda: y_up(k).wait_recv())
                pl.when(has_next_p)(lambda: y_down(k).wait_recv())
            pl.when(has_prev_s)(lambda: x_up(k).wait_recv())
            pl.when(has_next_s)(lambda: x_down(k).wait_recv())
        side_y = across(k, wide) if k > 0 else 0.0
        low = jnp.where(has_prev_s, halo_x[k, 0].astype(F32), 0.0)
        high = jnp.where(has_next_s, halo_x[k, 1].astype(F32), 0.0)
        along_x = []
        for i in range(ex):
            below = low if i == 0 else wide[i - 1]
            above = high if i == ex - 1 else wide[i + 1]
            along_x.append((below + above).astype(BF16))
        side_x = dot(jnp.concatenate(along_x, axis=0), cx_ref[...])
        side = (side_x + side_y).reshape(ex, ey, dof)
        residue = jnp.concatenate([(base_buf[i] + side[i]).astype(BF16) for i in range(ex)], axis=0)
        update = dot(residue, inverse_ref[...]).reshape(ex, ey, dof)
        return [v[i] + update[i] * inverses[i] for i in range(ex)]

    def keep(v, k):
        if k < SWEEPS:
            for i in range(ex):
                vb[k, i] = v[i].astype(BF16)
            send_halos(k)
        for i in range(ex):
            fluid_ref[i] = v[i]

    with jax.named_scope("sweep0"):
        keep(sweep(0, state_ref), 1)
        prelude(1)

    @pl.when(early)
    def _():
        learn_all()
        for j in order[:-1]:

            @pl.when(far_off(j))
            def _():
                point_second(j).start()
                send_pulls(j)


    def scatter(slab, acc):
        hot = onehot_row[slab]
        value = pulls[slab]
        scaled = jnp.concatenate([hot * value[c : c + 1] for c in range(comps)], axis=0)
        return acc + dot_nt(scaled, onehot_col[slab])

    inner = jnp.minimum(s, slabs - 1 - s)

    def nearest(t):
        step = lax.div(t + 1, 2)
        alternate = jnp.where(lax.rem(t, 2) == 1, s + step, s - step)
        return jnp.where(t <= 2 * inner, alternate, jnp.where(s < slabs - 1 - s, t, slabs - 1 - t))

    def settle_points(t):
        with jax.named_scope("w_point"):
            settle(points.at[nearest(t)], rp2.at[nearest(t)])

    def settle_pulls(t):
        with jax.named_scope("w_pull"):
            settle(pulls.at[nearest(t)], rq.at[nearest(t)])

    def prepared(t, carry):
        settle_points(t)
        build_points(nearest(t))
        return carry

    def gathered(t, acc):
        settle_pulls(t)
        return scatter(nearest(t), acc)

    def gathered_ahead(t, acc):
        settle_points(t + half - 1)
        settle_pulls(t)
        acc = scatter(nearest(t), acc)
        build_points(nearest(t + half - 1))
        return acc

    half = (slabs + 1) // 2
    build_points(s)
    with jax.named_scope("shell"):
        shell()
    with jax.named_scope("build1"):
        lax.fori_loop(1, half, prepared, 0)
    with jax.named_scope("w_own"):
        settle(pulls.at[s, :, pl.ds(0, (patches - 1) * cap)], rq.at[s])
    acc = scatter(s, jnp.zeros((comps * rows, cols), F32))
    last = slabs - half + 1
    with jax.named_scope("gather1"):
        acc = lax.fori_loop(1, half, gathered_ahead, acc)
    with jax.named_scope("sweep1"):
        keep(sweep(1, fluid_ref), 2)
    with jax.named_scope("gather2"):
        acc = lax.fori_loop(half, last, gathered_ahead, acc)
        acc = lax.fori_loop(last, slabs, gathered, acc)
    loads = acc.reshape(comps, rows, cols)
    fresh = [rest_buf[c] + loads[c] * gain_buf[...] for c in range(comps)]
    narrow = jnp.concatenate([x.astype(BF16) for x in fresh], axis=0)
    def picks_for(j):
        k = patch_peer(j)
        span = pl.ds(pl.multiple_of(k * cap, cap), cap)
        spread = dot(narrow, onehot_col[s, :, span]).reshape(comps, rows, cap)
        hot = onehot_row[s, :, span].astype(F32)
        for c in range(comps):
            picks_out[k, c : c + 1] = jnp.sum(spread[c] * hot, axis=0, keepdims=True).astype(BF16)

    far_first = sorted(range(1, patches), key=lambda j: -min(j, patches - j))
    with jax.named_scope("s_pick"):
        for j in far_first:
            picks_for(j)
            pick_copy(j).start()
    picks_for(0)
    picks_in[p] = picks_out[p]
    for c in range(comps):
        net_ref[c] = fresh[c]
    with jax.named_scope("sweep2"):
        prelude(2)
        keep(sweep(2, fluid_ref), SWEEPS)
    with jax.named_scope("w_pick"):
        settle(picks_in.at[pl.ds(0, patches - 1)], pick_sem.at[1])
    for k in range(patches):
        live = lives(k)
        for c in range(comps):
            wall_ref[c, 0, :, k * cap : (k + 1) * cap] = jnp.where(live, picks_in[k, c : c + 1].astype(F32), 0.0)

    with jax.named_scope("drain"):
        halo_sends(SWEEPS - 1, lambda copy: copy.wait_send())
        pl.when(has_next_p)(lambda: d_up().wait_send())
        pl.when(has_prev_p)(lambda: d_down().wait_send())
        for n, m in corners:
            pl.when(jnp.logical_and(to_s[n], to_p[m]))(lambda: tip_copy(n, m).wait_send())
        settle(points.at[s, pl.ds(0, patches - 1)], point_sem.at[0])
        settle(points.at[pl.ds(0, slabs - 1)], point_sem.at[2])
        settle(pulls.at[pl.ds(0, slabs - 1)], pull_sem.at[0])
        settle(pulls.at[s, :, pl.ds(0, (patches - 1) * cap)], pull_sem.at[1])
        settle(picks_in.at[pl.ds(0, patches - 1)], pick_sem.at[0])


def deliver(*refs):
    copies = [pltpu.make_async_copy(refs[n], refs[n + 3], refs[6].at[n]) for n in range(3)]
    for copy in copies:
        copy.start()
    for copy in copies:
        copy.wait()


def shards(slabs, patches, *args):
    state, disp, elem = args[0], args[11], args[8]
    ex, ey, dof = state.shape
    comps, rows, cols = disp.shape
    cap = elem.shape[2] // patches
    sem = pltpu.SemaphoreType.DMA
    vmem = pl.BlockSpec(memory_space=pltpu.VMEM)
    hot_bytes = slabs * patches * cap * (rows + cols) * 2
    outs = pl.pallas_call(
        functools.partial(kernel, slabs, patches, len(args)),
        out_shape=(
            pltpu.VMEM(state.shape, F32),
            pltpu.VMEM(disp.shape, F32),
            pltpu.VMEM((comps, 1, 1, elem.shape[2]), F32),
        ),
        in_specs=[pl.BlockSpec(memory_space=pltpu.HBM)] * len(args),
        out_specs=(vmem, vmem, vmem),
        scratch_shapes=[pltpu.VMEM(x.shape, x.dtype) for x in args[:3]]
        + [
            pltpu.VMEM((3,) + args[3].shape, BF16),
            pltpu.VMEM(args[7].shape, BF16),
            pltpu.VMEM((2,) + elem.shape, jnp.int32),
            pltpu.VMEM(args[10].shape, jnp.int32),
            pltpu.VMEM((comps + 1, rows, cols), F32),
            pltpu.VMEM(args[6].shape, BF16),
            pltpu.VMEM((SWEEPS, ex, ey, dof), BF16),
            pltpu.VMEM((SWEEPS, 2, ey, dof), BF16),
            pltpu.VMEM((SWEEPS, 2, ex, PACK, dof), BF16),
            pltpu.VMEM((2, comps, EDGE, cols), F32),
            pltpu.VMEM((slabs, patches, 1, cap), jnp.int32),
            pltpu.VMEM((slabs, comps, patches * cap), BF16),
            pltpu.VMEM((patches, comps, cap), BF16),
            pltpu.VMEM((patches, comps, cap), BF16),
            pltpu.VMEM((patches, comps, cap), BF16),
            pltpu.VMEM((patches, ex, ex * ey, cap), BF16),
            pltpu.VMEM((slabs, rows, patches * cap), BF16),
            pltpu.VMEM((slabs, cols, patches * cap), BF16),
            pltpu.VMEM((comps, rows, cols), F32),
            pltpu.VMEM((rows, cols), F32),
            pltpu.VMEM(state.shape, F32),
            pltpu.VMEM((5 * DEEP, ex * ey), BF16),
            pltpu.VMEM((2, 5 * DEEP, ex * ey), BF16),
            pltpu.VMEM((8, ex * ey), BF16),
            pltpu.VMEM((2, 8, ex * ey), BF16),
            pltpu.VMEM((2, DEEP, dof), BF16),
            pltpu.VMEM((4, TIP, dof), BF16),
            pltpu.VMEM((ex * ey, dof), BF16),
            sem((9,)),
            sem((2, 2)),
            sem((2, 2)),
            sem((2,)),
            sem((3,)),
            sem((slabs,)),
            sem((2,)),
            sem((slabs,)),
            sem((2,)),
            sem((2,)),
            sem((2,)),
            sem((2,)),
            sem((2,)),
            sem((4,)),
            pltpu.SemaphoreType.REGULAR((max(slabs.bit_length() - 2, 1),)),
        ],
        compiler_params=pltpu.CompilerParams(collective_id=0, has_side_effects=True),
    )(*args)
    return pl.pallas_call(
        deliver,
        out_shape=tuple(jax.ShapeDtypeStruct(x.shape, x.dtype) for x in outs),
        in_specs=[vmem] * 3,
        out_specs=(pl.BlockSpec(memory_space=pltpu.HBM),) * 3,
        scratch_shapes=[sem((3,))],
    )(*[pltpu.with_memory_space_constraint(x, pltpu.VMEM) for x in outs])


def solution(mesh):
    return jax.shard_map(
        functools.partial(shards, mesh.shape["slab"], mesh.shape["patch"]),
        mesh=mesh,
        in_specs=(
            P("slab", "patch", None),
            P("slab", "patch", None),
            P("slab", "patch"),
            P(),
            P(),
            P(),
            P(),
            P(),
            P("slab", "patch", None),
            P("slab", "patch", None),
            P("slab", "patch", None),
            P(None, "patch", None),
            P("patch", None),
        ),
        out_specs=(
            P("slab", "patch", None),
            P(None, "patch", None),
            P(None, "slab", "patch", None),
        ),
        check_vma=False,
    )
```
